128 devices in a mesh: gx: 8 (over z, x_hi), gy: 16 (over x_lo, y, core).
Axes of the slice: x: 4 (x_hi: 2, x_lo: 2; x = x_hi * 2 + x_lo), y: 4, z: 4, core: 2. Of those that a mesh axis runs over, the one named last changes fastest.
Arguments:
- ensemble: float32 [192, 384, 6, 128], P('gx', 'gy'), may hold values from -6 to 6
- cfl_ratio_primary_axis: float32 [192, 384, 6], P('gx', 'gy'), may hold values from -0.35 to 0.35
- cfl_ratio_secondary_axis: float32 [192, 384, 6], P('gx', 'gy'), may hold values from -0.35 to 0.35
- spreading_ratio: float32 [192, 384, 6], P('gx', 'gy'), may hold values from 0.02 to 0.07
- obs_owner: int32 [1024], replicated, may hold values from 0 to 127
- obs_local: int32 [1024], replicated, may hold values from 0 to 3455
- batch_order: int32 [1024], replicated, may hold values from 0 to 1023, each once
- obs_reach: int32 [1024], replicated, may hold values from 24 to 72
- obs_value: float32 [1024], replicated, may hold values from -6 to 6
- obs_variance: float32 [1024], replicated, may hold values from 0.25 to 4
- obs_noise: float32 [1024, 128], replicated, may hold values from -6 to 6
Outputs:
- analysis: float32 [192, 384, 6, 128], P('gx', 'gy')
The draws below stay inside these ranges and needn't reach their ends.
All inputs are finite; a program needn't handle non-finite values.
Results may differ from the reference program's by a relative error of at most 0.0001.
Values sent between devices are 32-bit elements; how exact they have to be, the bound alone decides.
A program may use at most 64 MiB of HBM per device.

```python
import math
import jax
import jax.numpy as jnp
from jax import lax

CX = 24
CY = 24
LEV = 6
MEM = 128
STEPS = 2
NOBS = 1024
OB = 64
NB = 16
NX = 192
NY = 384
N_GX = 8
N_GY = 16


def set_ends(entries, rng, smallest, largest):
    longest = entries.shape.index(max(entries.shape))
    spots = []
    for shift in (0, 1):
        where = [jax.random.randint(jax.random.fold_in(rng, axis), (), 0, length) for axis, length in enumerate(entries.shape)]
        where[longest] = (where[longest] + shift) % entries.shape[longest]
        spots.append(tuple(where))
    return entries.at[spots[0]].set(smallest).at[spots[1]].set(largest)


def steps_of(key, shape, cuts, least, largest):
    def one(axis_at, shards_of):
        steps = jax.random.uniform(jax.random.fold_in(jax.random.fold_in(key, 6), axis_at), (shards_of,), jnp.float32, least / len(cuts), largest / len(cuts))
        return jnp.repeat(jnp.exp(steps), shape[axis_at] // shards_of).reshape((-1,) + (1,) * (len(shape) - axis_at - 1))

    level = one(*cuts[0])
    for cut in cuts[1:]:
        level = level * one(*cut)
    return level


def scatter_about(rng, dims, width, limit, cuts=(), kind=jnp.bfloat16):
    values = jax.random.normal(rng, dims, jnp.float32) * width
    if len(cuts) > 0:
        values = steps_of(rng, dims, cuts, -0.22, 0.18) * values
    return jnp.clip(values, min=-limit, max=limit).astype(kind)


def setup_inputs(seed: int = 0) -> dict:
    streams_of = jax.random.split(jax.random.key(seed), 12)
    return {
        "ensemble": scatter_about(streams_of[0], (NX, NY, LEV, MEM), 1.0, 6.0, ((0, 8), (1, 16)), jnp.float32),
        "cfl_ratio_primary_axis": jnp.clip(jax.random.uniform(streams_of[1], (NX, NY, LEV), jnp.float32, -0.35, 0.35) * steps_of(streams_of[1], (NX, NY, LEV), ((0, 8), (1, 16)), -0.4, 0.0), -0.35, 0.35),
        "cfl_ratio_secondary_axis": jnp.clip(jax.random.uniform(streams_of[2], (NX, NY, LEV), jnp.float32, -0.35, 0.35) * steps_of(streams_of[2], (NX, NY, LEV), ((0, 8), (1, 16)), -0.4, 0.0), -0.35, 0.35),
        "spreading_ratio": jnp.clip(0.02 + 0.05 * jax.random.uniform(streams_of[3], (NX, NY, LEV), jnp.float32) ** steps_of(streams_of[3], (NX, NY, LEV), ((0, 8), (1, 16)), -0.2, 0.2), 0.02, 0.07),
        "obs_owner": set_ends(jax.random.randint(streams_of[4], (NOBS,), 0, N_GX * N_GY), jax.random.fold_in(streams_of[4], 1), 0, (N_GX * N_GY) - 1).astype(jnp.int32),
        "obs_local": set_ends(jax.random.randint(streams_of[5], (NOBS,), 0, CX * CY * LEV), jax.random.fold_in(streams_of[5], 1), 0, (CX * CY * LEV) - 1).astype(jnp.int32),
        "batch_order": jax.random.permutation(streams_of[6], NOBS).astype(jnp.int32),
        "obs_reach": set_ends(jax.random.randint(streams_of[7], (NOBS,), CX, 3 * CX + 1), jax.random.fold_in(streams_of[7], 1), CX, 3 * CX).astype(jnp.int32),
        "obs_value": scatter_about(streams_of[8], (NOBS,), 1.0, 6.0, (), jnp.float32),
        "obs_variance": jnp.clip(jnp.exp(jax.random.uniform(streams_of[9], (NOBS,), jnp.float32, math.log(0.25), math.log(4.0))), 0.25, 4.0),
        "obs_noise": scatter_about(streams_of[10], (NOBS, MEM), 1.0, 6.0, (), jnp.float32),
    }


def propagate_prediction(bordered_grid, primary_cfl, secondary_cfl, spreading_rate):
    centre = bordered_grid[1:-1, 1:-1]
    west = bordered_grid[:-2, 1:-1]
    east = bordered_grid[2:, 1:-1]
    south = bordered_grid[1:-1, :-2]
    north = bordered_grid[1:-1, 2:]
    cxe = primary_cfl[..., None]
    cye = secondary_cfl[..., None]
    kde = spreading_rate[..., None]
    tend = -(jnp.maximum(cxe, 0.0) * (centre - west) + jnp.minimum(cxe, 0.0) * (east - centre))
    tend = tend - (jnp.maximum(cye, 0.0) * (centre - south) + jnp.minimum(cye, 0.0) * (north - centre))
    tend = tend + kde * (east + west + north + south - 4.0 * centre)
    return centre + tend

def taper(col_x, col_y, obs_x, obs_y, reach):
    dx = col_x[:, None] - obs_x[None, :]
    dy = col_y[:, None] - obs_y[None, :]
    radius = reach.astype(jnp.float32)
    ratio = (dx * dx + dy * dy) / (radius * radius)[None, :]
    return jnp.maximum(1.0 - ratio, 0.0) ** 2

def batch_solve(hx, values, variance, noise):
    members = hx.shape[1]
    centred = hx - lax.optimization_barrier(jnp.mean(hx, axis=1, keepdims=True))
    scaled = centred / (members - 1.0)
    cov = jnp.dot(centred.astype(jnp.float32), scaled.T.astype(jnp.float32), precision=lax.Precision.HIGHEST, preferred_element_type=jnp.float32)
    cov = cov + jnp.diag(variance)
    innov = values[:, None] + jnp.sqrt(variance)[:, None] * noise - hx
    factor = jnp.linalg.cholesky(cov)
    return (scaled, jax.scipy.linalg.cho_solve((factor, True), innov))

def reference(ensemble, cfl_ratio_primary_axis, cfl_ratio_secondary_axis, spreading_ratio, obs_owner, obs_local, batch_order, obs_reach, obs_value, obs_variance, obs_noise):
    current_vector = ensemble
    for step in range(STEPS):
        bordered_grid = jnp.pad(current_vector, ((1, 1), (1, 1), (0, 0), (0, 0)))
        current_vector = propagate_prediction(bordered_grid, cfl_ratio_primary_axis, cfl_ratio_secondary_axis, spreading_ratio)
    nx_all = current_vector.shape[0]
    ny_all = current_vector.shape[1]
    ix = obs_local // (CY * LEV)
    iy = obs_local // LEV % CY
    level = obs_local % LEV
    pos_x = obs_owner // N_GY * CX + ix
    pos_y = obs_owner % N_GY * CY + iy
    flat_index = ((pos_x * ny_all + pos_y) * LEV + level).astype(jnp.int32)
    obs_fx = pos_x.astype(jnp.float32)
    obs_fy = pos_y.astype(jnp.float32)
    column = jnp.arange(nx_all * ny_all, dtype=jnp.int32)
    col_x = (column // ny_all).astype(jnp.float32)
    col_y = (column % ny_all).astype(jnp.float32)
    flat = current_vector.reshape(nx_all * ny_all * LEV, MEM)
    for batch in range(NB):
        chosen = batch_order[batch * OB:(batch + 1) * OB]
        hx = flat[flat_index[chosen]]
        scaled, solved = batch_solve(hx, obs_value[chosen], obs_variance[chosen], obs_noise[chosen])
        weights = taper(col_x, col_y, obs_fx[chosen], obs_fy[chosen], obs_reach[chosen])
        gain = jnp.dot(flat.astype(jnp.float32), scaled.T.astype(jnp.float32), precision=lax.Precision.HIGHEST, preferred_element_type=jnp.float32)
        gain = (gain.reshape(nx_all * ny_all, LEV, OB) * weights[:, None, :]).reshape(-1, OB)
        flat = flat + jnp.dot(gain.astype(jnp.float32), solved.astype(jnp.float32), precision=lax.Precision.HIGHEST, preferred_element_type=jnp.float32)
    return flat.reshape(nx_all, ny_all, LEV, MEM)
```

```python
import jax
import jax.numpy as jnp
from jax import lax
from jax.experimental import pallas as pl
from jax.experimental.pallas import tpu as pltpu
from jax.sharding import PartitionSpec as P

STEPS = 2
OB = 64
ITERS = 5
BOUND = 16.0
F32 = jnp.float32
BF16 = jnp.bfloat16


def with_halo(cells, sides, width):
    for axis, dim in sides:
        count = lax.axis_size(axis)
        ends = count - 1
        head = lax.slice_in_dim(cells, 0, width, axis=dim)
        tail = lax.slice_in_dim(cells, cells.shape[dim] - width, cells.shape[dim], axis=dim)
        cells = jnp.concatenate(
            [
                lax.ppermute(tail, axis, [(i, (i + 1) % count) for i in range(ends)]),
                cells,
                lax.ppermute(head, axis, [((i + 1) % count, i) for i in range(ends)]),
            ],
            axis=dim,
        )
    return cells


def propagate_prediction(bordered_grid, primary_cfl, secondary_cfl, spreading_rate):
    centre = bordered_grid[1:-1, 1:-1]
    west = bordered_grid[:-2, 1:-1]
    east = bordered_grid[2:, 1:-1]
    south = bordered_grid[1:-1, :-2]
    north = bordered_grid[1:-1, 2:]
    cxe = primary_cfl[..., None]
    cye = secondary_cfl[..., None]
    kde = spreading_rate[..., None]
    tend = -(jnp.maximum(cxe, 0.0) * (centre - west) + jnp.minimum(cxe, 0.0) * (east - centre))
    tend = tend - (
        jnp.maximum(cye, 0.0) * (centre - south) + jnp.minimum(cye, 0.0) * (north - centre)
    )
    tend = tend + kde * (east + west + north + south - 4.0 * centre)
    return centre + tend


def split(x):
    high = x.astype(BF16)
    return high, (x - high.astype(F32)).astype(BF16)


def assimilate(fx_ref, fy_ref, ir_ref, rows_x, rows_y, y_in, w_ref, x_ref, out_ref, y_ref, t_ref, v_ref):
    block_x, levels, block_y, members = x_ref.shape
    count = y_in.shape[0]
    batches = count // OB
    y_ref[...] = y_in[...]
    out_ref[...] = x_ref[...]
    lane = lax.broadcasted_iota(jnp.int32, (OB, 2 * OB), 1)
    row = lax.broadcasted_iota(jnp.int32, (OB, 2 * OB), 0)
    eye = jnp.where((lane == row) | (lane == row + OB), 1.0, 0.0).astype(F32)
    ys = lax.broadcasted_iota(jnp.int32, (block_y, 1), 0).astype(F32)

    def step(b, _):
        now = pl.ds(pl.multiple_of(b * OB, OB), OB)
        hx = y_ref[now, :]
        centred = hx - jnp.mean(hx, axis=1, keepdims=True)
        high, low = split(centred)
        high2 = jnp.concatenate([high, high], axis=1)
        low2 = jnp.concatenate([low, low], axis=1)
        side = jnp.concatenate([high2, low2, low2, high2], axis=0)

        def project(x):
            both = jnp.concatenate(split(x), axis=1)
            pair = lax.dot_general(both, side, (((1,), (1,)), ((), ())), preferred_element_type=F32)
            return pair[:, : 2 * OB] + pair[:, 2 * OB :]

        p = project(centred) * (1.0 / (members - 1.0))
        norm = jnp.max(jnp.sum(jnp.abs(p), axis=0, keepdims=True), axis=1, keepdims=True)
        c = 1.0 + jnp.maximum(norm, 0.0625)
        top = c + 1.0
        t = top / (c - 1.0)
        alpha = 2.0 / top
        r = ((c - 1.0) / top) * eye - alpha * p
        rhs = w_ref[now, :] - hx
        v = alpha * rhs
        for i in range(ITERS):
            t = 2.0 * t * t - 1.0
            back = 1.0 / t
            gain = 1.0 + back
            rh, rl = split(r)
            vh, vl = split(v)
            left = jnp.concatenate([rh, rl], axis=1)
            head = jnp.concatenate([rh, vh], axis=1)
            tail = jnp.concatenate([rl, vl], axis=1)
            right = jnp.concatenate([head, tail, head, tail], axis=0)
            prod = jnp.dot(left, right, preferred_element_type=F32)
            v = gain * (v + prod[:, 2 * OB :])
            if i + 1 < ITERS:
                r = gain * prod[:, : 2 * OB] - back * eye
        v_ref[...] = v

        @pl.when(jnp.max(norm) > BOUND)
        def _():
            t_ref[...] = p + eye
            v_ref[...] = rhs

            def pivot(k, _):
                at = lane[:1, :] == k
                trow = t_ref[pl.ds(k, 1), :]
                scale = 1.0 / jnp.sum(jnp.where(at, trow, 0.0), axis=1, keepdims=True)
                trow = trow * scale
                vrow = v_ref[pl.ds(k, 1), :] * scale
                mat = t_ref[...]
                col = jnp.sum(jnp.where(lane == k, mat, 0.0), axis=1, keepdims=True)
                mine = row == k
                t_ref[...] = jnp.where(mine, trow, mat - col * trow)
                v_ref[...] = jnp.where(mine, vrow, v_ref[...] - col * vrow)
                return 0

            lax.fori_loop(0, OB, pivot, 0)

        zh, zl = split(v_ref[...] * (1.0 / (members - 1.0)))
        solved = jnp.concatenate([zh, zl, zh, zl], axis=0)

        def spread(g):
            both = jnp.concatenate(split(g), axis=1)
            return jnp.dot(both, solved, preferred_element_type=F32)

        px = fx_ref[pl.ds(b, 1), :]
        py = fy_ref[pl.ds(b, 1), :]
        ir = ir_ref[pl.ds(b, 1), :]

        def later(j, _):
            at = pl.ds(pl.multiple_of(j * OB, OB), OB)
            old = y_ref[at, :]
            dx = rows_x[at, :] - px
            dy = rows_y[at, :] - py
            near = jnp.maximum(1.0 - (dx * dx + dy * dy) * ir, 0.0)
            y_ref[at, :] = old + spread(project(old) * (near * near))
            return 0

        lax.fori_loop(b + 1, batches, later, 0)
        dy = ys - py
        dy2 = dy * dy * ir

        def cells(i, _):
            dx = i.astype(F32) - px
            near = jnp.maximum((1.0 - dx * dx * ir) - dy2, 0.0)
            rho = near * near
            old = out_ref[i].reshape(levels * block_y, members)
            g = project(old).reshape(levels, block_y, members) * rho[None]
            new = old + spread(g.reshape(levels * block_y, members))
            out_ref[i] = new.reshape(levels, block_y, members)
            return 0

        lax.fori_loop(0, block_x, cells, 0)
        return 0

    lax.fori_loop(0, batches, step, 0)


def per_device(
    ensemble,
    cfl_ratio_primary_axis,
    cfl_ratio_secondary_axis,
    spreading_ratio,
    obs_owner,
    obs_local,
    batch_order,
    obs_reach,
    obs_value,
    obs_variance,
    obs_noise,
):
    block_x, block_y, levels, members = ensemble.shape
    current_vector = ensemble
    for step in range(STEPS):
        bordered_grid = with_halo(current_vector, (("gx", 0), ("gy", 1)), 1)
        current_vector = propagate_prediction(
            bordered_grid, cfl_ratio_primary_axis, cfl_ratio_secondary_axis, spreading_ratio
        )
    row_index = lax.axis_index("gx")
    col_index = lax.axis_index("gy")
    span_y = lax.axis_size("gy")
    myself = row_index * span_y + col_index
    owner = obs_owner[batch_order]
    local = obs_local[batch_order]
    ix = local // (block_y * levels)
    iy = local // levels % block_y
    lev = local % levels
    fx = (owner // span_y * block_x + ix - row_index * block_x).astype(F32)
    fy = (owner % span_y * block_y + iy - col_index * block_y).astype(F32)
    reach = obs_reach[batch_order].astype(F32)
    count = local.shape[0]
    batches = count // OB

    def lanes(v):
        v = v.reshape(batches, OB)
        return jnp.concatenate([v, v], axis=1)

    root = jnp.sqrt(obs_variance[batch_order])
    inv = 1.0 / root
    wanted = obs_noise[batch_order] + (obs_value[batch_order] * inv)[:, None]
    state = jnp.transpose(current_vector, (0, 2, 1, 3))
    flat = state.reshape(-1, members)
    picked = jnp.take(flat, (ix * levels + lev) * block_y + iy, axis=0)
    picked = picked * jnp.where(owner == myself, inv, 0.0)[:, None]
    seen = lax.psum(picked, ("gx", "gy"))
    args = (
        lanes(fx),
        lanes(fy),
        lanes(1.0 / (reach * reach)),
        jnp.broadcast_to(fx[:, None], (count, members)),
        jnp.broadcast_to(fy[:, None], (count, members)),
        seen,
        wanted,
        state,
    )
    out = pl.pallas_call(
        assimilate,
        out_shape=jax.ShapeDtypeStruct(state.shape, F32),
        in_specs=[pl.BlockSpec(memory_space=pltpu.VMEM)] * len(args),
        out_specs=pl.BlockSpec(memory_space=pltpu.VMEM),
        scratch_shapes=[
            pltpu.VMEM((count, members), F32),
            pltpu.VMEM((OB, 2 * OB), F32),
            pltpu.VMEM((OB, members), F32),
        ],
        name="assimilate",
    )(*args)
    return jnp.transpose(out, (0, 2, 1, 3))


def solution(mesh):
    return jax.shard_map(
        per_device,
        mesh=mesh,
        in_specs=(
            P("gx", "gy", None, None),
            P("gx", "gy", None),
            P("gx", "gy", None),
            P("gx", "gy", None),
            P(),
            P(),
            P(),
            P(),
            P(),
            P(),
            P(),
        ),
        out_specs=P("gx", "gy", None, None),
        check_vma=False,
    )
```

```python
import jax
import jax.numpy as jnp
from jax import lax
from jax.experimental import pallas as pl
from jax.experimental.pallas import tpu as pltpu
from jax.sharding import PartitionSpec as P

OB = 64
MESH = pl.DeviceIdType.MESH
ITERS = 5
BOUND = 16.0
F32 = jnp.float32
BF16 = jnp.bfloat16


def forecast(x_ref, coef_ref, edge_ref, out_ref, mid_ref, cols_ref, rows_in, cols_in, send_sem, recv_sem):
    strip, members = rows_in.shape[2:]
    block_x, block_y = coef_ref.shape[:2]
    levels = strip // block_y
    gx, gy = lax.axis_index("gx"), lax.axis_index("gy")
    nx, ny = lax.axis_size("gx"), lax.axis_size("gy")
    west, east = (lax.rem(gx + nx - 1, nx), gy), (lax.rem(gx + 1, nx), gy)
    south, north = (gx, lax.rem(gy + ny - 1, ny)), (gx, lax.rem(gy + 1, ny))
    barrier = pltpu.get_barrier_semaphore()
    for device in (west, east, south, north):
        pl.semaphore_signal(barrier, inc=1, device_id=device, device_id_type=MESH)
    from_west = jnp.where(gx > 0, 1.0, 0.0).astype(F32)
    from_east = jnp.where(gx < nx - 1, 1.0, 0.0).astype(F32)
    from_south = jnp.where(gy > 0, 1.0, 0.0).astype(F32)
    from_north = jnp.where(gy < ny - 1, 1.0, 0.0).astype(F32)
    count = block_x * levels

    def pack(field, turn):
        cols_ref[turn, 0] = field[pl.ds(0, count, stride=block_y), :]
        cols_ref[turn, 1] = field[pl.ds(block_y - 1, count, stride=block_y), :]

    def sends(field, turn):
        last = (block_x - 1) * strip
        plan = (
            (field.at[pl.ds(last, strip)], rows_in.at[turn, 0], east),
            (field.at[pl.ds(0, strip)], rows_in.at[turn, 1], west),
            (cols_ref.at[turn, 1], cols_in.at[turn, 0], north),
            (cols_ref.at[turn, 0], cols_in.at[turn, 1], south),
        )
        return [
            pltpu.make_async_remote_copy(
                src_ref=source,
                dst_ref=target,
                send_sem=send_sem.at[turn, i],
                recv_sem=recv_sem.at[turn, i],
                device_id=device,
                device_id_type=MESH,
            )
            for i, (source, target, device) in enumerate(plan)
        ]

    def strip_of(field, i):
        return [field[pl.ds(pl.multiple_of((i * levels + l) * block_y, block_y), block_y), :] for l in range(levels)]

    def advance(i, centre, left, right, target):
        coef = coef_ref[i]
        for l in range(levels):
            w = [jnp.broadcast_to(coef[:, k * levels + l : k * levels + l + 1], (block_y, members)) for k in range(5)]
            c = centre[l]
            new = w[0] * c + w[1] * left[l] + w[2] * right[l]
            new = new + w[3] * pltpu.roll(c, 1, 0) + w[4] * pltpu.roll(c, block_y - 1, 0)
            target[pl.ds(pl.multiple_of((i * levels + l) * block_y, block_y), block_y), :] = new

    def turn_of(field, target, turn):
        copies = sends(field, turn)
        for copy in copies:
            copy.start()

        def inner(i, _):
            advance(i, strip_of(field, i), strip_of(field, i - 1), strip_of(field, i + 1), target)
            return 0

        lax.fori_loop(1, block_x - 1, inner, 0)
        copies[0].wait_recv()
        left = [rows_in[turn, 0, pl.ds(l * block_y, block_y), :] * from_west for l in range(levels)]
        advance(0, strip_of(field, 0), left, strip_of(field, 1), target)
        copies[1].wait_recv()
        right = [rows_in[turn, 1, pl.ds(l * block_y, block_y), :] * from_east for l in range(levels)]
        last = block_x - 1
        advance(last, strip_of(field, last), strip_of(field, last - 1), right, target)
        edge = edge_ref[...]
        for side, (at, here) in enumerate(((0, from_south), (block_y - 1, from_north))):
            copies[2 + side].wait_recv()
            rows = pl.ds(at, count, stride=block_y)
            gain = jnp.broadcast_to(edge[:, side : side + 1] * here, (count, members))
            target[rows, :] = target[rows, :] + gain * cols_in[turn, side]
        return copies

    pack(x_ref, 0)
    pl.semaphore_wait(barrier, 4)
    first = turn_of(x_ref, mid_ref, 0)
    pack(mid_ref, 1)
    second = turn_of(mid_ref, out_ref, 1)
    for copy in first + second:
        copy.wait_send()


def collect(
    order_ref, place_ref, scale_ref, fx_ref, fy_ref, ir_ref, shift_ref, field_ref, noise_ref,
    y_ref, w_ref, rows_x, rows_y, rows_r, part_ref, half_ref, sum_ref, slots_ref, send_sem, recv_sem,
):
    count = part_ref.shape[0]
    half = count // 2
    gx, gy = lax.axis_index("gx"), lax.axis_index("gy")
    nx, ny = lax.axis_size("gx"), lax.axis_size("gy") // 2
    chips = nx * ny
    piece = half // chips
    core = lax.rem(gy, 2)
    chip = gx * ny + gy // 2
    partner = (gx, gy + 1 - 2 * core)

    def device(t):
        return (t // ny, lax.rem(t, ny) * 2 + core)

    barrier = pltpu.get_barrier_semaphore()
    pl.semaphore_signal(barrier, inc=1, device_id=partner, device_id_type=MESH)

    def greet(k, _):
        pl.semaphore_signal(barrier, inc=1, device_id=device(lax.rem(chip + k, chips)), device_id_type=MESH)
        return 0

    lax.fori_loop(1, chips, greet, 0)
    wide = (1, part_ref.shape[1])

    def pick(g, _):
        for u in range(8):
            k = g * 8 + u
            o = order_ref[k]
            part_ref[pl.ds(k, 1), :] = field_ref[pl.ds(place_ref[o], 1), :] * jnp.full(wide, scale_ref[o])
        return 0

    lax.fori_loop(0, count // 8, pick, 0)

    def prepare(g, _):
        for u in range(8):
            k = g * 8 + u
            o = order_ref[k]
            at = pl.ds(k, 1)
            w_ref[at, :] = noise_ref[pl.ds(o, 1), :] + jnp.full(wide, shift_ref[o])
            rows_x[at, :] = jnp.full(wide, fx_ref[o])
            rows_y[at, :] = jnp.full(wide, fy_ref[o])
            rows_r[at, :] = jnp.full(wide, ir_ref[o])
        return 0

    groups = count // 8
    pl.semaphore_wait(barrier, chips)
    mine = pl.ds(pl.multiple_of(core * half, half), half)
    other = pl.ds(pl.multiple_of((1 - core) * half, half), half)
    swap = pltpu.make_async_remote_copy(
        src_ref=part_ref.at[other], dst_ref=half_ref, send_sem=send_sem.at[0], recv_sem=recv_sem.at[0],
        device_id=partner, device_id_type=MESH,
    )
    swap.start()
    lax.fori_loop(0, groups // 8, prepare, 0)
    swap.wait_recv()
    sum_ref[...] = (part_ref[mine, :] + half_ref[...]).reshape(sum_ref.shape)

    def scatter(k, _):
        t = lax.rem(chip + k, chips)
        pltpu.make_async_remote_copy(
            src_ref=sum_ref.at[t], dst_ref=slots_ref.at[chip], send_sem=send_sem.at[1], recv_sem=recv_sem.at[1],
            device_id=device(t), device_id_type=MESH,
        ).start()
        return 0

    lax.fori_loop(1, chips, scatter, 0)
    slots_ref[chip] = sum_ref[chip]
    lax.fori_loop(groups // 8, groups // 2, prepare, 0)
    some = slots_ref.at[pl.ds(0, chips - 1)]
    pltpu.make_async_copy(some, some, recv_sem.at[1]).wait()
    own = pl.ds(pl.multiple_of(core * half + chip * piece, piece), piece)
    y_ref[own, :] = jnp.sum(slots_ref[...], axis=0)

    def gather(k, _):
        pltpu.make_async_remote_copy(
            src_ref=y_ref.at[own], dst_ref=y_ref.at[own], send_sem=send_sem.at[2], recv_sem=recv_sem.at[2],
            device_id=device(lax.rem(chip + k, chips)), device_id_type=MESH,
        ).start()
        return 0

    lax.fori_loop(1, chips, gather, 0)
    lax.fori_loop(groups // 2, groups, prepare, 0)
    pltpu.make_async_copy(some, some, recv_sem.at[2]).wait()
    share = pltpu.make_async_remote_copy(
        src_ref=y_ref.at[mine], dst_ref=y_ref.at[mine], send_sem=send_sem.at[3], recv_sem=recv_sem.at[3],
        device_id=partner, device_id_type=MESH,
    )
    share.start()
    swap.wait_send()
    pltpu.make_async_copy(some, some, send_sem.at[1]).wait()
    pltpu.make_async_copy(some, some, send_sem.at[2]).wait()
    share.wait()


def split(x):
    high = x.astype(BF16)
    return high, (x - high.astype(F32)).astype(BF16)


def assimilate(rows_x, rows_y, rows_r, y_in, w_ref, x_ref, out_ref, y_ref, t_ref, v_ref):
    block_x, levels, block_y, members = x_ref.shape
    count = y_in.shape[0]
    batches = count // OB
    y_ref[...] = y_in[...]
    out_ref[...] = x_ref[...]
    lane = lax.broadcasted_iota(jnp.int32, (OB, 2 * OB), 1)
    row = lax.broadcasted_iota(jnp.int32, (OB, 2 * OB), 0)
    eye = jnp.where((lane == row) | (lane == row + OB), 1.0, 0.0).astype(F32)
    ys = lax.broadcasted_iota(jnp.int32, (block_y, 1), 0).astype(F32)

    def step(b, _):
        now = pl.ds(pl.multiple_of(b * OB, OB), OB)
        hx = y_ref[now, :]
        centred = hx - jnp.mean(hx, axis=1, keepdims=True)
        high, low = split(centred)
        high2 = jnp.concatenate([high, high], axis=1)
        low2 = jnp.concatenate([low, low], axis=1)
        side = jnp.concatenate([high2, low2, low2, high2], axis=0)

        def project(x):
            both = jnp.concatenate(split(x), axis=1)
            pair = lax.dot_general(both, side, (((1,), (1,)), ((), ())), preferred_element_type=F32)
            return pair[:, : 2 * OB] + pair[:, 2 * OB :]

        p = project(centred) * (1.0 / (members - 1.0))
        norm = jnp.max(jnp.sum(jnp.abs(p), axis=0, keepdims=True), axis=1, keepdims=True)
        c = 1.0 + jnp.maximum(norm, 0.0625)
        top = c + 1.0
        t = top / (c - 1.0)
        alpha = 2.0 / top
        r = ((c - 1.0) / top) * eye - alpha * p
        rhs = w_ref[now, :] - hx
        v = alpha * rhs
        for i in range(ITERS):
            t = 2.0 * t * t - 1.0
            back = 1.0 / t
            gain = 1.0 + back
            rh, rl = split(r)
            vh, vl = split(v)
            left = jnp.concatenate([rh, rl], axis=1)
            head = jnp.concatenate([rh, vh], axis=1)
            tail = jnp.concatenate([rl, vl], axis=1)
            right = jnp.concatenate([head, tail, head, tail], axis=0)
            prod = jnp.dot(left, right, preferred_element_type=F32)
            v = gain * (v + prod[:, 2 * OB :])
            if i + 1 < ITERS:
                r = gain * prod[:, : 2 * OB] - back * eye
        v_ref[...] = v

        @pl.when(jnp.max(norm) > BOUND)
        def _():
            t_ref[...] = p + eye
            v_ref[...] = rhs

            def pivot(k, _):
                at = lane[:1, :] == k
                trow = t_ref[pl.ds(k, 1), :]
                scale = 1.0 / jnp.sum(jnp.where(at, trow, 0.0), axis=1, keepdims=True)
                trow = trow * scale
                vrow = v_ref[pl.ds(k, 1), :] * scale
                mat = t_ref[...]
                col = jnp.sum(jnp.where(lane == k, mat, 0.0), axis=1, keepdims=True)
                mine = row == k
                t_ref[...] = jnp.where(mine, trow, mat - col * trow)
                v_ref[...] = jnp.where(mine, vrow, v_ref[...] - col * vrow)
                return 0

            lax.fori_loop(0, OB, pivot, 0)

        zh, zl = split(v_ref[...] * (1.0 / (members - 1.0)))
        solved = jnp.concatenate([zh, zl, zh, zl], axis=0)

        def spread(g):
            both = jnp.concatenate(split(g), axis=1)
            return jnp.dot(both, solved, preferred_element_type=F32)

        px = jnp.sum(rows_x[now, :] * eye, axis=0, keepdims=True)
        py = jnp.sum(rows_y[now, :] * eye, axis=0, keepdims=True)
        ir = jnp.sum(rows_r[now, :] * eye, axis=0, keepdims=True)

        def later(j, _):
            at = pl.ds(pl.multiple_of(j * OB, OB), OB)
            old = y_ref[at, :]
            dx = rows_x[at, :] - px
            dy = rows_y[at, :] - py
            near = jnp.maximum(1.0 - (dx * dx + dy * dy) * ir, 0.0)
            y_ref[at, :] = old + spread(project(old) * (near * near))
            return 0

        lax.fori_loop(b + 1, batches, later, 0)
        dy = ys - py
        dy2 = dy * dy * ir

        def cells(i, _):
            dx = i.astype(F32) - px
            near = jnp.maximum((1.0 - dx * dx * ir) - dy2, 0.0)
            rho = near * near
            old = out_ref[i].reshape(levels * block_y, members)
            g = project(old).reshape(levels, block_y, members) * rho[None]
            new = old + spread(g.reshape(levels * block_y, members))
            out_ref[i] = new.reshape(levels, block_y, members)
            return 0

        lax.fori_loop(0, block_x, cells, 0)
        return 0

    lax.fori_loop(0, batches, step, 0)


def per_device(
    ensemble,
    cfl_ratio_primary_axis,
    cfl_ratio_secondary_axis,
    spreading_ratio,
    obs_owner,
    obs_local,
    batch_order,
    obs_reach,
    obs_value,
    obs_variance,
    obs_noise,
):
    block_x, block_y, levels, members = ensemble.shape
    span_y = lax.axis_size("gy")
    span = lax.axis_size("gx") * span_y
    row_index = lax.axis_index("gx")
    col_index = lax.axis_index("gy")
    myself = row_index * span_y + col_index
    count = obs_local.shape[0]
    size = block_x * levels * block_y
    strip = levels * block_y
    flat = jnp.transpose(ensemble, (0, 2, 1, 3)).reshape(size, members)
    cx, cy, kd = cfl_ratio_primary_axis, cfl_ratio_secondary_axis, spreading_ratio
    west = kd + jnp.maximum(cx, 0.0)
    east = kd - jnp.minimum(cx, 0.0)
    south = kd + jnp.maximum(cy, 0.0)
    north = kd - jnp.minimum(cy, 0.0)
    centre = 1.0 - (west + east + south + north)
    spot = lax.broadcasted_iota(jnp.int32, cx.shape, 1)
    inner_south = jnp.where(spot == 0, 0.0, south)
    inner_north = jnp.where(spot == block_y - 1, 0.0, north)
    coef = jnp.concatenate([centre, west, east, inner_south, inner_north], axis=2)
    edge = jnp.stack([south[:, 0, :].reshape(-1), north[:, block_y - 1, :].reshape(-1)], axis=1)
    vmem = pl.BlockSpec(memory_space=pltpu.VMEM)
    smem = pl.BlockSpec(memory_space=pltpu.SMEM)
    state = pl.pallas_call(
        forecast,
        out_shape=jax.ShapeDtypeStruct((size, members), F32),
        in_specs=[vmem] * 3,
        out_specs=vmem,
        scratch_shapes=[
            pltpu.VMEM((size, members), F32),
            pltpu.VMEM((2, 2, block_x * levels, members), F32),
            pltpu.VMEM((2, 2, strip, members), F32),
            pltpu.VMEM((2, 2, block_x * levels, members), F32),
            pltpu.SemaphoreType.DMA((2, 4)),
            pltpu.SemaphoreType.DMA((2, 4)),
        ],
        compiler_params=pltpu.CompilerParams(collective_id=0, has_side_effects=True),
        name="forecast",
    )(flat, coef, edge)
    ix = obs_local // (block_y * levels)
    iy = obs_local // levels % block_y
    lev = obs_local % levels
    fx = (obs_owner // span_y * block_x + ix - row_index * block_x).astype(F32)
    fy = (obs_owner % span_y * block_y + iy - col_index * block_y).astype(F32)
    reach = obs_reach.astype(F32)
    inv = lax.rsqrt(obs_variance)
    pieces = span // 2
    table = jax.ShapeDtypeStruct((count, members), F32)
    seen, wanted, rows_x, rows_y, rows_r = pl.pallas_call(
        collect,
        out_shape=[table] * 5,
        in_specs=[smem] * 7 + [vmem] * 2,
        out_specs=[vmem] * 5,
        scratch_shapes=[
            pltpu.VMEM((count, members), F32),
            pltpu.VMEM((count // 2, members), F32),
            pltpu.VMEM((pieces, count // span, members), F32),
            pltpu.VMEM((pieces, count // span, members), F32),
            pltpu.SemaphoreType.DMA((4,)),
            pltpu.SemaphoreType.DMA((4,)),
        ],
        compiler_params=pltpu.CompilerParams(collective_id=1, has_side_effects=True),
        name="collect",
    )(
        batch_order,
        (ix * levels + lev) * block_y + iy,
        jnp.where(obs_owner == myself, inv, 0.0),
        fx,
        fy,
        1.0 / (reach * reach),
        obs_value * inv,
        state,
        obs_noise,
    )
    args = (rows_x, rows_y, rows_r, seen, wanted, state.reshape(block_x, levels, block_y, members))
    out = pl.pallas_call(
        assimilate,
        out_shape=jax.ShapeDtypeStruct((block_x, levels, block_y, members), F32),
        in_specs=[vmem] * len(args),
        out_specs=vmem,
        scratch_shapes=[
            pltpu.VMEM((count, members), F32),
            pltpu.VMEM((OB, 2 * OB), F32),
            pltpu.VMEM((OB, members), F32),
        ],
        name="assimilate",
    )(*args)
    return jnp.transpose(out, (0, 2, 1, 3))


def solution(mesh):
    return jax.shard_map(
        per_device,
        mesh=mesh,
        in_specs=(
            P("gx", "gy", None, None),
            P("gx", "gy", None),
            P("gx", "gy", None),
            P("gx", "gy", None),
            P(),
            P(),
            P(),
            P(),
            P(),
            P(),
            P(),
        ),
        out_specs=P("gx", "gy", None, None),
        check_vma=False,
    )
```

```python
import functools

import jax
import jax.numpy as jnp
from jax import lax
from jax.experimental import pallas as pl
from jax.experimental.pallas import tpu as pltpu
from jax.sharding import PartitionSpec as P

OB = 64
QUICK = 6.5
WIDE = 63.0
LONG = 6
MESH = pl.DeviceIdType.MESH
F32 = jnp.float32
BF16 = jnp.bfloat16


def forecast(x_ref, coef_ref, edge_ref, out_ref, mid_ref, cols_ref, rows_in, cols_in, send_sem, recv_sem):
    strip, members = rows_in.shape[2:]
    block_x, block_y = coef_ref.shape[:2]
    levels = strip // block_y
    gx, gy = lax.axis_index("gx"), lax.axis_index("gy")
    nx, ny = lax.axis_size("gx"), lax.axis_size("gy")
    west, east = (lax.rem(gx + nx - 1, nx), gy), (lax.rem(gx + 1, nx), gy)
    south, north = (gx, lax.rem(gy + ny - 1, ny)), (gx, lax.rem(gy + 1, ny))
    barrier = pltpu.get_barrier_semaphore()
    for device in (west, east, south, north):
        pl.semaphore_signal(barrier, inc=1, device_id=device, device_id_type=MESH)
    from_west = jnp.where(gx > 0, 1.0, 0.0).astype(F32)
    from_east = jnp.where(gx < nx - 1, 1.0, 0.0).astype(F32)
    from_south = jnp.where(gy > 0, 1.0, 0.0).astype(F32)
    from_north = jnp.where(gy < ny - 1, 1.0, 0.0).astype(F32)
    count = block_x * levels

    def pack(field, turn):
        cols_ref[turn, 0] = field[pl.ds(0, count, stride=block_y), :]
        cols_ref[turn, 1] = field[pl.ds(block_y - 1, count, stride=block_y), :]

    def sends(field, turn):
        last = (block_x - 1) * strip
        plan = (
            (field.at[pl.ds(last, strip)], rows_in.at[turn, 0], east),
            (field.at[pl.ds(0, strip)], rows_in.at[turn, 1], west),
            (cols_ref.at[turn, 1], cols_in.at[turn, 0], north),
            (cols_ref.at[turn, 0], cols_in.at[turn, 1], south),
        )
        return [
            pltpu.make_async_remote_copy(
                src_ref=source,
                dst_ref=target,
                send_sem=send_sem.at[turn, i],
                recv_sem=recv_sem.at[turn, i],
                device_id=device,
                device_id_type=MESH,
            )
            for i, (source, target, device) in enumerate(plan)
        ]

    def strip_of(field, i):
        return [field[pl.ds(pl.multiple_of((i * levels + l) * block_y, block_y), block_y), :] for l in range(levels)]

    def advance(i, centre, left, right, target):
        coef = coef_ref[i]
        for l in range(levels):
            w = [jnp.broadcast_to(coef[:, k * levels + l : k * levels + l + 1], (block_y, members)) for k in range(5)]
            c = centre[l]
            new = w[0] * c + w[1] * left[l] + w[2] * right[l]
            new = new + w[3] * pltpu.roll(c, 1, 0) + w[4] * pltpu.roll(c, block_y - 1, 0)
            target[pl.ds(pl.multiple_of((i * levels + l) * block_y, block_y), block_y), :] = new

    def turn_of(field, target, turn):
        copies = sends(field, turn)
        for copy in copies:
            copy.start()

        def inner(i, _):
            advance(i, strip_of(field, i), strip_of(field, i - 1), strip_of(field, i + 1), target)
            return 0

        lax.fori_loop(1, block_x - 1, inner, 0)
        copies[0].wait_recv()
        left = [rows_in[turn, 0, pl.ds(l * block_y, block_y), :] * from_west for l in range(levels)]
        advance(0, strip_of(field, 0), left, strip_of(field, 1), target)
        copies[1].wait_recv()
        right = [rows_in[turn, 1, pl.ds(l * block_y, block_y), :] * from_east for l in range(levels)]
        last = block_x - 1
        advance(last, strip_of(field, last), strip_of(field, last - 1), right, target)
        edge = edge_ref[...]
        for side, (at, here) in enumerate(((0, from_south), (block_y - 1, from_north))):
            copies[2 + side].wait_recv()
            rows = pl.ds(at, count, stride=block_y)
            gain = jnp.broadcast_to(edge[:, side : side + 1] * here, (count, members))
            target[rows, :] = target[rows, :] + gain * cols_in[turn, side]
        return copies

    pack(x_ref, 0)
    pl.semaphore_wait(barrier, 4)
    first = turn_of(x_ref, mid_ref, 0)
    pack(mid_ref, 1)
    second = turn_of(mid_ref, out_ref, 1)
    for copy in first + second:
        copy.wait_send()


def collect(
    order_ref, place_ref, scale_ref, fx_ref, fy_ref, ir_ref, shift_ref, field_ref, noise_ref,
    y_ref, w_ref, rows_x, rows_y, rows_r, part_ref, half_ref, sum_ref, slots_ref, send_sem, recv_sem,
):
    count = part_ref.shape[0]
    half = count // 2
    gx, gy = lax.axis_index("gx"), lax.axis_index("gy")
    nx, ny = lax.axis_size("gx"), lax.axis_size("gy") // 2
    chips = nx * ny
    piece = half // chips
    core = lax.rem(gy, 2)
    chip = gx * ny + gy // 2
    partner = (gx, gy + 1 - 2 * core)

    def device(t):
        return (t // ny, lax.rem(t, ny) * 2 + core)

    barrier = pltpu.get_barrier_semaphore()
    pl.semaphore_signal(barrier, inc=1, device_id=partner, device_id_type=MESH)

    def greet(k, _):
        pl.semaphore_signal(barrier, inc=1, device_id=device(lax.rem(chip + k, chips)), device_id_type=MESH)
        return 0

    lax.fori_loop(1, chips, greet, 0)
    wide = (1, part_ref.shape[1])

    def pick(g, _):
        for u in range(8):
            k = g * 8 + u
            o = order_ref[k]
            part_ref[pl.ds(k, 1), :] = field_ref[pl.ds(place_ref[o], 1), :] * jnp.full(wide, scale_ref[o])
        return 0

    lax.fori_loop(0, count // 8, pick, 0)

    def prepare(g, _):
        for u in range(8):
            k = g * 8 + u
            o = order_ref[k]
            at = pl.ds(k, 1)
            w_ref[at, :] = noise_ref[pl.ds(o, 1), :] + jnp.full(wide, shift_ref[o])
            rows_x[at, :] = jnp.full(wide, fx_ref[o])
            rows_y[at, :] = jnp.full(wide, fy_ref[o])
            rows_r[at, :] = jnp.full(wide, ir_ref[o])
        return 0

    groups = count // 8
    pl.semaphore_wait(barrier, chips)
    mine = pl.ds(pl.multiple_of(core * half, half), half)
    other = pl.ds(pl.multiple_of((1 - core) * half, half), half)
    swap = pltpu.make_async_remote_copy(
        src_ref=part_ref.at[other], dst_ref=half_ref, send_sem=send_sem.at[0], recv_sem=recv_sem.at[0],
        device_id=partner, device_id_type=MESH,
    )
    swap.start()
    lax.fori_loop(0, groups // 8, prepare, 0)
    swap.wait_recv()
    sum_ref[...] = (part_ref[mine, :] + half_ref[...]).reshape(sum_ref.shape)

    def scatter(k, _):
        t = lax.rem(chip + k, chips)
        pltpu.make_async_remote_copy(
            src_ref=sum_ref.at[t], dst_ref=slots_ref.at[chip], send_sem=send_sem.at[1], recv_sem=recv_sem.at[1],
            device_id=device(t), device_id_type=MESH,
        ).start()
        return 0

    lax.fori_loop(1, chips, scatter, 0)
    slots_ref[chip] = sum_ref[chip]
    lax.fori_loop(groups // 8, groups // 2, prepare, 0)
    some = slots_ref.at[pl.ds(0, chips - 1)]
    pltpu.make_async_copy(some, some, recv_sem.at[1]).wait()
    own = pl.ds(pl.multiple_of(core * half + chip * piece, piece), piece)
    y_ref[own, :] = jnp.sum(slots_ref[...], axis=0)

    def gather(k, _):
        pltpu.make_async_remote_copy(
            src_ref=y_ref.at[own], dst_ref=y_ref.at[own], send_sem=send_sem.at[2], recv_sem=recv_sem.at[2],
            device_id=device(lax.rem(chip + k, chips)), device_id_type=MESH,
        ).start()
        return 0

    lax.fori_loop(1, chips, gather, 0)
    lax.fori_loop(groups // 2, groups, prepare, 0)
    pltpu.make_async_copy(some, some, recv_sem.at[2]).wait()
    share = pltpu.make_async_remote_copy(
        src_ref=y_ref.at[mine], dst_ref=y_ref.at[mine], send_sem=send_sem.at[3], recv_sem=recv_sem.at[3],
        device_id=partner, device_id_type=MESH,
    )
    share.start()
    swap.wait_send()
    pltpu.make_async_copy(some, some, send_sem.at[1]).wait()
    pltpu.make_async_copy(some, some, send_sem.at[2]).wait()
    share.wait()


def split(x):
    high = x.astype(BF16)
    return high, (x - high.astype(F32)).astype(BF16)


def wide(x):
    return jnp.concatenate(split(x), axis=1)


def project(side, x):
    pair = lax.dot_general(wide(x), side, (((1,), (1,)), ((), ())), preferred_element_type=F32)
    half = pair.shape[1] // 2
    return pair[:, :half] + pair[:, half:]


def spread(solved, g):
    return jnp.dot(wide(g), solved, preferred_element_type=F32)


def stack_solved(v, scale):
    high, low = split(v * scale)
    return jnp.concatenate([high, low, high, low], axis=0)


def sharpen(r, v, t, eye, last):
    t = 2.0 * t * t - 1.0
    back = 1.0 / t
    gain = 1.0 + back
    rh, rl = split(r)
    vh, vl = split(v)
    left = jnp.concatenate([rh, rl], axis=1)
    head = jnp.concatenate([rh, vh], axis=1)
    tail = jnp.concatenate([rl, vl], axis=1)
    right = jnp.concatenate([head, tail, head, tail], axis=0)
    prod = jnp.dot(left, right, preferred_element_type=F32)
    v = gain * (v + prod[:, 2 * OB :])
    r = None if last else gain * prod[:, : 2 * OB] - back * eye
    return r, v, t


def begin(p, rhs, norm, eye):
    c = 1.0 + jnp.maximum(norm, 0.0625)
    top = c + 1.0
    alpha = 2.0 / top
    return ((c - 1.0) / top) * eye - alpha * p, alpha * rhs, top / (c - 1.0)


def assimilate(
    rows_x, rows_y, rows_r, y_in, w_ref, x_ref, out_ref, y_ref, t_ref, v_ref, cur_ref, side_ref, solved_ref, lanes_ref
):
    block_x, levels, block_y, members = x_ref.shape
    count = y_in.shape[0]
    batches = count // OB
    scale = 1.0 / (members - 1.0)
    y_ref[...] = y_in[...]
    out_ref[...] = x_ref[...]
    cur_ref[...] = y_in[pl.ds(0, OB), :]
    side_ref[...] = jnp.zeros_like(side_ref)
    solved_ref[...] = jnp.zeros_like(solved_ref)
    lanes_ref[...] = jnp.zeros_like(lanes_ref)
    lane = lax.broadcasted_iota(jnp.int32, (OB, 2 * OB), 1)
    row = lax.broadcasted_iota(jnp.int32, (OB, 2 * OB), 0)
    eye = jnp.where((lane == row) | (lane == row + OB), 1.0, 0.0).astype(F32)
    ys = lax.broadcasted_iota(jnp.int32, (block_y, 1), 0).astype(F32)

    def rho_rows(at, px, py, ir):
        dx = rows_x[at, :] - px
        dy = rows_y[at, :] - py
        near = jnp.maximum(1.0 - (dx * dx + dy * dy) * ir, 0.0)
        return near * near

    def cells(n, side, solved, px, dy2, ir):
        rhos = []
        for u in range(6):
            dx = jnp.float32(1.0) * (n * 6 + u) - px
            near = jnp.maximum((1.0 - dx * dx * ir) - dy2, 0.0)
            rhos.append((near * near)[None, None])
        rho = jnp.concatenate(rhos, axis=0)
        at = pl.ds(n * 6, 6)
        old = out_ref[at].reshape(6 * levels * block_y, members)
        g = project(side, old).reshape(6, levels, block_y, members) * rho
        new = old + spread(solved, g.reshape(6 * levels * block_y, members))
        out_ref[at] = new.reshape(6, levels, block_y, members)

    def previous():
        px, py, ir = lanes_ref[pl.ds(0, 1), :], lanes_ref[pl.ds(1, 1), :], lanes_ref[pl.ds(2, 1), :]
        dy = ys - py
        return side_ref[...], solved_ref[...], px, py, dy * dy * ir, ir

    def step(first, b, _):
        now = pl.ds(pl.multiple_of(b * OB, OB), OB)
        after = pl.ds(pl.multiple_of(jnp.minimum(b + 1, batches - 1) * OB, OB), OB)
        side0, solved0, px0, py0, dy20, ir0 = previous()

        def later(start, size):
            at = pl.ds(start, size)
            old = y_ref[at, :]
            y_ref[at, :] = old + spread(solved0, project(side0, old) * rho_rows(at, px0, py0, ir0))

        pieces = []
        for start in range((first + 1) * OB, count, 384):
            pieces.append(functools.partial(later, start, min(384, count - start)))
        ahead_of = len(pieces)
        for n in range(block_x // 6):
            pieces.append(functools.partial(cells, n, side0, solved0, px0, dy20, ir0))
        plan = list([0.15, 0.3, 0.45, 0.6, 0.75, 0.9, 1])
        total = len(pieces)
        done = [0]

        def fill():
            share = plan.pop(0)
            upto = total if not plan else min(total, round(share * total))
            while done[0] < upto:
                pieces[done[0]]()
                done[0] += 1

        hx = cur_ref[...]
        centred = hx - jnp.mean(hx, axis=1, keepdims=True)
        high, low = split(centred)
        high2 = jnp.concatenate([high, high], axis=1)
        low2 = jnp.concatenate([low, low], axis=1)
        side = jnp.concatenate([high2, low2, low2, high2], axis=0)
        fill()
        p = project(side, centred) * scale
        fill()
        norm = jnp.max(jnp.sum(jnp.abs(p), axis=0, keepdims=True), axis=1, keepdims=True)
        rhs = w_ref[now, :] - hx
        r, v, t = begin(p, rhs, norm, eye)
        for i in range(4):
            r, v, t = sharpen(r, v, t, eye, i + 1 == 4)
            fill()
            if i == 4 - 2:
                while done[0] < ahead_of:
                    pieces[done[0]]()
                    done[0] += 1
                ahead = y_ref[after, :]
                px = jnp.sum(rows_x[now, :] * eye, axis=0, keepdims=True)
                py = jnp.sum(rows_y[now, :] * eye, axis=0, keepdims=True)
                ir = jnp.sum(rows_r[now, :] * eye, axis=0, keepdims=True)
                g = project(side, ahead) * rho_rows(after, px, py, ir)
        new_solved = stack_solved(v, scale)
        fresh = ahead + spread(new_solved, g)
        fill()
        side_ref[...] = side
        solved_ref[...] = new_solved
        lanes_ref[pl.ds(0, 1), :] = px
        lanes_ref[pl.ds(1, 1), :] = py
        lanes_ref[pl.ds(2, 1), :] = ir
        cur_ref[...] = fresh

        @pl.when(jnp.max(norm) > QUICK)
        def _():
            t_ref[...] = p + eye
            v_ref[...] = rhs

            @pl.when(jnp.max(norm) <= WIDE)
            def _():
                r, v, t = begin(p, rhs, norm, eye)
                for i in range(LONG):
                    r, v, t = sharpen(r, v, t, eye, i + 1 == LONG)
                v_ref[...] = v

            @pl.when(jnp.max(norm) > WIDE)
            def _():
                lax.fori_loop(0, OB, pivot, 0)

            exact = stack_solved(v_ref[...], scale)
            solved_ref[...] = exact
            cur_ref[...] = ahead + spread(exact, g)

        return 0

    def pivot(k, _):
        trow = t_ref[pl.ds(k, 1), :]
        here = lane[:1, :] == k
        inverse = 1.0 / jnp.sum(jnp.where(here, trow, 0.0), axis=1, keepdims=True)
        trow = trow * inverse
        vrow = v_ref[pl.ds(k, 1), :] * inverse
        mat = t_ref[...]
        col = jnp.sum(jnp.where(lane == k, mat, 0.0), axis=1, keepdims=True)
        mine = row == k
        t_ref[...] = jnp.where(mine, trow, mat - col * trow)
        v_ref[...] = jnp.where(mine, vrow, v_ref[...] - col * vrow)
        return 0

    for first in range(0, batches, 4):
        lax.fori_loop(first, min(first + 4, batches), functools.partial(step, first), 0)
    side, solved, px, _, dy2, ir = previous()
    for n in range(block_x // 6):
        cells(n, side, solved, px, dy2, ir)


def run_assimilate(*args):
    vmem = pl.BlockSpec(memory_space=pltpu.VMEM)
    count, members = args[0].shape
    return pl.pallas_call(
        assimilate,
        out_shape=jax.ShapeDtypeStruct(args[-1].shape, F32),
        in_specs=[vmem] * len(args),
        out_specs=vmem,
        scratch_shapes=[
            pltpu.VMEM((count, members), F32),
            pltpu.VMEM((OB, 2 * OB), F32),
            pltpu.VMEM((OB, members), F32),
            pltpu.VMEM((OB, members), F32),
            pltpu.VMEM((4 * OB, 2 * members), BF16),
            pltpu.VMEM((4 * OB, members), BF16),
            pltpu.VMEM((8, members), F32),
        ],
        name="assimilate",
    )(*args)


def per_device(
    ensemble,
    cfl_ratio_primary_axis,
    cfl_ratio_secondary_axis,
    spreading_ratio,
    obs_owner,
    obs_local,
    batch_order,
    obs_reach,
    obs_value,
    obs_variance,
    obs_noise,
):
    block_x, block_y, levels, members = ensemble.shape
    span_y = lax.axis_size("gy")
    span = lax.axis_size("gx") * span_y
    row_index = lax.axis_index("gx")
    col_index = lax.axis_index("gy")
    myself = row_index * span_y + col_index
    count = obs_local.shape[0]
    size = block_x * levels * block_y
    strip = levels * block_y
    flat = jnp.transpose(ensemble, (0, 2, 1, 3)).reshape(size, members)
    cx, cy, kd = cfl_ratio_primary_axis, cfl_ratio_secondary_axis, spreading_ratio
    west = kd + jnp.maximum(cx, 0.0)
    east = kd - jnp.minimum(cx, 0.0)
    south = kd + jnp.maximum(cy, 0.0)
    north = kd - jnp.minimum(cy, 0.0)
    centre = 1.0 - (west + east + south + north)
    spot = lax.broadcasted_iota(jnp.int32, cx.shape, 1)
    inner_south = jnp.where(spot == 0, 0.0, south)
    inner_north = jnp.where(spot == block_y - 1, 0.0, north)
    coef = jnp.concatenate([centre, west, east, inner_south, inner_north], axis=2)
    edge = jnp.stack([south[:, 0, :].reshape(-1), north[:, block_y - 1, :].reshape(-1)], axis=1)
    vmem = pl.BlockSpec(memory_space=pltpu.VMEM)
    smem = pl.BlockSpec(memory_space=pltpu.SMEM)
    state = pl.pallas_call(
        forecast,
        out_shape=jax.ShapeDtypeStruct((size, members), F32),
        in_specs=[vmem] * 3,
        out_specs=vmem,
        scratch_shapes=[
            pltpu.VMEM((size, members), F32),
            pltpu.VMEM((2, 2, block_x * levels, members), F32),
            pltpu.VMEM((2, 2, strip, members), F32),
            pltpu.VMEM((2, 2, block_x * levels, members), F32),
            pltpu.SemaphoreType.DMA((2, 4)),
            pltpu.SemaphoreType.DMA((2, 4)),
        ],
        compiler_params=pltpu.CompilerParams(collective_id=0, has_side_effects=True),
        name="forecast",
    )(flat, coef, edge)
    ix = obs_local // (block_y * levels)
    iy = obs_local // levels % block_y
    lev = obs_local % levels
    fx = (obs_owner // span_y * block_x + ix - row_index * block_x).astype(F32)
    fy = (obs_owner % span_y * block_y + iy - col_index * block_y).astype(F32)
    reach = obs_reach.astype(F32)
    inv = lax.rsqrt(obs_variance)
    pieces = span // 2
    table = jax.ShapeDtypeStruct((count, members), F32)
    seen, wanted, rows_x, rows_y, rows_r = pl.pallas_call(
        collect,
        out_shape=[table] * 5,
        in_specs=[smem] * 7 + [vmem] * 2,
        out_specs=[vmem] * 5,
        scratch_shapes=[
            pltpu.VMEM((count, members), F32),
            pltpu.VMEM((count // 2, members), F32),
            pltpu.VMEM((pieces, count // span, members), F32),
            pltpu.VMEM((pieces, count // span, members), F32),
            pltpu.SemaphoreType.DMA((4,)),
            pltpu.SemaphoreType.DMA((4,)),
        ],
        compiler_params=pltpu.CompilerParams(collective_id=1, has_side_effects=True),
        name="collect",
    )(
        batch_order,
        (ix * levels + lev) * block_y + iy,
        jnp.where(obs_owner == myself, inv, 0.0),
        fx,
        fy,
        1.0 / (reach * reach),
        obs_value * inv,
        state,
        obs_noise,
    )
    out = run_assimilate(
        rows_x, rows_y, rows_r, seen, wanted, state.reshape(block_x, levels, block_y, members)
    )
    return jnp.transpose(out, (0, 2, 1, 3))


def solution(mesh):
    return jax.shard_map(
        per_device,
        mesh=mesh,
        in_specs=(
            P("gx", "gy", None, None),
            P("gx", "gy", None),
            P("gx", "gy", None),
            P("gx", "gy", None),
            P(),
            P(),
            P(),
            P(),
            P(),
            P(),
            P(),
        ),
        out_specs=P("gx", "gy", None, None),
        check_vma=False,
    )
```

```python
import functools

import jax
import jax.numpy as jnp
from jax import lax
from jax.experimental import pallas as pl
from jax.experimental.pallas import tpu as pltpu
from jax.sharding import PartitionSpec as P

OB = 64
QUICK = 6.5
WIDE = 63.0
LONG = 6
MESH = pl.DeviceIdType.MESH
F32 = jnp.float32
BF16 = jnp.bfloat16


def floor_div(x, n):
    return jnp.floor((x.astype(F32) + 0.5) * (1.0 / n)).astype(jnp.int32)


def thirds(x):
    high = x.astype(BF16).astype(F32)
    rest = x - high
    mid = rest.astype(BF16).astype(F32)
    return [high, mid, rest - mid]


def forecast(
    x_ref, cx_ref, cy_ref, kd_ref, owner_ref, local_ref, reach_ref, value_ref, variance_ref,
    out_ref, place_ref, code_ref, inv_ref, shift_ref,
    mid_ref, wide_ref, flip_ref, cols_ref, rows_in, cols_in, send_sem, recv_sem,
):
    strip, members = rows_in.shape[2:]
    block_y = cx_ref.shape[1]
    levels = strip // block_y
    block_x = cx_ref.shape[0] // levels
    count = block_x * levels
    size = count * block_y
    gx, gy = lax.axis_index("gx"), lax.axis_index("gy")
    nx, ny = lax.axis_size("gx"), lax.axis_size("gy")
    west, east = (lax.rem(gx + nx - 1, nx), gy), (lax.rem(gx + 1, nx), gy)
    south, north = (gx, lax.rem(gy + ny - 1, ny)), (gx, lax.rem(gy + 1, ny))
    barrier = pltpu.get_barrier_semaphore()
    for device in (west, east, south, north):
        pl.semaphore_signal(barrier, inc=1, device_id=device, device_id_type=MESH)
    from_west = jnp.where(gx > 0, 1.0, 0.0).astype(F32)
    from_east = jnp.where(gx < nx - 1, 1.0, 0.0).astype(F32)
    from_south = jnp.where(gy > 0, 1.0, 0.0).astype(F32)
    from_north = jnp.where(gy < ny - 1, 1.0, 0.0).astype(F32)

    def pack(field, turn):
        cols_ref[turn, 0] = field[pl.ds(0, count, stride=block_y), :]
        cols_ref[turn, 1] = field[pl.ds(block_y - 1, count, stride=block_y), :]

    def sends(field, turn):
        last = (block_x - 1) * strip
        plan = (
            (field.at[pl.ds(last, strip)], rows_in.at[turn, 0], east),
            (field.at[pl.ds(0, strip)], rows_in.at[turn, 1], west),
            (cols_ref.at[turn, 1], cols_in.at[turn, 0], north),
            (cols_ref.at[turn, 0], cols_in.at[turn, 1], south),
        )
        return [
            pltpu.make_async_remote_copy(
                src_ref=source,
                dst_ref=target,
                send_sem=send_sem.at[turn, i],
                recv_sem=recv_sem.at[turn, i],
                device_id=device,
                device_id_type=MESH,
            )
            for i, (source, target, device) in enumerate(plan)
        ]

    def rows_of(i, l):
        return pl.ds(pl.multiple_of((i * levels + l) * block_y, block_y), block_y)

    def strip_of(field, i):
        return [field[rows_of(i, l), :] for l in range(levels)]

    zero = jnp.zeros((1, members), F32)

    def advance(i, centre, left, right, target):
        for l in range(levels):
            w = [wide_ref[k, rows_of(i, l), :] for k in range(5)]
            c = centre[l]
            new = w[0] * c + w[1] * left[l] + w[2] * right[l]
            new = new + w[3] * jnp.concatenate([zero, c[:-1]], axis=0)
            new = new + w[4] * jnp.concatenate([c[1:], zero], axis=0)
            target[rows_of(i, l), :] = new

    def turn_of(field, target, turn):
        copies = sends(field, turn)
        for copy in copies:
            copy.start()

        def inner(i, _):
            advance(i, strip_of(field, i), strip_of(field, i - 1), strip_of(field, i + 1), target)
            return 0

        lax.fori_loop(1, block_x - 1, inner, 0)
        copies[0].wait_recv()
        left = [rows_in[turn, 0, pl.ds(l * block_y, block_y), :] * from_west for l in range(levels)]
        advance(0, strip_of(field, 0), left, strip_of(field, 1), target)
        copies[1].wait_recv()
        right = [rows_in[turn, 1, pl.ds(l * block_y, block_y), :] * from_east for l in range(levels)]
        last = block_x - 1
        advance(last, strip_of(field, last), strip_of(field, last - 1), right, target)
        for side, (at, here) in enumerate(((0, from_south), (block_y - 1, from_north))):
            copies[2 + side].wait_recv()
            rows = pl.ds(at, count, stride=block_y)
            target[rows, :] = target[rows, :] + wide_ref[3 + side, rows, :] * (cols_in[turn, side] * here)
        return copies

    pack(x_ref, 0)

    def flip(i, _):
        rows = pl.ds(i, levels, stride=block_x)
        cx, cy, kd = cx_ref[rows, :], cy_ref[rows, :], kd_ref[rows, :]
        w1, w2 = kd + jnp.maximum(cx, 0.0), kd - jnp.minimum(cx, 0.0)
        w3, w4 = kd + jnp.maximum(cy, 0.0), kd - jnp.minimum(cy, 0.0)
        packed = jnp.concatenate([1.0 - (w1 + w2 + w3 + w4), w1, w2, w3, w4], axis=0)
        packed = jnp.concatenate(thirds(packed), axis=0)
        at = pl.ds(pl.multiple_of(i * block_y, block_y), block_y)
        flip_ref[at, pl.ds(0, 15 * levels)] = packed.T
        return 0

    lax.fori_loop(0, block_x, flip, 0, unroll=4)
    kinds = 5 * levels
    r = lax.broadcasted_iota(jnp.int32, (3 * kinds, members), 0)
    pick = [((r == k) | (r == k + kinds) | (r == k + 2 * kinds)).astype(F32).astype(BF16) for k in range(kinds)]
    pair = 2 * block_y

    def widen(n, _):
        left = flip_ref[pl.ds(pl.multiple_of(n * pair, pair), pair), pl.ds(0, 3 * kinds)].astype(BF16)
        for k in range(0, kinds, 2):
            right = jnp.concatenate(pick[k : k + 2], axis=1)
            spread_out = jnp.dot(left, right, preferred_element_type=F32)
            for u in range(2):
                for v in range(2):
                    kind, l = divmod(k + v, levels)
                    piece = spread_out[u * block_y : (u + 1) * block_y, v * members : (v + 1) * members]
                    wide_ref[kind, rows_of(n * 2 + u, l), :] = piece
        return 0

    lax.fori_loop(0, block_x // 2, widen, 0)
    local, owner = local_ref[...], owner_ref[...]
    ix = floor_div(local, block_y * levels)
    rest = local - ix * (block_y * levels)
    iy = floor_div(rest, levels)
    lev = rest - iy * levels
    ox = floor_div(owner, ny)
    oy = owner - ox * ny
    mine = owner == gx * ny + gy
    place_ref[...] = jnp.where(mine, (ix * levels + lev) * block_y + iy, size)
    px = (ox - gx) * block_x + ix + nx * block_x
    py = (oy - gy) * block_y + iy + ny * block_y
    code_ref[...] = (px * 1024 + py) * 128 + reach_ref[...]
    inv = lax.rsqrt(variance_ref[...])
    inv_ref[...] = inv
    shift_ref[...] = value_ref[...] * inv
    out_ref[pl.ds(size, 8), :] = jnp.zeros((8, members), F32)
    pl.semaphore_wait(barrier, 4)
    first = turn_of(x_ref, mid_ref, 0)
    pack(mid_ref, 1)
    second = turn_of(mid_ref, out_ref, 1)
    for copy in first + second:
        copy.wait_send()


def collect(
    order_ref, place_ref, code_ref, inv_ref, shift_ref, field_ref, noise_ref,
    y_ref, w_ref, rows_c, rows_i, part_ref, half_ref, sum_ref, slots_ref, send_sem, recv_sem,
):
    count = part_ref.shape[0]
    half = count // 2
    gx, gy = lax.axis_index("gx"), lax.axis_index("gy")
    nx, ny = lax.axis_size("gx"), lax.axis_size("gy") // 2
    chips = nx * ny
    piece = half // chips
    core = lax.rem(gy, 2)
    chip = gx * ny + gy // 2
    partner = (gx, gy + 1 - 2 * core)

    def device(t):
        return (t // ny, lax.rem(t, ny) * 2 + core)

    barrier = pltpu.get_barrier_semaphore()
    pl.semaphore_signal(barrier, inc=1, device_id=partner, device_id_type=MESH)

    def greet(k, _):
        pl.semaphore_signal(barrier, inc=1, device_id=device(lax.rem(chip + k, chips)), device_id_type=MESH)
        return 0

    lax.fori_loop(1, chips, greet, 0)
    wide = (1, part_ref.shape[1])

    def pick(g, _):
        for u in range(8):
            k = g * 8 + u
            part_ref[pl.ds(k, 1), :] = field_ref[pl.ds(place_ref[order_ref[k]], 1), :]
        return 0

    lax.fori_loop(0, count // 8, pick, 0)

    def prepare(g, _):
        for u in range(8):
            k = g * 8 + u
            o = order_ref[k]
            at = pl.ds(k, 1)
            w_ref[at, :] = noise_ref[pl.ds(o, 1), :] + jnp.full(wide, shift_ref[o])
            rows_c[at, :] = jnp.full(wide, code_ref[o])
            rows_i[at, :] = jnp.full(wide, inv_ref[o])
        return 0

    groups = count // 8
    pl.semaphore_wait(barrier, chips)
    mine = pl.ds(pl.multiple_of(core * half, half), half)
    other = pl.ds(pl.multiple_of((1 - core) * half, half), half)
    swap = pltpu.make_async_remote_copy(
        src_ref=part_ref.at[other], dst_ref=half_ref, send_sem=send_sem.at[0], recv_sem=recv_sem.at[0],
        device_id=partner, device_id_type=MESH,
    )
    swap.start()
    lax.fori_loop(0, groups // 8, prepare, 0)
    swap.wait_recv()
    sum_ref[...] = (part_ref[mine, :] + half_ref[...]).reshape(sum_ref.shape)

    def scatter(k, _):
        t = lax.rem(chip + k, chips)
        pltpu.make_async_remote_copy(
            src_ref=sum_ref.at[t], dst_ref=slots_ref.at[chip], send_sem=send_sem.at[1], recv_sem=recv_sem.at[1],
            device_id=device(t), device_id_type=MESH,
        ).start()
        return 0

    lax.fori_loop(1, chips, scatter, 0)
    slots_ref[chip] = sum_ref[chip]
    lax.fori_loop(groups // 8, groups // 2, prepare, 0)
    some = slots_ref.at[pl.ds(0, chips - 1)]
    pltpu.make_async_copy(some, some, recv_sem.at[1]).wait()
    own = pl.ds(pl.multiple_of(core * half + chip * piece, piece), piece)
    y_ref[own, :] = jnp.sum(slots_ref[...], axis=0)

    def gather(k, _):
        pltpu.make_async_remote_copy(
            src_ref=y_ref.at[own], dst_ref=y_ref.at[own], send_sem=send_sem.at[2], recv_sem=recv_sem.at[2],
            device_id=device(lax.rem(chip + k, chips)), device_id_type=MESH,
        ).start()
        return 0

    lax.fori_loop(1, chips, gather, 0)
    lax.fori_loop(groups // 2, groups, prepare, 0)
    pltpu.make_async_copy(some, some, recv_sem.at[2]).wait()
    share = pltpu.make_async_remote_copy(
        src_ref=y_ref.at[mine], dst_ref=y_ref.at[mine], send_sem=send_sem.at[3], recv_sem=recv_sem.at[3],
        device_id=partner, device_id_type=MESH,
    )
    share.start()
    swap.wait_send()
    pltpu.make_async_copy(some, some, send_sem.at[1]).wait()
    pltpu.make_async_copy(some, some, send_sem.at[2]).wait()
    share.wait()


def split(x):
    high = x.astype(BF16)
    return high, (x - high.astype(F32)).astype(BF16)


def wide(x):
    return jnp.concatenate(split(x), axis=1)


def project(side, x):
    pair = lax.dot_general(wide(x), side, (((1,), (1,)), ((), ())), preferred_element_type=F32)
    half = pair.shape[1] // 2
    return pair[:, :half] + pair[:, half:]


def spread(solved, g):
    return jnp.dot(wide(g), solved, preferred_element_type=F32)


def stack_solved(v, scale):
    high, low = split(v * scale)
    return jnp.concatenate([high, low, high, low], axis=0)


def sharpen(r, v, t, eye, last):
    t = 2.0 * t * t - 1.0
    back = 1.0 / t
    gain = 1.0 + back
    rh, rl = split(r)
    vh, vl = split(v)
    left = jnp.concatenate([rh, rl], axis=1)
    head = jnp.concatenate([rh, vh], axis=1)
    tail = jnp.concatenate([rl, vl], axis=1)
    right = jnp.concatenate([head, tail, head, tail], axis=0)
    prod = jnp.dot(left, right, preferred_element_type=F32)
    v = gain * (v + prod[:, 2 * OB :])
    r = None if last else gain * prod[:, : 2 * OB] - back * eye
    return r, v, t


def begin(p, rhs, norm, eye):
    c = 1.0 + jnp.maximum(norm, 0.0625)
    top = c + 1.0
    alpha = 2.0 / top
    return ((c - 1.0) / top) * eye - alpha * p, alpha * rhs, top / (c - 1.0)


def assimilate(
    span_x, span_y,
    rows_c, rows_i, y_in, w_ref, x_ref, out_ref,
    rows_x, rows_y, rows_r, y_ref, t_ref, v_ref, cur_ref, side_ref, solved_ref, lanes_ref,
):
    block_x, levels, block_y, members = out_ref.shape
    count = y_in.shape[0]
    batches = count // OB
    scale = 1.0 / (members - 1.0)
    code = rows_c[...]
    rows_x[...] = ((code >> 17) - span_x).astype(F32)
    rows_y[...] = (((code >> 7) & 1023) - span_y).astype(F32)
    reach = (code & 127).astype(F32)
    rows_r[...] = 1.0 / (reach * reach)
    y_ref[...] = y_in[...] * rows_i[...]
    out_ref[...] = x_ref[pl.ds(0, block_x * levels * block_y), :].reshape(out_ref.shape)
    cur_ref[...] = y_ref[pl.ds(0, OB), :]
    side_ref[...] = jnp.zeros_like(side_ref)
    solved_ref[...] = jnp.zeros_like(solved_ref)
    lanes_ref[...] = jnp.zeros_like(lanes_ref)
    lane = lax.broadcasted_iota(jnp.int32, (OB, 2 * OB), 1)
    row = lax.broadcasted_iota(jnp.int32, (OB, 2 * OB), 0)
    eye = jnp.where((lane == row) | (lane == row + OB), 1.0, 0.0).astype(F32)
    ys = lax.broadcasted_iota(jnp.int32, (block_y, 1), 0).astype(F32)

    def rho_rows(at, px, py, ir):
        dx = rows_x[at, :] - px
        dy = rows_y[at, :] - py
        near = jnp.maximum(1.0 - (dx * dx + dy * dy) * ir, 0.0)
        return near * near

    def cells(n, side, solved, px, dy2, ir):
        rhos = []
        for u in range(6):
            dx = jnp.float32(1.0) * (n * 6 + u) - px
            near = jnp.maximum((1.0 - dx * dx * ir) - dy2, 0.0)
            rhos.append((near * near)[None, None])
        rho = jnp.concatenate(rhos, axis=0)
        at = pl.ds(n * 6, 6)
        old = out_ref[at].reshape(6 * levels * block_y, members)
        g = project(side, old).reshape(6, levels, block_y, members) * rho
        new = old + spread(solved, g.reshape(6 * levels * block_y, members))
        out_ref[at] = new.reshape(6, levels, block_y, members)

    def previous():
        px, py, ir = lanes_ref[pl.ds(0, 1), :], lanes_ref[pl.ds(1, 1), :], lanes_ref[pl.ds(2, 1), :]
        dy = ys - py
        return side_ref[...], solved_ref[...], px, py, dy * dy * ir, ir

    def step(first, b, _):
        now = pl.ds(pl.multiple_of(b * OB, OB), OB)
        after = pl.ds(pl.multiple_of(jnp.minimum(b + 1, batches - 1) * OB, OB), OB)
        side0, solved0, px0, py0, dy20, ir0 = previous()

        def later(start, size):
            at = pl.ds(start, size)
            old = y_ref[at, :]
            y_ref[at, :] = old + spread(solved0, project(side0, old) * rho_rows(at, px0, py0, ir0))

        pieces = []
        for start in range((first + 1) * OB, count, 384):
            pieces.append(functools.partial(later, start, min(384, count - start)))
        ahead_of = len(pieces)
        for n in range(block_x // 6):
            pieces.append(functools.partial(cells, n, side0, solved0, px0, dy20, ir0))
        plan = list([0.15, 0.3, 0.45, 0.6, 0.75, 0.9, 1])
        total = len(pieces)
        done = [0]

        def fill():
            share = plan.pop(0)
            upto = total if not plan else min(total, round(share * total))
            while done[0] < upto:
                pieces[done[0]]()
                done[0] += 1

        hx = cur_ref[...]
        centred = hx - jnp.mean(hx, axis=1, keepdims=True)
        high, low = split(centred)
        high2 = jnp.concatenate([high, high], axis=1)
        low2 = jnp.concatenate([low, low], axis=1)
        side = jnp.concatenate([high2, low2, low2, high2], axis=0)
        fill()
        p = project(side, centred) * scale
        fill()
        norm = jnp.max(jnp.sum(jnp.abs(p), axis=0, keepdims=True), axis=1, keepdims=True)
        rhs = w_ref[now, :] - hx
        r, v, t = begin(p, rhs, norm, eye)
        for i in range(4):
            r, v, t = sharpen(r, v, t, eye, i + 1 == 4)
            fill()
            if i == 4 - 2:
                while done[0] < ahead_of:
                    pieces[done[0]]()
                    done[0] += 1
                ahead = y_ref[after, :]
                px = jnp.sum(rows_x[now, :] * eye, axis=0, keepdims=True)
                py = jnp.sum(rows_y[now, :] * eye, axis=0, keepdims=True)
                ir = jnp.sum(rows_r[now, :] * eye, axis=0, keepdims=True)
                g = project(side, ahead) * rho_rows(after, px, py, ir)
        new_solved = stack_solved(v, scale)
        fresh = ahead + spread(new_solved, g)
        fill()
        side_ref[...] = side
        solved_ref[...] = new_solved
        lanes_ref[pl.ds(0, 1), :] = px
        lanes_ref[pl.ds(1, 1), :] = py
        lanes_ref[pl.ds(2, 1), :] = ir
        cur_ref[...] = fresh

        @pl.when(jnp.max(norm) > QUICK)
        def _():
            t_ref[...] = p + eye
            v_ref[...] = rhs

            @pl.when(jnp.max(norm) <= WIDE)
            def _():
                r, v, t = begin(p, rhs, norm, eye)
                for i in range(LONG):
                    r, v, t = sharpen(r, v, t, eye, i + 1 == LONG)
                v_ref[...] = v

            @pl.when(jnp.max(norm) > WIDE)
            def _():
                lax.fori_loop(0, OB, pivot, 0)

            exact = stack_solved(v_ref[...], scale)
            solved_ref[...] = exact
            cur_ref[...] = ahead + spread(exact, g)

        return 0

    def pivot(k, _):
        trow = t_ref[pl.ds(k, 1), :]
        here = lane[:1, :] == k
        inverse = 1.0 / jnp.sum(jnp.where(here, trow, 0.0), axis=1, keepdims=True)
        trow = trow * inverse
        vrow = v_ref[pl.ds(k, 1), :] * inverse
        mat = t_ref[...]
        col = jnp.sum(jnp.where(lane == k, mat, 0.0), axis=1, keepdims=True)
        mine = row == k
        t_ref[...] = jnp.where(mine, trow, mat - col * trow)
        v_ref[...] = jnp.where(mine, vrow, v_ref[...] - col * vrow)
        return 0

    for first in range(0, batches, 4):
        lax.fori_loop(first, min(first + 4, batches), functools.partial(step, first), 0)
    side, solved, px, _, dy2, ir = previous()
    for n in range(block_x // 6):
        cells(n, side, solved, px, dy2, ir)


def run_assimilate(shape, spans, *args):
    vmem = pl.BlockSpec(memory_space=pltpu.VMEM)
    count, members = args[0].shape
    return pl.pallas_call(
        functools.partial(assimilate, *spans),
        out_shape=jax.ShapeDtypeStruct(shape, F32),
        in_specs=[vmem] * len(args),
        out_specs=vmem,
        scratch_shapes=[
            pltpu.VMEM((count, members), F32),
            pltpu.VMEM((count, members), F32),
            pltpu.VMEM((count, members), F32),
            pltpu.VMEM((count, members), F32),
            pltpu.VMEM((OB, 2 * OB), F32),
            pltpu.VMEM((OB, members), F32),
            pltpu.VMEM((OB, members), F32),
            pltpu.VMEM((4 * OB, 2 * members), BF16),
            pltpu.VMEM((4 * OB, members), BF16),
            pltpu.VMEM((8, members), F32),
        ],
        name="assimilate",
    )(*args)


def per_device(
    ensemble,
    cfl_ratio_primary_axis,
    cfl_ratio_secondary_axis,
    spreading_ratio,
    obs_owner,
    obs_local,
    batch_order,
    obs_reach,
    obs_value,
    obs_variance,
    obs_noise,
):
    block_x, block_y, levels, members = ensemble.shape
    span_x, span_y = lax.axis_size("gx"), lax.axis_size("gy")
    span = span_x * span_y
    count = obs_local.shape[0]
    size = block_x * levels * block_y
    strip = levels * block_y
    lines = block_x * levels
    flat = jnp.transpose(ensemble, (0, 2, 1, 3)).reshape(size, members)
    plane = (levels * block_x, block_y)
    coefs = [
        jnp.transpose(c, (2, 0, 1)).reshape(plane)
        for c in (cfl_ratio_primary_axis, cfl_ratio_secondary_axis, spreading_ratio)
    ]
    tile = (count // 128, 128)
    tables = [v.reshape(tile) for v in (obs_owner, obs_local, obs_reach, obs_value, obs_variance)]
    vmem = pl.BlockSpec(memory_space=pltpu.VMEM)
    smem = pl.BlockSpec(memory_space=pltpu.SMEM)
    state, place, code, inv, shift = pl.pallas_call(
        forecast,
        out_shape=[
            jax.ShapeDtypeStruct((size + 8, members), F32),
            jax.ShapeDtypeStruct(tile, jnp.int32),
            jax.ShapeDtypeStruct(tile, jnp.int32),
            jax.ShapeDtypeStruct(tile, F32),
            jax.ShapeDtypeStruct(tile, F32),
        ],
        in_specs=[vmem] * 9,
        out_specs=[vmem] * 5,
        scratch_shapes=[
            pltpu.VMEM((size, members), F32),
            pltpu.VMEM((5, size, members), F32),
            pltpu.VMEM((block_x * block_y, 128), F32),
            pltpu.VMEM((2, 2, lines, members), F32),
            pltpu.VMEM((2, 2, strip, members), F32),
            pltpu.VMEM((2, 2, lines, members), F32),
            pltpu.SemaphoreType.DMA((2, 4)),
            pltpu.SemaphoreType.DMA((2, 4)),
        ],
        compiler_params=pltpu.CompilerParams(collective_id=0, has_side_effects=True),
        name="forecast",
    )(flat, *coefs, *tables)
    pieces = span // 2
    table = jax.ShapeDtypeStruct((count, members), F32)
    seen, wanted, rows_c, rows_i = pl.pallas_call(
        collect,
        out_shape=[table, table, jax.ShapeDtypeStruct((count, members), jnp.int32), table],
        in_specs=[smem] * 5 + [vmem] * 2,
        out_specs=[vmem] * 4,
        scratch_shapes=[
            pltpu.VMEM((count, members), F32),
            pltpu.VMEM((count // 2, members), F32),
            pltpu.VMEM((pieces, count // span, members), F32),
            pltpu.VMEM((pieces, count // span, members), F32),
            pltpu.SemaphoreType.DMA((4,)),
            pltpu.SemaphoreType.DMA((4,)),
        ],
        compiler_params=pltpu.CompilerParams(collective_id=1, has_side_effects=True),
        name="collect",
    )(batch_order, *[v.reshape(count) for v in (place, code, inv, shift)], state, obs_noise)
    shape = (block_x, levels, block_y, members)
    spans = (span_x * block_x, span_y * block_y)
    out = run_assimilate(shape, spans, rows_c, rows_i, seen, wanted, state)
    return jnp.transpose(out, (0, 2, 1, 3))


def solution(mesh):
    return jax.shard_map(
        per_device,
        mesh=mesh,
        in_specs=(
            P("gx", "gy", None, None),
            P("gx", "gy", None),
            P("gx", "gy", None),
            P("gx", "gy", None),
            P(),
            P(),
            P(),
            P(),
            P(),
            P(),
            P(),
        ),
        out_specs=P("gx", "gy", None, None),
        check_vma=False,
    )
```

```python
import functools

import jax
import jax.numpy as jnp
from jax import lax
from jax.experimental import pallas as pl
from jax.experimental.pallas import tpu as pltpu
from jax.sharding import PartitionSpec as P

OB = 64
QUICK = 6.5
WIDE = 63.0
LONG = 6
MESH = pl.DeviceIdType.MESH
F32 = jnp.float32
BF16 = jnp.bfloat16


def floor_div(x, n, top):
    shift = 1
    while any((v * -(-(1 << shift) // n)) >> shift != v // n for v in range(top)):
        shift += 1
    return (x * -(-(1 << shift) // n)) >> shift


def thirds(x):
    high = x.astype(BF16).astype(F32)
    rest = x - high
    mid = rest.astype(BF16).astype(F32)
    return [high, mid, rest - mid]


def exchange(
    x_ref, cx_ref, cy_ref, kd_ref, owner_ref, local_ref, reach_ref, value_ref, variance_ref, order_ref, noise_hbm,
    state_hbm, y_ref, w_hbm, rows_c_hbm, rows_i_hbm,
    field_ref, mid_ref, wide_ref, flip_ref, cols_ref, rows_in, cols_in,
    noise_ref, w_ref, rows_c, rows_i, part_ref, half_ref, sum_ref, slots_ref, ints_ref, floats_ref,
    place_s, code_s, inv_s, shift_s, halo_send, halo_recv, send_sem, recv_sem, copy_sem,
):
    strip, members = rows_in.shape[2:]
    block_y = cx_ref.shape[1]
    levels = strip // block_y
    block_x = cx_ref.shape[0] // levels
    lines = block_x * levels
    size = lines * block_y
    gx, gy = lax.axis_index("gx"), lax.axis_index("gy")
    nx, ny = lax.axis_size("gx"), lax.axis_size("gy")
    west, east = (lax.rem(gx + nx - 1, nx), gy), (lax.rem(gx + 1, nx), gy)
    south, north = (gx, lax.rem(gy + ny - 1, ny)), (gx, lax.rem(gy + 1, ny))
    count = part_ref.shape[0]
    half = count // 2
    my = ny // 2
    chips = nx * my
    piece = half // chips
    core = lax.rem(gy, 2)
    chip = gx * my + gy // 2
    partner = (gx, gy + 1 - 2 * core)

    def others(visit):
        def line(a, start):
            ox = lax.rem(gx + a, nx)
            for b in range(start, my):
                oy = lax.rem(gy // 2 + b, my)
                visit(ox * my + oy, (ox, oy * 2 + core))

        line(0, 1)

        def body(a, _):
            line(a, 0)
            return 0

        lax.fori_loop(1, nx, body, 0)

    barrier = pltpu.get_barrier_semaphore()

    def greet(_, device):
        pl.semaphore_signal(barrier, inc=1, device_id=device, device_id_type=MESH)

    for device in (west, east, south, north, partner):
        greet(None, device)
    others(greet)
    fetch = pltpu.make_async_copy(noise_hbm, noise_ref, copy_sem.at[0])
    fetch.start()
    from_west = jnp.where(gx > 0, 1.0, 0.0).astype(F32)
    from_east = jnp.where(gx < nx - 1, 1.0, 0.0).astype(F32)
    from_south = jnp.where(gy > 0, 1.0, 0.0).astype(F32)
    from_north = jnp.where(gy < ny - 1, 1.0, 0.0).astype(F32)

    def pack(field, turn):
        cols_ref[turn, 0] = field[pl.ds(0, lines, stride=block_y), :]
        cols_ref[turn, 1] = field[pl.ds(block_y - 1, lines, stride=block_y), :]

    def sends(field, turn):
        last = (block_x - 1) * strip
        plan = (
            (field.at[pl.ds(last, strip)], rows_in.at[turn, 0], east),
            (field.at[pl.ds(0, strip)], rows_in.at[turn, 1], west),
            (cols_ref.at[turn, 1], cols_in.at[turn, 0], north),
            (cols_ref.at[turn, 0], cols_in.at[turn, 1], south),
        )
        return [
            pltpu.make_async_remote_copy(
                src_ref=source,
                dst_ref=target,
                send_sem=halo_send.at[turn, i],
                recv_sem=halo_recv.at[turn, i],
                device_id=device,
                device_id_type=MESH,
            )
            for i, (source, target, device) in enumerate(plan)
        ]

    def rows_of(i, l):
        return pl.ds(pl.multiple_of((i * levels + l) * block_y, block_y), block_y)

    def strip_of(field, i):
        return [field[rows_of(i, l), :] for l in range(levels)]

    zero = jnp.zeros((1, members), F32)

    def advance(i, centre, left, right, target):
        for l in range(levels):
            w = [wide_ref[k, rows_of(i, l), :] for k in range(5)]
            c = centre[l]
            new = w[0] * c + w[1] * left[l] + w[2] * right[l]
            new = new + w[3] * jnp.concatenate([zero, c[:-1]], axis=0)
            new = new + w[4] * jnp.concatenate([c[1:], zero], axis=0)
            target[rows_of(i, l), :] = new

    def inside(field, target):
        def inner(i, _):
            advance(i, strip_of(field, i), strip_of(field, i - 1), strip_of(field, i + 1), target)
            return 0

        lax.fori_loop(1, block_x - 1, inner, 0)

    def border(copies, field, target, turn):
        copies[0].wait_recv()
        left = [rows_in[turn, 0, pl.ds(l * block_y, block_y), :] * from_west for l in range(levels)]
        advance(0, strip_of(field, 0), left, strip_of(field, 1), target)
        copies[1].wait_recv()
        right = [rows_in[turn, 1, pl.ds(l * block_y, block_y), :] * from_east for l in range(levels)]
        last = block_x - 1
        advance(last, strip_of(field, last), strip_of(field, last - 1), right, target)
        for side, (at, here) in enumerate(((0, from_south), (block_y - 1, from_north))):
            copies[2 + side].wait_recv()
            rows = pl.ds(at, lines, stride=block_y)
            target[rows, :] = target[rows, :] + wide_ref[3 + side, rows, :] * (cols_in[turn, side] * here)

    pack(x_ref, 0)

    def flip(i, _):
        rows = pl.ds(i, levels, stride=block_x)
        cx, cy, kd = cx_ref[rows, :], cy_ref[rows, :], kd_ref[rows, :]
        w1, w2 = kd + jnp.maximum(cx, 0.0), kd - jnp.minimum(cx, 0.0)
        w3, w4 = kd + jnp.maximum(cy, 0.0), kd - jnp.minimum(cy, 0.0)
        packed = jnp.concatenate([1.0 - (w1 + w2 + w3 + w4), w1, w2, w3, w4], axis=0)
        packed = jnp.concatenate(thirds(packed), axis=0)
        at = pl.ds(pl.multiple_of(i * block_y, block_y), block_y)
        flip_ref[at, pl.ds(0, 15 * levels)] = packed.T
        return 0

    lax.fori_loop(0, block_x, flip, 0, unroll=4)
    kinds = 5 * levels
    r = lax.broadcasted_iota(jnp.int32, (3 * kinds, members), 0)
    pick = [((r == k) | (r == k + kinds) | (r == k + 2 * kinds)).astype(F32).astype(BF16) for k in range(kinds)]
    pair = 2 * block_y

    def widen(n, _):
        left = flip_ref[pl.ds(pl.multiple_of(n * pair, pair), pair), pl.ds(0, 3 * kinds)].astype(BF16)
        for k in range(0, kinds, 2):
            right = jnp.concatenate(pick[k : k + 2], axis=1)
            spread_out = jnp.dot(left, right, preferred_element_type=F32)
            for u in range(2):
                for v in range(2):
                    kind, l = divmod(k + v, levels)
                    piece_out = spread_out[u * block_y : (u + 1) * block_y, v * members : (v + 1) * members]
                    wide_ref[kind, rows_of(n * 2 + u, l), :] = piece_out
        return 0

    lax.fori_loop(0, block_x // 2, widen, 0)
    local, owner = local_ref[...], owner_ref[...]
    ix = floor_div(local, block_y * levels, size)
    rest = local - ix * (block_y * levels)
    iy = floor_div(rest, levels, block_y * levels)
    lev = rest - iy * levels
    ox = floor_div(owner, ny, nx * ny)
    oy = owner - ox * ny
    mine = owner == gx * ny + gy
    ints_ref[0] = jnp.where(mine, (ix * levels + lev) * block_y + iy, size)
    px = (ox - gx) * block_x + ix + nx * block_x
    py = (oy - gy) * block_y + iy + ny * block_y
    ints_ref[1] = (px * 1024 + py) * 128 + reach_ref[...]
    inv = lax.rsqrt(variance_ref[...])
    floats_ref[0] = inv
    floats_ref[1] = value_ref[...] * inv
    field_ref[pl.ds(size, 8), :] = jnp.zeros((8, members), F32)
    tables = [
        pltpu.make_async_copy(source, target, copy_sem.at[1 + i])
        for i, (source, target) in enumerate(
            ((ints_ref.at[0], place_s), (ints_ref.at[1], code_s), (floats_ref.at[0], inv_s), (floats_ref.at[1], shift_s))
        )
    ]
    inside(x_ref, mid_ref)
    pl.semaphore_wait(barrier, chips + 4)
    first = sends(x_ref, 0)
    for copy in first:
        copy.start()
    for table in tables:
        table.start()
    border(first, x_ref, mid_ref, 0)
    pack(mid_ref, 1)
    second = sends(mid_ref, 1)
    for copy in second:
        copy.start()
    inside(mid_ref, field_ref)
    fetch.wait()
    for table in tables:
        table.wait()
    full = (1, members)

    def look(ref, o):
        return ref[o >> 7, o & 127]

    def prepare(g, _):
        for u in range(8):
            k = g * 8 + u
            o = order_ref[k]
            at = pl.ds(k, 1)
            w_ref[at, :] = noise_ref[pl.ds(o, 1), :] + jnp.full(full, look(shift_s, o))
            rows_c[at, :] = jnp.full(full, look(code_s, o))
            rows_i[at, :] = jnp.full(full, look(inv_s, o))
        return 0

    groups = count // 8
    lax.fori_loop(0, groups // 8, prepare, 0)
    border(second, mid_ref, field_ref, 1)
    keep = pltpu.make_async_copy(field_ref, state_hbm, copy_sem.at[0])
    keep.start()

    def pick_rows(base):
        def body(g, _):
            for u in range(8):
                k = base + g * 8 + u
                part_ref[pl.ds(k, 1), :] = field_ref[pl.ds(look(place_s, order_ref[k]), 1), :]
            return 0

        lax.fori_loop(0, half // 8, body, 0)

    mine = pl.ds(pl.multiple_of(core * half, half), half)
    other = pl.ds(pl.multiple_of((1 - core) * half, half), half)
    pick_rows((1 - core) * half)
    swap = pltpu.make_async_remote_copy(
        src_ref=part_ref.at[other], dst_ref=half_ref, send_sem=send_sem.at[0], recv_sem=recv_sem.at[0],
        device_id=partner, device_id_type=MESH,
    )
    swap.start()
    pick_rows(core * half)
    swap.wait_recv()
    sum_ref[...] = (part_ref[mine, :] + half_ref[...]).reshape(sum_ref.shape)

    def scatter(t, device):
        pltpu.make_async_remote_copy(
            src_ref=sum_ref.at[t], dst_ref=slots_ref.at[chip], send_sem=send_sem.at[1], recv_sem=recv_sem.at[1],
            device_id=device, device_id_type=MESH,
        ).start()

    others(scatter)
    slots_ref[chip] = sum_ref[chip]
    lax.fori_loop(groups // 8, groups // 2, prepare, 0)
    some = slots_ref.at[pl.ds(0, chips - 1)]
    pltpu.make_async_copy(some, some, recv_sem.at[1]).wait()
    own = pl.ds(pl.multiple_of(core * half + chip * piece, piece), piece)
    y_ref[own, :] = jnp.sum(slots_ref[...], axis=0)

    def gather(t, device):
        pltpu.make_async_remote_copy(
            src_ref=y_ref.at[own], dst_ref=y_ref.at[own], send_sem=send_sem.at[2], recv_sem=recv_sem.at[2],
            device_id=device, device_id_type=MESH,
        ).start()

    others(gather)
    lax.fori_loop(groups // 2, groups, prepare, 0)
    stores = [
        pltpu.make_async_copy(source, target, copy_sem.at[1 + i])
        for i, (source, target) in enumerate(((w_ref, w_hbm), (rows_c, rows_c_hbm), (rows_i, rows_i_hbm)))
    ]
    for store in stores:
        store.start()
    pltpu.make_async_copy(some, some, recv_sem.at[2]).wait()
    share = pltpu.make_async_remote_copy(
        src_ref=y_ref.at[mine], dst_ref=y_ref.at[mine], send_sem=send_sem.at[3], recv_sem=recv_sem.at[3],
        device_id=partner, device_id_type=MESH,
    )
    share.start()
    for copy in first + second:
        copy.wait_send()
    swap.wait_send()
    keep.wait()
    for store in stores:
        store.wait()
    pltpu.make_async_copy(some, some, send_sem.at[1]).wait()
    pltpu.make_async_copy(some, some, send_sem.at[2]).wait()
    share.wait()


def split(x):
    high = x.astype(BF16)
    return high, (x - high.astype(F32)).astype(BF16)


def wide(x):
    return jnp.concatenate(split(x), axis=1)


def project(side, x):
    pair = lax.dot_general(wide(x), side, (((1,), (1,)), ((), ())), preferred_element_type=F32)
    half = pair.shape[1] // 2
    return pair[:, :half] + pair[:, half:]


def spread(solved, g):
    return jnp.dot(wide(g), solved, preferred_element_type=F32)


def stack_solved(v, scale):
    high, low = split(v * scale)
    return jnp.concatenate([high, low, high, low], axis=0)


def sharpen(r, v, t, eye, last):
    t = 2.0 * t * t - 1.0
    back = 1.0 / t
    gain = 1.0 + back
    rh, rl = split(r)
    vh, vl = split(v)
    left = jnp.concatenate([rh, rl], axis=1)
    head = jnp.concatenate([rh, vh], axis=1)
    tail = jnp.concatenate([rl, vl], axis=1)
    right = jnp.concatenate([head, tail, head, tail], axis=0)
    prod = jnp.dot(left, right, preferred_element_type=F32)
    v = gain * (v + prod[:, 2 * OB :])
    r = None if last else gain * prod[:, : 2 * OB] - back * eye
    return r, v, t


def begin(p, rhs, norm, eye):
    c = 1.0 + jnp.maximum(norm, 0.0625)
    top = c + 1.0
    alpha = 2.0 / top
    return ((c - 1.0) / top) * eye - alpha * p, alpha * rhs, top / (c - 1.0)


def assimilate(
    span_x, span_y,
    rows_c, rows_i, y_in, w_ref, x_ref, out_ref,
    rows_x, rows_y, rows_r, y_ref, t_ref, v_ref, cur_ref, side_ref, solved_ref, lanes_ref,
):
    block_x, levels, block_y, members = out_ref.shape
    count = y_in.shape[0]
    batches = count // OB
    scale = 1.0 / (members - 1.0)
    code = rows_c[...]
    rows_x[...] = ((code >> 17) - span_x).astype(F32)
    rows_y[...] = (((code >> 7) & 1023) - span_y).astype(F32)
    reach = (code & 127).astype(F32)
    rows_r[...] = 1.0 / (reach * reach)
    y_ref[...] = y_in[...] * rows_i[...]
    out_ref[...] = x_ref[pl.ds(0, block_x * levels * block_y), :].reshape(out_ref.shape)
    cur_ref[...] = y_ref[pl.ds(0, OB), :]
    side_ref[...] = jnp.zeros_like(side_ref)
    solved_ref[...] = jnp.zeros_like(solved_ref)
    lanes_ref[...] = jnp.zeros_like(lanes_ref)
    lane = lax.broadcasted_iota(jnp.int32, (OB, 2 * OB), 1)
    row = lax.broadcasted_iota(jnp.int32, (OB, 2 * OB), 0)
    eye = jnp.where((lane == row) | (lane == row + OB), 1.0, 0.0).astype(F32)
    ys = lax.broadcasted_iota(jnp.int32, (block_y, 1), 0).astype(F32)

    def rho_rows(at, px, py, ir):
        dx = rows_x[at, :] - px
        dy = rows_y[at, :] - py
        near = jnp.maximum(1.0 - (dx * dx + dy * dy) * ir, 0.0)
        return near * near

    def cells(n, side, solved, px, dy2, ir):
        rhos = []
        for u in range(6):
            dx = jnp.float32(1.0) * (n * 6 + u) - px
            near = jnp.maximum((1.0 - dx * dx * ir) - dy2, 0.0)
            rhos.append((near * near)[None, None])
        rho = jnp.concatenate(rhos, axis=0)
        at = pl.ds(n * 6, 6)
        old = out_ref[at].reshape(6 * levels * block_y, members)
        g = project(side, old).reshape(6, levels, block_y, members) * rho
        new = old + spread(solved, g.reshape(6 * levels * block_y, members))
        out_ref[at] = new.reshape(6, levels, block_y, members)

    def previous():
        px, py, ir = lanes_ref[pl.ds(0, 1), :], lanes_ref[pl.ds(1, 1), :], lanes_ref[pl.ds(2, 1), :]
        dy = ys - py
        return side_ref[...], solved_ref[...], px, py, dy * dy * ir, ir

    def step(first, b, _):
        now = pl.ds(pl.multiple_of(b * OB, OB), OB)
        after = pl.ds(pl.multiple_of(jnp.minimum(b + 1, batches - 1) * OB, OB), OB)
        side0, solved0, px0, py0, dy20, ir0 = previous()

        def later(start, size):
            at = pl.ds(start, size)
            old = y_ref[at, :]
            y_ref[at, :] = old + spread(solved0, project(side0, old) * rho_rows(at, px0, py0, ir0))

        pieces = []
        for start in range((first + 1) * OB, count, 384):
            pieces.append(functools.partial(later, start, min(384, count - start)))
        ahead_of = len(pieces)
        for n in range(block_x // 6):
            pieces.append(functools.partial(cells, n, side0, solved0, px0, dy20, ir0))
        plan = list([0.15, 0.3, 0.45, 0.6, 0.75, 0.9, 1])
        total = len(pieces)
        done = [0]

        def fill():
            share = plan.pop(0)
            upto = total if not plan else min(total, round(share * total))
            while done[0] < upto:
                pieces[done[0]]()
                done[0] += 1

        hx = cur_ref[...]
        centred = hx - jnp.mean(hx, axis=1, keepdims=True)
        high, low = split(centred)
        high2 = jnp.concatenate([high, high], axis=1)
        low2 = jnp.concatenate([low, low], axis=1)
        side = jnp.concatenate([high2, low2, low2, high2], axis=0)
        fill()
        p = project(side, centred) * scale
        fill()
        norm = jnp.max(jnp.sum(jnp.abs(p), axis=0, keepdims=True), axis=1, keepdims=True)
        rhs = w_ref[now, :] - hx
        r, v, t = begin(p, rhs, norm, eye)
        for i in range(4):
            r, v, t = sharpen(r, v, t, eye, i + 1 == 4)
            fill()
            if i == 4 - 2:
                while done[0] < ahead_of:
                    pieces[done[0]]()
                    done[0] += 1
                ahead = y_ref[after, :]
                px = jnp.sum(rows_x[now, :] * eye, axis=0, keepdims=True)
                py = jnp.sum(rows_y[now, :] * eye, axis=0, keepdims=True)
                ir = jnp.sum(rows_r[now, :] * eye, axis=0, keepdims=True)
                g = project(side, ahead) * rho_rows(after, px, py, ir)
        new_solved = stack_solved(v, scale)
        fresh = ahead + spread(new_solved, g)
        fill()
        side_ref[...] = side
        solved_ref[...] = new_solved
        lanes_ref[pl.ds(0, 1), :] = px
        lanes_ref[pl.ds(1, 1), :] = py
        lanes_ref[pl.ds(2, 1), :] = ir
        cur_ref[...] = fresh

        @pl.when(jnp.max(norm) > QUICK)
        def _():
            t_ref[...] = p + eye
            v_ref[...] = rhs

            @pl.when(jnp.max(norm) <= WIDE)
            def _():
                r, v, t = begin(p, rhs, norm, eye)
                for i in range(LONG):
                    r, v, t = sharpen(r, v, t, eye, i + 1 == LONG)
                v_ref[...] = v

            @pl.when(jnp.max(norm) > WIDE)
            def _():
                lax.fori_loop(0, OB, pivot, 0)

            exact = stack_solved(v_ref[...], scale)
            solved_ref[...] = exact
            cur_ref[...] = ahead + spread(exact, g)

        return 0

    def pivot(k, _):
        trow = t_ref[pl.ds(k, 1), :]
        here = lane[:1, :] == k
        inverse = 1.0 / jnp.sum(jnp.where(here, trow, 0.0), axis=1, keepdims=True)
        trow = trow * inverse
        vrow = v_ref[pl.ds(k, 1), :] * inverse
        mat = t_ref[...]
        col = jnp.sum(jnp.where(lane == k, mat, 0.0), axis=1, keepdims=True)
        mine = row == k
        t_ref[...] = jnp.where(mine, trow, mat - col * trow)
        v_ref[...] = jnp.where(mine, vrow, v_ref[...] - col * vrow)
        return 0

    for first in range(0, batches, 4):
        lax.fori_loop(first, min(first + 4, batches), functools.partial(step, first), 0)
    side, solved, px, _, dy2, ir = previous()
    for n in range(block_x // 6):
        cells(n, side, solved, px, dy2, ir)


def run_assimilate(shape, spans, *args):
    vmem = pl.BlockSpec(memory_space=pltpu.VMEM)
    count, members = args[0].shape
    return pl.pallas_call(
        functools.partial(assimilate, *spans),
        out_shape=jax.ShapeDtypeStruct(shape, F32),
        in_specs=[vmem] * len(args),
        out_specs=vmem,
        scratch_shapes=[
            pltpu.VMEM((count, members), F32),
            pltpu.VMEM((count, members), F32),
            pltpu.VMEM((count, members), F32),
            pltpu.VMEM((count, members), F32),
            pltpu.VMEM((OB, 2 * OB), F32),
            pltpu.VMEM((OB, members), F32),
            pltpu.VMEM((OB, members), F32),
            pltpu.VMEM((4 * OB, 2 * members), BF16),
            pltpu.VMEM((4 * OB, members), BF16),
            pltpu.VMEM((8, members), F32),
        ],
        name="assimilate",
    )(*args)


def per_device(
    ensemble,
    cfl_ratio_primary_axis,
    cfl_ratio_secondary_axis,
    spreading_ratio,
    obs_owner,
    obs_local,
    batch_order,
    obs_reach,
    obs_value,
    obs_variance,
    obs_noise,
):
    block_x, block_y, levels, members = ensemble.shape
    span_x, span_y = lax.axis_size("gx"), lax.axis_size("gy")
    span = span_x * span_y
    count = obs_local.shape[0]
    size = block_x * levels * block_y
    strip = levels * block_y
    lines = block_x * levels
    flat = jnp.transpose(ensemble, (0, 2, 1, 3)).reshape(size, members)
    plane = (levels * block_x, block_y)
    coefs = [
        jnp.transpose(c, (2, 0, 1)).reshape(plane)
        for c in (cfl_ratio_primary_axis, cfl_ratio_secondary_axis, spreading_ratio)
    ]
    tile = (count // 128, 128)
    tables = [v.reshape(tile) for v in (obs_owner, obs_local, obs_reach, obs_value, obs_variance)]
    vmem = pl.BlockSpec(memory_space=pltpu.VMEM)
    smem = pl.BlockSpec(memory_space=pltpu.SMEM)
    hbm = pl.BlockSpec(memory_space=pl.ANY)
    chips = span // 2
    table = jax.ShapeDtypeStruct((count, members), F32)
    codes = jax.ShapeDtypeStruct((count, members), jnp.int32)
    full = pltpu.VMEM((count, members), F32)
    state, seen, wanted, rows_c, rows_i = pl.pallas_call(
        exchange,
        out_shape=[jax.ShapeDtypeStruct((size + 8, members), F32), table, table, codes, table],
        in_specs=[vmem] * 9 + [smem, hbm],
        out_specs=[hbm, vmem, hbm, hbm, hbm],
        scratch_shapes=[
            pltpu.VMEM((size + 8, members), F32),
            pltpu.VMEM((size, members), F32),
            pltpu.VMEM((5, size, members), F32),
            pltpu.VMEM((block_x * block_y, 128), F32),
            pltpu.VMEM((2, 2, lines, members), F32),
            pltpu.VMEM((2, 2, strip, members), F32),
            pltpu.VMEM((2, 2, lines, members), F32),
            full,
            full,
            pltpu.VMEM((count, members), jnp.int32),
            full,
            full,
            pltpu.VMEM((count // 2, members), F32),
            pltpu.VMEM((chips, count // span, members), F32),
            pltpu.VMEM((chips, count // span, members), F32),
            pltpu.VMEM((2, *tile), jnp.int32),
            pltpu.VMEM((2, *tile), F32),
            pltpu.SMEM(tile, jnp.int32),
            pltpu.SMEM(tile, jnp.int32),
            pltpu.SMEM(tile, F32),
            pltpu.SMEM(tile, F32),
            pltpu.SemaphoreType.DMA((2, 4)),
            pltpu.SemaphoreType.DMA((2, 4)),
            pltpu.SemaphoreType.DMA((4,)),
            pltpu.SemaphoreType.DMA((4,)),
            pltpu.SemaphoreType.DMA((5,)),
        ],
        compiler_params=pltpu.CompilerParams(collective_id=0, has_side_effects=True),
        name="exchange",
    )(flat, *coefs, *tables, batch_order, obs_noise)
    shape = (block_x, levels, block_y, members)
    spans = (span_x * block_x, span_y * block_y)
    out = run_assimilate(shape, spans, rows_c, rows_i, seen, wanted, state)
    return jnp.transpose(out, (0, 2, 1, 3))


def solution(mesh):
    return jax.shard_map(
        per_device,
        mesh=mesh,
        in_specs=(
            P("gx", "gy", None, None),
            P("gx", "gy", None),
            P("gx", "gy", None),
            P("gx", "gy", None),
            P(),
            P(),
            P(),
            P(),
            P(),
            P(),
            P(),
        ),
        out_specs=P("gx", "gy", None, None),
        check_vma=False,
    )
```

```python
import functools

import jax
import jax.numpy as jnp
from jax import lax
from jax.experimental import pallas as pl
from jax.experimental.pallas import tpu as pltpu
from jax.sharding import PartitionSpec as P

OB = 64
QUICK = 6.5
WIDE = 63.0
LONG = 6
MESH = pl.DeviceIdType.MESH
F32 = jnp.float32
BF16 = jnp.bfloat16


def floor_div(x, n, top):
    shift = 1
    while any((v * -(-(1 << shift) // n)) >> shift != v // n for v in range(top)):
        shift += 1
    return (x * -(-(1 << shift) // n)) >> shift


def thirds(x):
    high = x.astype(BF16).astype(F32)
    rest = x - high
    mid = rest.astype(BF16).astype(F32)
    return [high, mid, rest - mid]


def exchange(
    x_ref, cx_ref, cy_ref, kd_ref, owner_ref, local_ref, reach_ref, value_ref, variance_ref, order_ref, noise_hbm,
    state_hbm, y_ref, w_hbm, rows_c_hbm, rows_i_hbm,
    field_ref, mid_ref, wide_ref, flip_ref, cols_ref, rows_in, cols_in,
    noise_ref, w_ref, rows_c, rows_i, part_ref, half_ref, sum_ref, slots_ref, ints_ref, floats_ref,
    place_s, code_s, inv_s, shift_s, halo_send, halo_recv, send_sem, recv_sem, copy_sem, table_sem,
):
    strip, members = rows_in.shape[2:]
    block_y = cx_ref.shape[1]
    levels = strip // block_y
    block_x = cx_ref.shape[0] // levels
    lines = block_x * levels
    size = lines * block_y
    gx, gy = lax.axis_index("gx"), lax.axis_index("gy")
    nx, ny = lax.axis_size("gx"), lax.axis_size("gy")
    west, east = (lax.rem(gx + nx - 1, nx), gy), (lax.rem(gx + 1, nx), gy)
    south, north = (gx, lax.rem(gy + ny - 1, ny)), (gx, lax.rem(gy + 1, ny))
    count = part_ref.shape[0]
    half = count // 2
    my = ny // 2
    chips = nx * my
    piece = half // chips
    core = lax.rem(gy, 2)
    chip = gx * my + gy // 2
    partner = (gx, gy + 1 - 2 * core)

    def others(visit):
        def line(a, start):
            ox = lax.rem(gx + a, nx)
            for b in range(start, my):
                oy = lax.rem(gy // 2 + b, my)
                visit(ox * my + oy, (ox, oy * 2 + core))

        line(0, 1)

        def body(a, _):
            line(a, 0)
            return 0

        lax.fori_loop(1, nx, body, 0)

    barrier = pltpu.get_barrier_semaphore()

    def greet(_, device):
        pl.semaphore_signal(barrier, inc=1, device_id=device, device_id_type=MESH)

    for device in (west, east, south, north, partner):
        greet(None, device)
    others(greet)
    fetch = pltpu.make_async_copy(noise_hbm, noise_ref, copy_sem.at[0])
    fetch.start()
    from_west = jnp.where(gx > 0, 1.0, 0.0).astype(F32)
    from_east = jnp.where(gx < nx - 1, 1.0, 0.0).astype(F32)
    from_south = jnp.where(gy > 0, 1.0, 0.0).astype(F32)
    from_north = jnp.where(gy < ny - 1, 1.0, 0.0).astype(F32)

    def pack(field, turn):
        cols_ref[turn, 0] = field[pl.ds(0, lines, stride=block_y), :]
        cols_ref[turn, 1] = field[pl.ds(block_y - 1, lines, stride=block_y), :]

    def sends(field, turn):
        last = (block_x - 1) * strip
        plan = (
            (field.at[pl.ds(last, strip)], rows_in.at[turn, 0], east),
            (field.at[pl.ds(0, strip)], rows_in.at[turn, 1], west),
            (cols_ref.at[turn, 1], cols_in.at[turn, 0], north),
            (cols_ref.at[turn, 0], cols_in.at[turn, 1], south),
        )
        return [
            pltpu.make_async_remote_copy(
                src_ref=source,
                dst_ref=target,
                send_sem=halo_send.at[turn, i],
                recv_sem=halo_recv.at[turn, i],
                device_id=device,
                device_id_type=MESH,
            )
            for i, (source, target, device) in enumerate(plan)
        ]

    def rows_of(i, l):
        return pl.ds(pl.multiple_of((i * levels + l) * block_y, block_y), block_y)

    def strip_of(field, i):
        return [field[rows_of(i, l), :] for l in range(levels)]

    zero = jnp.zeros((1, members), F32)

    def advance(i, centre, left, right, target):
        for l in range(levels):
            w = [wide_ref[k, rows_of(i, l), :] for k in range(5)]
            c = centre[l]
            new = w[0] * c + w[1] * left[l] + w[2] * right[l]
            new = new + w[3] * jnp.concatenate([zero, c[:-1]], axis=0)
            new = new + w[4] * jnp.concatenate([c[1:], zero], axis=0)
            target[rows_of(i, l), :] = new

    def inside(field, target):
        def inner(i, _):
            advance(i, strip_of(field, i), strip_of(field, i - 1), strip_of(field, i + 1), target)
            return 0

        lax.fori_loop(1, block_x - 1, inner, 0)

    def border(copies, field, target, turn):
        copies[0].wait_recv()
        left = [rows_in[turn, 0, pl.ds(l * block_y, block_y), :] * from_west for l in range(levels)]
        advance(0, strip_of(field, 0), left, strip_of(field, 1), target)
        copies[1].wait_recv()
        right = [rows_in[turn, 1, pl.ds(l * block_y, block_y), :] * from_east for l in range(levels)]
        last = block_x - 1
        advance(last, strip_of(field, last), strip_of(field, last - 1), right, target)
        for side, (at, here) in enumerate(((0, from_south), (block_y - 1, from_north))):
            copies[2 + side].wait_recv()
            rows = pl.ds(at, lines, stride=block_y)
            target[rows, :] = target[rows, :] + wide_ref[3 + side, rows, :] * (cols_in[turn, side] * here)

    pack(x_ref, 0)
    pl.semaphore_wait(barrier, chips + 4)
    first = sends(x_ref, 0)
    for copy in first:
        copy.start()

    def flip(i, _):
        rows = pl.ds(i, levels, stride=block_x)
        cx, cy, kd = cx_ref[rows, :], cy_ref[rows, :], kd_ref[rows, :]
        w1, w2 = kd + jnp.maximum(cx, 0.0), kd - jnp.minimum(cx, 0.0)
        w3, w4 = kd + jnp.maximum(cy, 0.0), kd - jnp.minimum(cy, 0.0)
        packed = jnp.concatenate([1.0 - (w1 + w2 + w3 + w4), w1, w2, w3, w4], axis=0)
        packed = jnp.concatenate(thirds(packed), axis=0)
        at = pl.ds(pl.multiple_of(i * block_y, block_y), block_y)
        flip_ref[at, pl.ds(0, 15 * levels)] = packed.T
        return 0

    lax.fori_loop(0, block_x, flip, 0, unroll=4)
    kinds = 5 * levels
    r = lax.broadcasted_iota(jnp.int32, (3 * kinds, members), 0)
    pick = [((r == k) | (r == k + kinds) | (r == k + 2 * kinds)).astype(F32).astype(BF16) for k in range(kinds)]
    pair = 2 * block_y

    def widen(n, _):
        left = flip_ref[pl.ds(pl.multiple_of(n * pair, pair), pair), pl.ds(0, 3 * kinds)].astype(BF16)
        for k in range(0, kinds, 2):
            right = jnp.concatenate(pick[k : k + 2], axis=1)
            spread_out = jnp.dot(left, right, preferred_element_type=F32)
            for u in range(2):
                for v in range(2):
                    kind, l = divmod(k + v, levels)
                    piece_out = spread_out[u * block_y : (u + 1) * block_y, v * members : (v + 1) * members]
                    wide_ref[kind, rows_of(n * 2 + u, l), :] = piece_out
        return 0

    lax.fori_loop(0, block_x // 2, widen, 0)
    local, owner = local_ref[...], owner_ref[...]
    ix = floor_div(local, block_y * levels, size)
    rest = local - ix * (block_y * levels)
    iy = floor_div(rest, levels, block_y * levels)
    lev = rest - iy * levels
    ox = floor_div(owner, ny, nx * ny)
    oy = owner - ox * ny
    mine = owner == gx * ny + gy
    ints_ref[0] = jnp.where(mine, (ix * levels + lev) * block_y + iy, size)
    px = (ox - gx) * block_x + ix + nx * block_x
    py = (oy - gy) * block_y + iy + ny * block_y
    ints_ref[1] = (px * 1024 + py) * 128 + reach_ref[...]
    inv = lax.rsqrt(variance_ref[...])
    floats_ref[0] = inv
    floats_ref[1] = value_ref[...] * inv
    field_ref[pl.ds(size, 8), :] = jnp.zeros((8, members), F32)
    width = ints_ref.shape[2]
    tables = [
        pltpu.make_async_copy(source.at[r], target.at[pl.ds(r * width, width)], table_sem.at[i, r])
        for i, (source, target) in enumerate(
            ((ints_ref.at[0], place_s), (ints_ref.at[1], code_s), (floats_ref.at[0], inv_s), (floats_ref.at[1], shift_s))
        )
        for r in range(count // width)
    ]
    for table in tables:
        table.start()
    inside(x_ref, mid_ref)
    border(first, x_ref, mid_ref, 0)
    pack(mid_ref, 1)
    second = sends(mid_ref, 1)
    for copy in second:
        copy.start()
    inside(mid_ref, field_ref)
    fetch.wait()
    for table in tables:
        table.wait()
    full = (1, members)

    def look(ref, o):
        return ref[o]

    def prepare(g, _):
        for u in range(8):
            k = g * 8 + u
            o = order_ref[k]
            at = pl.ds(k, 1)
            w_ref[at, :] = noise_ref[pl.ds(o, 1), :] + jnp.full(full, look(shift_s, o))
            rows_c[at, :] = jnp.full(full, look(code_s, o))
            rows_i[at, :] = jnp.full(full, look(inv_s, o))
        return 0

    groups = count // 8
    lax.fori_loop(0, groups // 8, prepare, 0)
    border(second, mid_ref, field_ref, 1)
    keep = pltpu.make_async_copy(field_ref, state_hbm, copy_sem.at[0])
    keep.start()

    def pick_rows(base):
        def body(g, _):
            for u in range(8):
                k = base + g * 8 + u
                part_ref[pl.ds(k, 1), :] = field_ref[pl.ds(look(place_s, order_ref[k]), 1), :]
            return 0

        lax.fori_loop(0, half // 8, body, 0)

    mine = pl.ds(pl.multiple_of(core * half, half), half)
    other = pl.ds(pl.multiple_of((1 - core) * half, half), half)
    pick_rows((1 - core) * half)
    swap = pltpu.make_async_remote_copy(
        src_ref=part_ref.at[other], dst_ref=half_ref, send_sem=send_sem.at[0], recv_sem=recv_sem.at[0],
        device_id=partner, device_id_type=MESH,
    )
    swap.start()
    pick_rows(core * half)
    swap.wait_recv()
    sum_ref[...] = (part_ref[mine, :] + half_ref[...]).reshape(sum_ref.shape)

    def scatter(t, device):
        pltpu.make_async_remote_copy(
            src_ref=sum_ref.at[t], dst_ref=slots_ref.at[chip], send_sem=send_sem.at[1], recv_sem=recv_sem.at[1],
            device_id=device, device_id_type=MESH,
        ).start()

    others(scatter)
    slots_ref[chip] = sum_ref[chip]
    lax.fori_loop(groups // 8, groups // 2, prepare, 0)
    some = slots_ref.at[pl.ds(0, chips - 1)]
    pltpu.make_async_copy(some, some, recv_sem.at[1]).wait()
    own = pl.ds(pl.multiple_of(core * half + chip * piece, piece), piece)
    y_ref[own, :] = jnp.sum(slots_ref[...], axis=0)

    def gather(t, device):
        pltpu.make_async_remote_copy(
            src_ref=y_ref.at[own], dst_ref=y_ref.at[own], send_sem=send_sem.at[2], recv_sem=recv_sem.at[2],
            device_id=device, device_id_type=MESH,
        ).start()

    others(gather)
    lax.fori_loop(groups // 2, groups, prepare, 0)
    stores = [
        pltpu.make_async_copy(source, target, copy_sem.at[1 + i])
        for i, (source, target) in enumerate(((w_ref, w_hbm), (rows_c, rows_c_hbm), (rows_i, rows_i_hbm)))
    ]
    for store in stores:
        store.start()
    pltpu.make_async_copy(some, some, recv_sem.at[2]).wait()
    share = pltpu.make_async_remote_copy(
        src_ref=y_ref.at[mine], dst_ref=y_ref.at[mine], send_sem=send_sem.at[3], recv_sem=recv_sem.at[3],
        device_id=partner, device_id_type=MESH,
    )
    share.start()
    for copy in first + second:
        copy.wait_send()
    swap.wait_send()
    keep.wait()
    for store in stores:
        store.wait()
    pltpu.make_async_copy(some, some, send_sem.at[1]).wait()
    pltpu.make_async_copy(some, some, send_sem.at[2]).wait()
    share.wait()


def split(x):
    high = x.astype(BF16)
    return high, (x - high.astype(F32)).astype(BF16)


def wide(x):
    return jnp.concatenate(split(x), axis=1)


def project(side, x):
    pair = lax.dot_general(wide(x), side, (((1,), (1,)), ((), ())), preferred_element_type=F32)
    half = pair.shape[1] // 2
    return pair[:, :half] + pair[:, half:]


def spread(solved, g):
    return jnp.dot(wide(g), solved, preferred_element_type=F32)


def stack_solved(v, scale):
    high, low = split(v * scale)
    return jnp.concatenate([high, low, high, low], axis=0)


def sharpen(r, v, t, eye, last):
    t = 2.0 * t * t - 1.0
    back = 1.0 / t
    gain = 1.0 + back
    rh, rl = split(r)
    vh, vl = split(v)
    left = jnp.concatenate([rh, rl], axis=1)
    head = jnp.concatenate([rh, vh], axis=1)
    tail = jnp.concatenate([rl, vl], axis=1)
    right = jnp.concatenate([head, tail, head, tail], axis=0)
    prod = jnp.dot(left, right, preferred_element_type=F32)
    v = gain * (v + prod[:, 2 * OB :])
    r = None if last else gain * prod[:, : 2 * OB] - back * eye
    return r, v, t


def begin(p, rhs, norm, eye):
    c = 1.0 + jnp.maximum(norm, 0.0625)
    top = c + 1.0
    alpha = 2.0 / top
    return ((c - 1.0) / top) * eye - alpha * p, alpha * rhs, top / (c - 1.0)


def hinted(x):
    return x if isinstance(x, int) else pl.multiple_of(x, OB)


def assimilate(
    span_x, span_y,
    shape,
    rows_c, rows_i, y_in, w_ref, x_hbm, out_hbm,
    rows_x, rows_y, rows_r, y_ref, t_ref, v_ref, cur_ref, side_ref, solved_ref, lanes_ref,
    first_ref, pair_ref, mix_ref, back_ref, both_ref, out_ref, copy_sem,
):
    block_x, levels, block_y, members = shape
    size = block_x * levels * block_y
    load = pltpu.make_async_copy(x_hbm.at[pl.ds(0, size)], out_ref, copy_sem.at[0])
    load.start()
    count = y_in.shape[0]
    batches = count // OB
    scale = 1.0 / (members - 1.0)
    code = rows_c[...]
    rows_x[...] = ((code >> 17) - span_x).astype(F32)
    rows_y[...] = (((code >> 7) & 1023) - span_y).astype(F32)
    reach = (code & 127).astype(F32)
    rows_r[...] = 1.0 / (reach * reach)
    y_ref[...] = y_in[...] * rows_i[...]
    cur_ref[...] = y_ref[pl.ds(0, OB), :]
    lane = lax.broadcasted_iota(jnp.int32, (OB, 2 * OB), 1)
    row = lax.broadcasted_iota(jnp.int32, (OB, 2 * OB), 0)
    upper = lane >= OB
    eye = jnp.where((lane == row) | (lane == row + OB), 1.0, 0.0).astype(F32)
    ys = lax.broadcasted_iota(jnp.int32, (block_y, 1), 0).astype(F32)
    none = jnp.zeros((OB, 2 * members), BF16)

    def rho_rows(at, px, py, ir):
        dx = rows_x[at, :] - px
        dy = rows_y[at, :] - py
        near = jnp.maximum(1.0 - (dx * dx + dy * dy) * ir, 0.0)
        return near * near

    def fold(x):
        return x[:, :members] + x[:, members:]

    def cells(n):
        px, py, ir = both_ref[pl.ds(0, 1), :], both_ref[pl.ds(1, 1), :], both_ref[pl.ds(2, 1), :]
        dy = ys - py
        dy2 = dy * dy * ir
        rhos = []
        for u in range(6):
            dx = jnp.float32(n * 6 + u) - px
            near = jnp.maximum((1.0 - dx * dx * ir) - dy2, 0.0)
            rhos.append((near * near)[None, None])
        rho = jnp.concatenate(rhos, axis=0)
        rows = 6 * levels * block_y
        at = pl.ds(n * rows, rows)
        flat = (rows, members)
        tall = (6, levels, block_y, members)
        old = out_ref[at, :]
        raw = project(pair_ref[...], old)
        g = (raw.reshape(tall) * rho).reshape(flat)
        raw = raw + fold(jnp.dot(wide(g), mix_ref[...], preferred_element_type=F32))
        g = (raw.reshape(tall) * rho).reshape(flat)
        new = old + fold(jnp.dot(wide(g), back_ref[...], preferred_element_type=F32))
        out_ref[at, :] = new
        return at

    def step(first, blocks, odd, b):
        fresh = b is None
        b = 0 if fresh else b
        now = pl.ds(hinted(b * OB), OB)
        after = pl.ds(hinted(jnp.minimum(b + 1, batches - 1) * OB), OB)
        pieces = []
        if not fresh:
            side0, solved0 = side_ref[...], solved_ref[...]
            px0, py0, ir0 = lanes_ref[pl.ds(0, 1), :], lanes_ref[pl.ds(1, 1), :], lanes_ref[pl.ds(2, 1), :]

            def later(start, size):
                at = pl.ds(start, size)
                old = y_ref[at, :]
                y_ref[at, :] = old + spread(solved0, project(side0, old) * rho_rows(at, px0, py0, ir0))

            for start in range((first + 1) * OB, count, 1024):
                pieces.append(functools.partial(later, start, min(1024, count - start)))
        ahead_of = len(pieces)
        for n in blocks:
            pieces.append(functools.partial(cells, n))
        plan = list([0.3, 0.6, 0.8, 1, 1, 1, 1] if odd else [0.3, 0.6, 0.8, 1, 1, 1, 1])
        total = len(pieces)
        done = [0]

        def fill():
            share = plan.pop(0)
            upto = total if not plan else min(total, round(share * total))
            while done[0] < upto:
                pieces[done[0]]()
                done[0] += 1

        hx = cur_ref[...]
        centred = hx - jnp.mean(hx, axis=1, keepdims=True)
        high, low = split(centred)
        high2 = jnp.concatenate([high, high], axis=1)
        low2 = jnp.concatenate([low, low], axis=1)
        side = jnp.concatenate([high2, low2, low2, high2], axis=0)
        fill()
        p = project(side, centred) * scale
        fill()
        norm = jnp.max(jnp.sum(jnp.abs(p), axis=0, keepdims=True), axis=1, keepdims=True)
        rhs = w_ref[now, :] - hx
        r, v, t = begin(p, rhs, norm, eye)
        for i in range(4):
            r, v, t = sharpen(r, v, t, eye, i + 1 == 4)
            fill()
            if i == 2:
                while done[0] < ahead_of:
                    pieces[done[0]]()
                    done[0] += 1
                ahead = y_ref[after, :]
                px = jnp.sum(rows_x[now, :] * eye, axis=0, keepdims=True)
                py = jnp.sum(rows_y[now, :] * eye, axis=0, keepdims=True)
                ir = jnp.sum(rows_r[now, :] * eye, axis=0, keepdims=True)
                g = project(side, ahead) * rho_rows(after, px, py, ir)
                if odd:
                    mix = project(side, first_ref[...])

        def settle(v):
            solved = stack_solved(v, scale)
            cur_ref[...] = ahead + spread(solved, g)
            solved_ref[...] = solved
            if odd:
                bh = jnp.concatenate([solved0[:OB], solved[:OB]], axis=0)
                bl = jnp.concatenate([solved0[OB : 2 * OB], solved[OB : 2 * OB]], axis=0)
                half = jnp.concatenate([bh, bl], axis=1)
                back_ref[...] = jnp.concatenate([half, half], axis=0)
            else:
                first_ref[...] = v * scale

        fill()
        settle(v)
        side_ref[...] = side
        lanes_ref[pl.ds(0, 1), :] = px
        lanes_ref[pl.ds(1, 1), :] = py
        lanes_ref[pl.ds(2, 1), :] = ir
        if odd:
            pair_ref[...] = jnp.concatenate([side0[:OB], high2, side0[OB : 2 * OB], low2], axis=0)
            mh, ml = split(jnp.where(upper, mix, 0.0))
            mrow = jnp.concatenate([mh, ml], axis=1)
            mix_ref[...] = jnp.concatenate([mrow, none, mrow, none], axis=0)
            low_half = ~upper[:1, :]
            both_ref[pl.ds(0, 1), :] = jnp.where(low_half, px0, px)
            both_ref[pl.ds(1, 1), :] = jnp.where(low_half, py0, py)
            both_ref[pl.ds(2, 1), :] = jnp.where(low_half, ir0, ir)

        @pl.when(jnp.max(norm) > QUICK)
        def _():
            t_ref[...] = p + eye
            v_ref[...] = rhs

            @pl.when(jnp.max(norm) <= WIDE)
            def _():
                r, v, t = begin(p, rhs, norm, eye)
                for i in range(LONG):
                    r, v, t = sharpen(r, v, t, eye, i + 1 == LONG)
                v_ref[...] = v

            @pl.when(jnp.max(norm) > WIDE)
            def _():
                lax.fori_loop(0, OB, pivot, 0)

            settle(v_ref[...])

    def pivot(k, _):
        trow = t_ref[pl.ds(k, 1), :]
        here = lane[:1, :] == k
        inverse = 1.0 / jnp.sum(jnp.where(here, trow, 0.0), axis=1, keepdims=True)
        trow = trow * inverse
        vrow = v_ref[pl.ds(k, 1), :] * inverse
        mat = t_ref[...]
        col = jnp.sum(jnp.where(lane == k, mat, 0.0), axis=1, keepdims=True)
        mine = row == k
        t_ref[...] = jnp.where(mine, trow, mat - col * trow)
        v_ref[...] = jnp.where(mine, vrow, v_ref[...] - col * vrow)
        return 0

    groups = block_x // 6
    early, late = range(groups // 2), range(groups // 2, groups)
    step(0, (), False, None)
    step(0, (), True, 1)

    def two(first, q, _):
        step(first, early, False, 2 * q)
        step(first, late, True, 2 * q + 1)
        return 0

    load.wait()
    two(0, 1, 0)
    for first in range(4, batches, 4):
        lax.fori_loop(first // 2, min(first + 4, batches) // 2, functools.partial(two, first), 0)
    stores = []
    for n in range(groups):
        at = cells(n)
        stores.append(pltpu.make_async_copy(out_ref.at[at], out_hbm.at[at], copy_sem.at[1 + n]))
        stores[-1].start()
    for store in stores:
        store.wait()


def run_assimilate(shape, spans, *args):
    vmem = pl.BlockSpec(memory_space=pltpu.VMEM)
    hbm = pl.BlockSpec(memory_space=pl.ANY)
    count, members = args[0].shape
    size = shape[0] * shape[1] * shape[2]
    out = pl.pallas_call(
        functools.partial(assimilate, *spans, shape),
        out_shape=jax.ShapeDtypeStruct((size, members), F32),
        in_specs=[vmem] * (len(args) - 1) + [hbm],
        out_specs=hbm,
        scratch_shapes=[
            pltpu.VMEM((count, members), F32),
            pltpu.VMEM((count, members), F32),
            pltpu.VMEM((count, members), F32),
            pltpu.VMEM((count, members), F32),
            pltpu.VMEM((OB, 2 * OB), F32),
            pltpu.VMEM((OB, members), F32),
            pltpu.VMEM((OB, members), F32),
            pltpu.VMEM((4 * OB, 2 * members), BF16),
            pltpu.VMEM((4 * OB, members), BF16),
            pltpu.VMEM((8, members), F32),
            pltpu.VMEM((OB, members), F32),
            pltpu.VMEM((4 * OB, 2 * members), BF16),
            pltpu.VMEM((4 * OB, 2 * members), BF16),
            pltpu.VMEM((4 * OB, 2 * members), BF16),
            pltpu.VMEM((8, members), F32),
            pltpu.VMEM((size, members), F32),
            pltpu.SemaphoreType.DMA((1 + shape[0] // 6,)),
        ],
        name="assimilate",
    )(*args)
    return out.reshape(shape)


def per_device(
    ensemble,
    cfl_ratio_primary_axis,
    cfl_ratio_secondary_axis,
    spreading_ratio,
    obs_owner,
    obs_local,
    batch_order,
    obs_reach,
    obs_value,
    obs_variance,
    obs_noise,
):
    block_x, block_y, levels, members = ensemble.shape
    span_x, span_y = lax.axis_size("gx"), lax.axis_size("gy")
    span = span_x * span_y
    count = obs_local.shape[0]
    size = block_x * levels * block_y
    strip = levels * block_y
    lines = block_x * levels
    flat = jnp.transpose(ensemble, (0, 2, 1, 3)).reshape(size, members)
    plane = (levels * block_x, block_y)
    coefs = [
        jnp.transpose(c, (2, 0, 1)).reshape(plane)
        for c in (cfl_ratio_primary_axis, cfl_ratio_secondary_axis, spreading_ratio)
    ]
    tile = (count // 128, 128)
    tables = [v.reshape(tile) for v in (obs_owner, obs_local, obs_reach, obs_value, obs_variance)]
    vmem = pl.BlockSpec(memory_space=pltpu.VMEM)
    smem = pl.BlockSpec(memory_space=pltpu.SMEM)
    hbm = pl.BlockSpec(memory_space=pl.ANY)
    chips = span // 2
    table = jax.ShapeDtypeStruct((count, members), F32)
    codes = jax.ShapeDtypeStruct((count, members), jnp.int32)
    full = pltpu.VMEM((count, members), F32)
    state, seen, wanted, rows_c, rows_i = pl.pallas_call(
        exchange,
        out_shape=[jax.ShapeDtypeStruct((size + 8, members), F32), table, table, codes, table],
        in_specs=[vmem] * 9 + [smem, hbm],
        out_specs=[hbm, vmem, hbm, hbm, hbm],
        scratch_shapes=[
            pltpu.VMEM((size + 8, members), F32),
            pltpu.VMEM((size, members), F32),
            pltpu.VMEM((5, size, members), F32),
            pltpu.VMEM((block_x * block_y, 128), F32),
            pltpu.VMEM((2, 2, lines, members), F32),
            pltpu.VMEM((2, 2, strip, members), F32),
            pltpu.VMEM((2, 2, lines, members), F32),
            full,
            full,
            pltpu.VMEM((count, members), jnp.int32),
            full,
            full,
            pltpu.VMEM((count // 2, members), F32),
            pltpu.VMEM((chips, count // span, members), F32),
            pltpu.VMEM((chips, count // span, members), F32),
            pltpu.VMEM((2, *tile), jnp.int32),
            pltpu.VMEM((2, *tile), F32),
            pltpu.SMEM((count,), jnp.int32),
            pltpu.SMEM((count,), jnp.int32),
            pltpu.SMEM((count,), F32),
            pltpu.SMEM((count,), F32),
            pltpu.SemaphoreType.DMA((2, 4)),
            pltpu.SemaphoreType.DMA((2, 4)),
            pltpu.SemaphoreType.DMA((4,)),
            pltpu.SemaphoreType.DMA((4,)),
            pltpu.SemaphoreType.DMA((5,)),
            pltpu.SemaphoreType.DMA((4, count // 128)),
        ],
        compiler_params=pltpu.CompilerParams(collective_id=0, has_side_effects=True),
        name="exchange",
    )(flat, *coefs, *tables, batch_order, obs_noise)
    shape = (block_x, levels, block_y, members)
    spans = (span_x * block_x, span_y * block_y)
    out = run_assimilate(shape, spans, rows_c, rows_i, seen, wanted, state)
    return jnp.transpose(out, (0, 2, 1, 3))


def solution(mesh):
    return jax.shard_map(
        per_device,
        mesh=mesh,
        in_specs=(
            P("gx", "gy", None, None),
            P("gx", "gy", None),
            P("gx", "gy", None),
            P("gx", "gy", None),
            P(),
            P(),
            P(),
            P(),
            P(),
            P(),
            P(),
        ),
        out_specs=P("gx", "gy", None, None),
        check_vma=False,
    )
```

```python
import functools

import jax
import jax.numpy as jnp
from jax import lax
from jax.experimental import pallas as pl
from jax.experimental.pallas import tpu as pltpu
from jax.sharding import PartitionSpec as P

OB = 64
QUICK = 6.5
WIDE = 63.0
LONG = 6
MESH = pl.DeviceIdType.MESH
F32 = jnp.float32
BF16 = jnp.bfloat16


def floor_div(x, n, top):
    shift = 1
    while any((v * -(-(1 << shift) // n)) >> shift != v // n for v in range(top)):
        shift += 1
    return (x * -(-(1 << shift) // n)) >> shift


def thirds(x):
    high = x.astype(BF16).astype(F32)
    rest = x - high
    mid = rest.astype(BF16).astype(F32)
    return [high, mid, rest - mid]


def exchange(
    x_ref, cx_ref, cy_ref, kd_ref, owner_ref, local_ref, reach_ref, value_ref, variance_ref, order_ref, noise_hbm,
    state_hbm, y_ref, w_hbm, rows_c_hbm, rows_i_hbm,
    field_ref, mid_ref, wide_ref, flip_ref, cols_ref, rows_in, cols_in,
    noise_ref, w_ref, rows_c, rows_i, part_ref, half_ref, sum_ref, slots_ref, code_ref, inv_ref, place_ref,
    place_s, spot_s, halo_send, halo_recv, send_sem, recv_sem, copy_sem, table_sem, line_recv, share_send, share_recv, step_sem,
):
    strip, members = rows_in.shape[2:]
    block_y = cx_ref.shape[1]
    levels = strip // block_y
    block_x = cx_ref.shape[0] // levels
    lines = block_x * levels
    size = lines * block_y
    gx, gy = lax.axis_index("gx"), lax.axis_index("gy")
    nx, ny = lax.axis_size("gx"), lax.axis_size("gy")
    west, east = (lax.rem(gx + nx - 1, nx), gy), (lax.rem(gx + 1, nx), gy)
    south, north = (gx, lax.rem(gy + ny - 1, ny)), (gx, lax.rem(gy + 1, ny))
    count = part_ref.shape[0]
    half = count // 2
    my = ny // 2
    chips = nx * my
    piece = half // chips
    core = lax.rem(gy, 2)
    chip = gx * my + gy // 2
    partner = (gx, gy + 1 - 2 * core)

    def others(visit):
        def line(a, start):
            ox = lax.rem(gx + a, nx)
            for b in range(start, my):
                oy = lax.rem(gy // 2 + b, my)
                visit(a, ox * my + oy, (ox, oy * 2 + core))

        line(0, 1)

        def body(a, _):
            line(a, 0)
            return 0

        lax.fori_loop(1, nx, body, 0)

    barrier = pltpu.get_barrier_semaphore()

    side_x = lax.rem(gx, 2)
    rings = nx // 2
    columns = my // 2
    at_z, at_x, at_y = gx // 2, gy // my, lax.rem(gy, my) // 2

    def near_by(dz, flip_high, flip_low, dy):
        high = 1 - side_x if flip_high else side_x
        low = 1 - at_x if flip_low else at_x
        z = lax.rem(at_z + dz + rings, rings)
        y = lax.rem(at_y + dy + columns, columns)
        return (z * 2 + high, low * my + y * 2 + core)

    up, down = near_by(1, 0, 0, 0), near_by(-1, 0, 0, 0)
    ahead_y, behind_y = near_by(0, 0, 0, 1), near_by(0, 0, 0, -1)
    across, beside = near_by(0, 1, 0, 0), near_by(0, 0, 1, 0)
    greeted = (west, east, south, north, partner, up, down, ahead_y, behind_y, across, beside)
    for device in greeted:
        pl.semaphore_signal(barrier, inc=1, device_id=device, device_id_type=MESH)

    def tell(step, devices):
        for device in devices:
            pl.semaphore_signal(step_sem.at[step], inc=1, device_id=device, device_id_type=MESH)

    def hear(step, signals):
        pl.semaphore_wait(step_sem.at[step], signals)

    fetch = pltpu.make_async_copy(noise_hbm, noise_ref, copy_sem.at[0])
    fetch.start()
    from_west = jnp.where(gx > 0, 1.0, 0.0).astype(F32)
    from_east = jnp.where(gx < nx - 1, 1.0, 0.0).astype(F32)
    from_south = jnp.where(gy > 0, 1.0, 0.0).astype(F32)
    from_north = jnp.where(gy < ny - 1, 1.0, 0.0).astype(F32)

    def pack(field, turn):
        cols_ref[turn, 0] = field[pl.ds(0, lines, stride=block_y), :]
        cols_ref[turn, 1] = field[pl.ds(block_y - 1, lines, stride=block_y), :]

    def sends(field, turn):
        last = (block_x - 1) * strip
        plan = (
            (field.at[pl.ds(last, strip)], rows_in.at[turn, 0], east),
            (field.at[pl.ds(0, strip)], rows_in.at[turn, 1], west),
            (cols_ref.at[turn, 1], cols_in.at[turn, 0], north),
            (cols_ref.at[turn, 0], cols_in.at[turn, 1], south),
        )
        return [
            pltpu.make_async_remote_copy(
                src_ref=source,
                dst_ref=target,
                send_sem=halo_send.at[turn, i],
                recv_sem=halo_recv.at[turn, i],
                device_id=device,
                device_id_type=MESH,
            )
            for i, (source, target, device) in enumerate(plan)
        ]

    def rows_of(i, l):
        return pl.ds(pl.multiple_of((i * levels + l) * block_y, block_y), block_y)

    def strip_of(field, i):
        return [field[rows_of(i, l), :] for l in range(levels)]

    zero = jnp.zeros((1, members), F32)

    def advance(i, centre, left, right, target):
        for l in range(levels):
            w = [wide_ref[k, rows_of(i, l), :] for k in range(5)]
            c = centre[l]
            new = w[0] * c + w[1] * left[l] + w[2] * right[l]
            new = new + w[3] * jnp.concatenate([zero, c[:-1]], axis=0)
            new = new + w[4] * jnp.concatenate([c[1:], zero], axis=0)
            target[rows_of(i, l), :] = new

    def inside(field, target):
        def inner(i, _):
            advance(i, strip_of(field, i), strip_of(field, i - 1), strip_of(field, i + 1), target)
            return 0

        lax.fori_loop(1, block_x - 1, inner, 0)

    def border(copies, field, target, turn):
        copies[0].wait_recv()
        left = [rows_in[turn, 0, pl.ds(l * block_y, block_y), :] * from_west for l in range(levels)]
        advance(0, strip_of(field, 0), left, strip_of(field, 1), target)
        copies[1].wait_recv()
        right = [rows_in[turn, 1, pl.ds(l * block_y, block_y), :] * from_east for l in range(levels)]
        last = block_x - 1
        advance(last, strip_of(field, last), strip_of(field, last - 1), right, target)
        for side, (at, here) in enumerate(((0, from_south), (block_y - 1, from_north))):
            copies[2 + side].wait_recv()
            rows = pl.ds(at, lines, stride=block_y)
            target[rows, :] = target[rows, :] + wide_ref[3 + side, rows, :] * (cols_in[turn, side] * here)

    pack(x_ref, 0)
    pl.semaphore_wait(barrier, len(greeted))
    first = sends(x_ref, 0)
    for copy in first:
        copy.start()
    tell(0, (beside,))

    def flip(i, _):
        rows = pl.ds(i, levels, stride=block_x)
        cx, cy, kd = cx_ref[rows, :], cy_ref[rows, :], kd_ref[rows, :]
        w1, w2 = kd + jnp.maximum(cx, 0.0), kd - jnp.minimum(cx, 0.0)
        w3, w4 = kd + jnp.maximum(cy, 0.0), kd - jnp.minimum(cy, 0.0)
        packed = jnp.concatenate([1.0 - (w1 + w2 + w3 + w4), w1, w2, w3, w4], axis=0)
        packed = jnp.concatenate(thirds(packed), axis=0)
        at = pl.ds(pl.multiple_of(i * block_y, block_y), block_y)
        flip_ref[at, pl.ds(0, 15 * levels)] = packed.T
        return 0

    lax.fori_loop(0, block_x, flip, 0, unroll=4)
    hear(0, 1)
    tell(1, (ahead_y, behind_y))
    kinds = 5 * levels
    r = lax.broadcasted_iota(jnp.int32, (3 * kinds, members), 0)
    pick = [((r == k) | (r == k + kinds) | (r == k + 2 * kinds)).astype(F32).astype(BF16) for k in range(kinds)]
    pair = 2 * block_y

    def widen(n, _):
        left = flip_ref[pl.ds(pl.multiple_of(n * pair, pair), pair), pl.ds(0, 3 * kinds)].astype(BF16)
        for k in range(0, kinds, 2):
            right = jnp.concatenate(pick[k : k + 2], axis=1)
            spread_out = jnp.dot(left, right, preferred_element_type=F32)
            for u in range(2):
                for v in range(2):
                    kind, l = divmod(k + v, levels)
                    piece_out = spread_out[u * block_y : (u + 1) * block_y, v * members : (v + 1) * members]
                    wide_ref[kind, rows_of(n * 2 + u, l), :] = piece_out
        return 0

    lax.fori_loop(0, block_x // 2, widen, 0)
    local, owner = local_ref[...], owner_ref[...]
    ix = floor_div(local, block_y * levels, size)
    rest = local - ix * (block_y * levels)
    iy = floor_div(rest, levels, block_y * levels)
    lev = rest - iy * levels
    ox = floor_div(owner, ny, nx * ny)
    oy = owner - ox * ny
    mine = owner == gx * ny + gy
    place_ref[...] = jnp.where(mine, (ix * levels + lev) * block_y + iy, size)
    px = (ox - gx) * block_x + ix + nx * block_x
    py = (oy - gy) * block_y + iy + ny * block_y
    code = ((px * 1024 + py) * 128 + reach_ref[...]).T
    inv = lax.rsqrt(variance_ref[...])
    field_ref[pl.ds(size, 8), :] = jnp.zeros((8, members), F32)
    shift = (value_ref[...] * inv).T
    inv = inv.T
    width = place_ref.shape[1]
    tables = [
        pltpu.make_async_copy(place_ref.at[r], place_s.at[pl.ds(r * width, width)], table_sem.at[r])
        for r in range(count // width)
    ]
    for table in tables:
        table.start()
    hear(1, 2)
    tell(2, (ahead_y,))
    inside(x_ref, mid_ref)
    border(first, x_ref, mid_ref, 0)
    pack(mid_ref, 1)
    second = sends(mid_ref, 1)
    for copy in second:
        copy.start()
    hear(2, 1)
    tell(3, (up, down))
    inside(mid_ref, field_ref)
    hear(3, 2)
    tell(4, (up,))
    fetch.wait()
    for table in tables:
        table.wait()
    for d in range(count // width):
        rows = pl.ds(d * width, width)
        code_ref[rows, :] = jnp.broadcast_to(code[:, d : d + 1], (width, members))
        inv_ref[rows, :] = jnp.broadcast_to(inv[:, d : d + 1], (width, members))
        noise_ref[rows, :] = noise_ref[rows, :] + jnp.broadcast_to(shift[:, d : d + 1], (width, members))

    def spot(g, _):
        for u in range(8):
            spot_s[g * 8 + u] = place_s[order_ref[g * 8 + u]]
        return 0

    groups = count // 8
    lax.fori_loop(0, groups, spot, 0)

    def prepare(g, _):
        for u in range(8):
            at = pl.ds(g * 8 + u, 1)
            o = pl.ds(order_ref[g * 8 + u], 1)
            w_ref[at, :] = noise_ref[o, :]
            rows_c[at, :] = code_ref[o, :]
            rows_i[at, :] = inv_ref[o, :]
        return 0

    border(second, mid_ref, field_ref, 1)
    hear(4, 1)
    keep = pltpu.make_async_copy(field_ref, state_hbm, copy_sem.at[0])
    keep.start()

    def pick_rows(base):
        def body(g, _):
            for u in range(8):
                k = base + g * 8 + u
                part_ref[pl.ds(k, 1), :] = field_ref[pl.ds(spot_s[k], 1), :]
            return 0

        lax.fori_loop(0, half // 8, body, 0)

    mine = pl.ds(pl.multiple_of(core * half, half), half)
    other = pl.ds(pl.multiple_of((1 - core) * half, half), half)
    pick_rows((1 - core) * half)
    swap = pltpu.make_async_remote_copy(
        src_ref=part_ref.at[other], dst_ref=half_ref, send_sem=send_sem.at[0], recv_sem=recv_sem.at[0],
        device_id=partner, device_id_type=MESH,
    )
    swap.start()
    pick_rows(core * half)
    swap.wait_recv()
    sum_ref[...] = (part_ref[mine, :] + half_ref[...]).reshape(sum_ref.shape)

    def scatter(a, t, device):
        pltpu.make_async_remote_copy(
            src_ref=sum_ref.at[t], dst_ref=slots_ref.at[chip], send_sem=send_sem.at[1], recv_sem=recv_sem.at[1],
            device_id=device, device_id_type=MESH,
        ).start()

    others(scatter)
    slots_ref[chip] = sum_ref[chip]
    lax.fori_loop(0, groups // 2, prepare, 0)
    some = slots_ref.at[pl.ds(0, chips - 1)]
    pltpu.make_async_copy(some, some, recv_sem.at[1]).wait()
    own = pl.ds(pl.multiple_of(core * half + chip * piece, piece), piece)
    y_ref[own, :] = jnp.sum(slots_ref[...], axis=0)

    def gather(a, t, device):
        pltpu.make_async_remote_copy(
            src_ref=y_ref.at[own], dst_ref=y_ref.at[own], send_sem=send_sem.at[2], recv_sem=line_recv.at[a],
            device_id=device, device_id_type=MESH,
        ).start()

    others(gather)
    lax.fori_loop(groups // 2, groups, prepare, 0)
    stores = [
        pltpu.make_async_copy(source, target, copy_sem.at[1 + i])
        for i, (source, target) in enumerate(((w_ref, w_hbm), (rows_c, rows_c_hbm), (rows_i, rows_i_hbm)))
    ]
    for store in stores:
        store.start()
    block = my * piece

    def share(a):
        ox = lax.rem(gx + nx - a, nx)
        rows = pl.ds(pl.multiple_of(core * half + ox * block, block), block)
        return pltpu.make_async_remote_copy(
            src_ref=y_ref.at[rows], dst_ref=y_ref.at[rows], send_sem=share_send.at[a], recv_sem=share_recv.at[a],
            device_id=partner, device_id_type=MESH,
        )

    near = y_ref.at[pl.ds(0, block - piece)]
    pltpu.make_async_copy(near, near, line_recv.at[0]).wait()
    share(0).start()
    row_block = y_ref.at[pl.ds(0, block)]

    def pass_on(a, _):
        pltpu.make_async_copy(row_block, row_block, line_recv.at[a]).wait()
        share(a).start()
        return 0

    lax.fori_loop(1, nx, pass_on, 0)
    for copy in first + second:
        copy.wait_send()
    swap.wait_send()
    keep.wait()
    for store in stores:
        store.wait()
    pltpu.make_async_copy(some, some, send_sem.at[1]).wait()
    pltpu.make_async_copy(some, some, send_sem.at[2]).wait()

    def finish(a, _):
        share(a).wait()
        return 0

    lax.fori_loop(0, nx, finish, 0)


def split(x):
    high = x.astype(BF16)
    return high, (x - high.astype(F32)).astype(BF16)


def wide(x):
    return jnp.concatenate(split(x), axis=1)


def project(side, x):
    pair = lax.dot_general(wide(x), side, (((1,), (1,)), ((), ())), preferred_element_type=F32)
    half = pair.shape[1] // 2
    return pair[:, :half] + pair[:, half:]


def spread(solved, g):
    return jnp.dot(wide(g), solved, preferred_element_type=F32)


def stack_solved(v, scale):
    high, low = split(v * scale)
    return jnp.concatenate([high, low, high, low], axis=0)


def sharpen(r, v, t, eye, last):
    t = 2.0 * t * t - 1.0
    back = 1.0 / t
    gain = 1.0 + back
    rh, rl = split(r)
    vh, vl = split(v)
    left = jnp.concatenate([rh, rl], axis=1)
    head = jnp.concatenate([rh, vh], axis=1)
    tail = jnp.concatenate([rl, vl], axis=1)
    right = jnp.concatenate([head, tail, head, tail], axis=0)
    prod = jnp.dot(left, right, preferred_element_type=F32)
    v = gain * (v + prod[:, 2 * OB :])
    r = None if last else gain * prod[:, : 2 * OB] - back * eye
    return r, v, t


def begin(p, rhs, norm, eye):
    c = 1.0 + jnp.maximum(norm, 0.0625)
    top = c + 1.0
    alpha = 2.0 / top
    return ((c - 1.0) / top) * eye - alpha * p, alpha * rhs, top / (c - 1.0)


def hinted(x):
    return x if isinstance(x, int) else pl.multiple_of(x, OB)


def assimilate(
    span_x, span_y,
    shape,
    rows_c, rows_i, y_in, w_ref, x_hbm, out_hbm,
    rows_x, rows_y, rows_r, y_ref, t_ref, v_ref, cur_ref, side_ref, solved_ref, lanes_ref,
    first_ref, pair_ref, mix_ref, back_ref, both_ref, out_ref, copy_sem,
):
    block_x, levels, block_y, members = shape
    size = block_x * levels * block_y
    load = pltpu.make_async_copy(x_hbm.at[pl.ds(0, size)], out_ref, copy_sem.at[0])
    load.start()
    count = y_in.shape[0]
    batches = count // OB
    scale = 1.0 / (members - 1.0)
    code = rows_c[...]
    rows_x[...] = ((code >> 17) - span_x).astype(F32)
    rows_y[...] = (((code >> 7) & 1023) - span_y).astype(F32)
    reach = (code & 127).astype(F32)
    rows_r[...] = 1.0 / (reach * reach)
    y_ref[...] = y_in[...] * rows_i[...]
    cur_ref[...] = y_ref[pl.ds(0, OB), :]
    lane = lax.broadcasted_iota(jnp.int32, (OB, 2 * OB), 1)
    row = lax.broadcasted_iota(jnp.int32, (OB, 2 * OB), 0)
    upper = lane >= OB
    eye = jnp.where((lane == row) | (lane == row + OB), 1.0, 0.0).astype(F32)
    ys = lax.broadcasted_iota(jnp.int32, (block_y, 1), 0).astype(F32)
    none = jnp.zeros((OB, 2 * members), BF16)

    def rho_rows(at, px, py, ir):
        dx = rows_x[at, :] - px
        dy = rows_y[at, :] - py
        near = jnp.maximum(1.0 - (dx * dx + dy * dy) * ir, 0.0)
        return near * near

    def fold(x):
        return x[:, :members] + x[:, members:]

    def cells(n):
        px, py, ir = both_ref[pl.ds(0, 1), :], both_ref[pl.ds(1, 1), :], both_ref[pl.ds(2, 1), :]
        dy = ys - py
        dy2 = dy * dy * ir
        rhos = []
        for u in range(6):
            dx = jnp.float32(n * 6 + u) - px
            near = jnp.maximum((1.0 - dx * dx * ir) - dy2, 0.0)
            rhos.append((near * near)[None, None])
        rho = jnp.concatenate(rhos, axis=0)
        rows = 6 * levels * block_y
        at = pl.ds(n * rows, rows)
        flat = (rows, members)
        tall = (6, levels, block_y, members)
        old = out_ref[at, :]
        raw = project(pair_ref[...], old)
        g = (raw.reshape(tall) * rho).reshape(flat)
        raw = raw + fold(jnp.dot(wide(g), mix_ref[...], preferred_element_type=F32))
        g = (raw.reshape(tall) * rho).reshape(flat)
        new = old + fold(jnp.dot(wide(g), back_ref[...], preferred_element_type=F32))
        out_ref[at, :] = new
        return at

    def step(first, blocks, odd, b):
        fresh = b is None
        b = 0 if fresh else b
        now = pl.ds(hinted(b * OB), OB)
        after = pl.ds(hinted(jnp.minimum(b + 1, batches - 1) * OB), OB)
        pieces = []
        if not fresh:
            side0, solved0 = side_ref[...], solved_ref[...]
            px0, py0, ir0 = lanes_ref[pl.ds(0, 1), :], lanes_ref[pl.ds(1, 1), :], lanes_ref[pl.ds(2, 1), :]

            def later(start, size):
                at = pl.ds(start, size)
                old = y_ref[at, :]
                y_ref[at, :] = old + spread(solved0, project(side0, old) * rho_rows(at, px0, py0, ir0))

            for start in range((first + 1) * OB, count, 1024):
                pieces.append(functools.partial(later, start, min(1024, count - start)))
        ahead_of = len(pieces)
        for n in blocks:
            pieces.append(functools.partial(cells, n))
        plan = list([0.3, 0.6, 0.8, 1, 1, 1, 1] if odd else [0.3, 0.6, 0.8, 1, 1, 1, 1])
        total = len(pieces)
        done = [0]

        def fill():
            share = plan.pop(0)
            upto = total if not plan else min(total, round(share * total))
            while done[0] < upto:
                pieces[done[0]]()
                done[0] += 1

        hx = cur_ref[...]
        centred = hx - jnp.mean(hx, axis=1, keepdims=True)
        high, low = split(centred)
        high2 = jnp.concatenate([high, high], axis=1)
        low2 = jnp.concatenate([low, low], axis=1)
        side = jnp.concatenate([high2, low2, low2, high2], axis=0)
        fill()
        p = project(side, centred) * scale
        fill()
        norm = jnp.max(jnp.sum(jnp.abs(p), axis=0, keepdims=True), axis=1, keepdims=True)
        rhs = w_ref[now, :] - hx
        r, v, t = begin(p, rhs, norm, eye)
        for i in range(4):
            r, v, t = sharpen(r, v, t, eye, i + 1 == 4)
            fill()
            if i == 2:
                while done[0] < ahead_of:
                    pieces[done[0]]()
                    done[0] += 1
                ahead = y_ref[after, :]
                px = jnp.sum(rows_x[now, :] * eye, axis=0, keepdims=True)
                py = jnp.sum(rows_y[now, :] * eye, axis=0, keepdims=True)
                ir = jnp.sum(rows_r[now, :] * eye, axis=0, keepdims=True)
                g = project(side, ahead) * rho_rows(after, px, py, ir)
                if odd:
                    mix = project(side, first_ref[...])

        def settle(v):
            solved = stack_solved(v, scale)
            cur_ref[...] = ahead + spread(solved, g)
            solved_ref[...] = solved
            if odd:
                bh = jnp.concatenate([solved0[:OB], solved[:OB]], axis=0)
                bl = jnp.concatenate([solved0[OB : 2 * OB], solved[OB : 2 * OB]], axis=0)
                half = jnp.concatenate([bh, bl], axis=1)
                back_ref[...] = jnp.concatenate([half, half], axis=0)
            else:
                first_ref[...] = v * scale

        fill()
        settle(v)
        side_ref[...] = side
        lanes_ref[pl.ds(0, 1), :] = px
        lanes_ref[pl.ds(1, 1), :] = py
        lanes_ref[pl.ds(2, 1), :] = ir
        if odd:
            pair_ref[...] = jnp.concatenate([side0[:OB], high2, side0[OB : 2 * OB], low2], axis=0)
            mh, ml = split(jnp.where(upper, mix, 0.0))
            mrow = jnp.concatenate([mh, ml], axis=1)
            mix_ref[...] = jnp.concatenate([mrow, none, mrow, none], axis=0)
            low_half = ~upper[:1, :]
            both_ref[pl.ds(0, 1), :] = jnp.where(low_half, px0, px)
            both_ref[pl.ds(1, 1), :] = jnp.where(low_half, py0, py)
            both_ref[pl.ds(2, 1), :] = jnp.where(low_half, ir0, ir)

        @pl.when(jnp.max(norm) > QUICK)
        def _():
            t_ref[...] = p + eye
            v_ref[...] = rhs

            @pl.when(jnp.max(norm) <= WIDE)
            def _():
                r, v, t = begin(p, rhs, norm, eye)
                for i in range(LONG):
                    r, v, t = sharpen(r, v, t, eye, i + 1 == LONG)
                v_ref[...] = v

            @pl.when(jnp.max(norm) > WIDE)
            def _():
                lax.fori_loop(0, OB, pivot, 0)

            settle(v_ref[...])

    def pivot(k, _):
        trow = t_ref[pl.ds(k, 1), :]
        here = lane[:1, :] == k
        inverse = 1.0 / jnp.sum(jnp.where(here, trow, 0.0), axis=1, keepdims=True)
        trow = trow * inverse
        vrow = v_ref[pl.ds(k, 1), :] * inverse
        mat = t_ref[...]
        col = jnp.sum(jnp.where(lane == k, mat, 0.0), axis=1, keepdims=True)
        mine = row == k
        t_ref[...] = jnp.where(mine, trow, mat - col * trow)
        v_ref[...] = jnp.where(mine, vrow, v_ref[...] - col * vrow)
        return 0

    groups = block_x // 6
    early, late = range(groups // 2), range(groups // 2, groups)
    step(0, (), False, None)
    step(0, (), True, 1)

    def two(first, q, _):
        step(first, early, False, 2 * q)
        step(first, late, True, 2 * q + 1)
        return 0

    load.wait()
    two(0, 1, 0)
    for first in range(4, batches, 4):
        lax.fori_loop(first // 2, min(first + 4, batches) // 2, functools.partial(two, first), 0)
    stores = []
    for n in range(groups):
        at = cells(n)
        stores.append(pltpu.make_async_copy(out_ref.at[at], out_hbm.at[at], copy_sem.at[1 + n]))
        stores[-1].start()
    for store in stores:
        store.wait()


def run_assimilate(shape, spans, *args):
    vmem = pl.BlockSpec(memory_space=pltpu.VMEM)
    hbm = pl.BlockSpec(memory_space=pl.ANY)
    count, members = args[0].shape
    size = shape[0] * shape[1] * shape[2]
    out = pl.pallas_call(
        functools.partial(assimilate, *spans, shape),
        out_shape=jax.ShapeDtypeStruct((size, members), F32),
        in_specs=[vmem] * (len(args) - 1) + [hbm],
        out_specs=hbm,
        scratch_shapes=[
            pltpu.VMEM((count, members), F32),
            pltpu.VMEM((count, members), F32),
            pltpu.VMEM((count, members), F32),
            pltpu.VMEM((count, members), F32),
            pltpu.VMEM((OB, 2 * OB), F32),
            pltpu.VMEM((OB, members), F32),
            pltpu.VMEM((OB, members), F32),
            pltpu.VMEM((4 * OB, 2 * members), BF16),
            pltpu.VMEM((4 * OB, members), BF16),
            pltpu.VMEM((8, members), F32),
            pltpu.VMEM((OB, members), F32),
            pltpu.VMEM((4 * OB, 2 * members), BF16),
            pltpu.VMEM((4 * OB, 2 * members), BF16),
            pltpu.VMEM((4 * OB, 2 * members), BF16),
            pltpu.VMEM((8, members), F32),
            pltpu.VMEM((size, members), F32),
            pltpu.SemaphoreType.DMA((1 + shape[0] // 6,)),
        ],
        name="assimilate",
    )(*args)
    return out.reshape(shape)


def per_device(
    ensemble,
    cfl_ratio_primary_axis,
    cfl_ratio_secondary_axis,
    spreading_ratio,
    obs_owner,
    obs_local,
    batch_order,
    obs_reach,
    obs_value,
    obs_variance,
    obs_noise,
):
    block_x, block_y, levels, members = ensemble.shape
    span_x, span_y = lax.axis_size("gx"), lax.axis_size("gy")
    span = span_x * span_y
    count = obs_local.shape[0]
    size = block_x * levels * block_y
    strip = levels * block_y
    lines = block_x * levels
    flat = jnp.transpose(ensemble, (0, 2, 1, 3)).reshape(size, members)
    plane = (levels * block_x, block_y)
    coefs = [
        jnp.transpose(c, (2, 0, 1)).reshape(plane)
        for c in (cfl_ratio_primary_axis, cfl_ratio_secondary_axis, spreading_ratio)
    ]
    tile = (count // 128, 128)
    tables = [v.reshape(tile) for v in (obs_owner, obs_local, obs_reach, obs_value, obs_variance)]
    vmem = pl.BlockSpec(memory_space=pltpu.VMEM)
    smem = pl.BlockSpec(memory_space=pltpu.SMEM)
    hbm = pl.BlockSpec(memory_space=pl.ANY)
    chips = span // 2
    table = jax.ShapeDtypeStruct((count, members), F32)
    codes = jax.ShapeDtypeStruct((count, members), jnp.int32)
    full = pltpu.VMEM((count, members), F32)
    state, seen, wanted, rows_c, rows_i = pl.pallas_call(
        exchange,
        out_shape=[jax.ShapeDtypeStruct((size + 8, members), F32), table, table, codes, table],
        in_specs=[vmem] * 9 + [smem, hbm],
        out_specs=[hbm, vmem, hbm, hbm, hbm],
        scratch_shapes=[
            pltpu.VMEM((size + 8, members), F32),
            pltpu.VMEM((size, members), F32),
            pltpu.VMEM((5, size, members), F32),
            pltpu.VMEM((block_x * block_y, 128), F32),
            pltpu.VMEM((2, 2, lines, members), F32),
            pltpu.VMEM((2, 2, strip, members), F32),
            pltpu.VMEM((2, 2, lines, members), F32),
            full,
            full,
            pltpu.VMEM((count, members), jnp.int32),
            full,
            full,
            pltpu.VMEM((count // 2, members), F32),
            pltpu.VMEM((chips, count // span, members), F32),
            pltpu.VMEM((chips, count // span, members), F32),
            pltpu.VMEM((count, members), jnp.int32),
            full,
            pltpu.VMEM(tile, jnp.int32),
            pltpu.SMEM((count,), jnp.int32),
            pltpu.SMEM((count,), jnp.int32),
            pltpu.SemaphoreType.DMA((2, 4)),
            pltpu.SemaphoreType.DMA((2, 4)),
            pltpu.SemaphoreType.DMA((4,)),
            pltpu.SemaphoreType.DMA((4,)),
            pltpu.SemaphoreType.DMA((5,)),
            pltpu.SemaphoreType.DMA((count // 128,)),
            pltpu.SemaphoreType.DMA((span_x,)),
            pltpu.SemaphoreType.DMA((span_x,)),
            pltpu.SemaphoreType.DMA((span_x,)),
            pltpu.SemaphoreType.REGULAR((5,)),
        ],
        compiler_params=pltpu.CompilerParams(collective_id=0, has_side_effects=True),
        name="exchange",
    )(flat, *coefs, *tables, batch_order, obs_noise)
    shape = (block_x, levels, block_y, members)
    spans = (span_x * block_x, span_y * block_y)
    out = run_assimilate(shape, spans, rows_c, rows_i, seen, wanted, state)
    return jnp.transpose(out, (0, 2, 1, 3))


def solution(mesh):
    return jax.shard_map(
        per_device,
        mesh=mesh,
        in_specs=(
            P("gx", "gy", None, None),
            P("gx", "gy", None),
            P("gx", "gy", None),
            P("gx", "gy", None),
            P(),
            P(),
            P(),
            P(),
            P(),
            P(),
            P(),
        ),
        out_specs=P("gx", "gy", None, None),
        check_vma=False,
    )
```

```python
import functools

import jax
import jax.numpy as jnp
from jax import lax
from jax.experimental import pallas as pl
from jax.experimental.pallas import tpu as pltpu
from jax.sharding import PartitionSpec as P

OB = 64
SWAPS = 2
QUICK = 6.5
WIDE = 63.0
LONG = 6
MESH = pl.DeviceIdType.MESH
F32 = jnp.float32
BF16 = jnp.bfloat16


def floor_div(x, n, top):
    shift = 1
    while any((v * -(-(1 << shift) // n)) >> shift != v // n for v in range(top)):
        shift += 1
    return (x * -(-(1 << shift) // n)) >> shift


def thirds(x):
    high = x.astype(BF16).astype(F32)
    rest = x - high
    mid = rest.astype(BF16).astype(F32)
    return [high, mid, rest - mid]


def exchange(
    x_hbm, cx_ref, cy_ref, kd_ref, owner_ref, local_ref, reach_ref, value_ref, variance_ref, order_ref, noise_hbm,
    state_hbm, y_ref, w_hbm, rows_c_hbm, rows_i_hbm,
    field_ref, mid_ref, wide_ref, flip_ref, cols_ref, rows_in, cols_in,
    noise_ref, w_ref, rows_c, rows_i, part_ref, half_ref, sum_ref, slots_ref, code_ref, inv_ref, place_ref,
    place_s, spot_s, halo_send, halo_recv, send_sem, recv_sem, copy_sem, table_sem, line_recv, share_send, share_recv, step_sem, x_ref, load_sem, swap_send, swap_recv,
):
    strip, members = rows_in.shape[2:]
    block_y = cx_ref.shape[1]
    levels = strip // block_y
    block_x = cx_ref.shape[0] // levels
    lines = block_x * levels
    size = lines * block_y
    gx, gy = lax.axis_index("gx"), lax.axis_index("gy")
    nx, ny = lax.axis_size("gx"), lax.axis_size("gy")
    west, east = (lax.rem(gx + nx - 1, nx), gy), (lax.rem(gx + 1, nx), gy)
    south, north = (gx, lax.rem(gy + ny - 1, ny)), (gx, lax.rem(gy + 1, ny))
    count = part_ref.shape[0]
    half = count // 2
    my = ny // 2
    chips = nx * my
    piece = half // chips
    core = lax.rem(gy, 2)
    chip = gx * my + gy // 2
    partner = (gx, gy + 1 - 2 * core)

    def others(visit):
        def line(a, start):
            ox = lax.rem(gx + a, nx)
            for b in range(start, my):
                oy = lax.rem(gy // 2 + b, my)
                visit(a, ox * my + oy, (ox, oy * 2 + core))

        line(0, 1)

        def body(a, _):
            line(a, 0)
            return 0

        lax.fori_loop(1, nx, body, 0)

    barrier = pltpu.get_barrier_semaphore()

    side_x = lax.rem(gx, 2)
    rings = nx // 2
    columns = my // 2
    at_z, at_x, at_y = gx // 2, gy // my, lax.rem(gy, my) // 2

    def near_by(dz, flip_high, flip_low, dy):
        high = 1 - side_x if flip_high else side_x
        low = 1 - at_x if flip_low else at_x
        z = lax.rem(at_z + dz + rings, rings)
        y = lax.rem(at_y + dy + columns, columns)
        return (z * 2 + high, low * my + y * 2 + core)

    up, down = near_by(1, 0, 0, 0), near_by(-1, 0, 0, 0)
    ahead_y, behind_y = near_by(0, 0, 0, 1), near_by(0, 0, 0, -1)
    across, beside = near_by(0, 1, 0, 0), near_by(0, 0, 1, 0)
    greeted = (west, east, south, north, partner, up, down, ahead_y, behind_y, across, beside)
    for device in greeted:
        pl.semaphore_signal(barrier, inc=1, device_id=device, device_id_type=MESH)

    load = pltpu.make_async_copy(x_hbm, x_ref, load_sem)
    load.start()

    def tell(step, devices):
        for device in devices:
            pl.semaphore_signal(step_sem.at[step], inc=1, device_id=device, device_id_type=MESH)

    def hear(step, signals):
        pl.semaphore_wait(step_sem.at[step], signals)

    fetch = pltpu.make_async_copy(noise_hbm, noise_ref, copy_sem.at[0])
    fetch.start()
    from_west = jnp.where(gx > 0, 1.0, 0.0).astype(F32)
    from_east = jnp.where(gx < nx - 1, 1.0, 0.0).astype(F32)
    from_south = jnp.where(gy > 0, 1.0, 0.0).astype(F32)
    from_north = jnp.where(gy < ny - 1, 1.0, 0.0).astype(F32)

    def pack(field, turn):
        cols_ref[turn, 0] = field[pl.ds(0, lines, stride=block_y), :]
        cols_ref[turn, 1] = field[pl.ds(block_y - 1, lines, stride=block_y), :]

    def sends(field, turn):
        last = (block_x - 1) * strip
        plan = (
            (field.at[pl.ds(last, strip)], rows_in.at[turn, 0], east),
            (field.at[pl.ds(0, strip)], rows_in.at[turn, 1], west),
            (cols_ref.at[turn, 1], cols_in.at[turn, 0], north),
            (cols_ref.at[turn, 0], cols_in.at[turn, 1], south),
        )
        return [
            pltpu.make_async_remote_copy(
                src_ref=source,
                dst_ref=target,
                send_sem=halo_send.at[turn, i],
                recv_sem=halo_recv.at[turn, i],
                device_id=device,
                device_id_type=MESH,
            )
            for i, (source, target, device) in enumerate(plan)
        ]

    def rows_of(i, l):
        return pl.ds(pl.multiple_of((i * levels + l) * block_y, block_y), block_y)

    def strip_of(field, i):
        return [field[rows_of(i, l), :] for l in range(levels)]

    zero = jnp.zeros((1, members), F32)

    def advance(i, centre, left, right, target):
        for l in range(levels):
            w = [wide_ref[k, rows_of(i, l), :] for k in range(5)]
            c = centre[l]
            new = w[0] * c + w[1] * left[l] + w[2] * right[l]
            new = new + w[3] * jnp.concatenate([zero, c[:-1]], axis=0)
            new = new + w[4] * jnp.concatenate([c[1:], zero], axis=0)
            target[rows_of(i, l), :] = new

    def inside(field, target):
        def inner(i, _):
            advance(i, strip_of(field, i), strip_of(field, i - 1), strip_of(field, i + 1), target)
            return 0

        lax.fori_loop(1, block_x - 1, inner, 0)

    def border(copies, field, target, turn):
        copies[0].wait_recv()
        left = [rows_in[turn, 0, pl.ds(l * block_y, block_y), :] * from_west for l in range(levels)]
        advance(0, strip_of(field, 0), left, strip_of(field, 1), target)
        copies[1].wait_recv()
        right = [rows_in[turn, 1, pl.ds(l * block_y, block_y), :] * from_east for l in range(levels)]
        last = block_x - 1
        advance(last, strip_of(field, last), strip_of(field, last - 1), right, target)
        for side, (at, here) in enumerate(((0, from_south), (block_y - 1, from_north))):
            copies[2 + side].wait_recv()
            rows = pl.ds(at, lines, stride=block_y)
            target[rows, :] = target[rows, :] + wide_ref[3 + side, rows, :] * (cols_in[turn, side] * here)

    pl.semaphore_wait(barrier, len(greeted))
    first = sends(x_hbm, 0)
    for copy in first[:2]:
        copy.start()
    tell(0, (beside,))
    load.wait()
    pack(x_ref, 0)
    for copy in first[2:]:
        copy.start()

    def flip(i, _):
        rows = pl.ds(i, levels, stride=block_x)
        cx, cy, kd = cx_ref[rows, :], cy_ref[rows, :], kd_ref[rows, :]
        w1, w2 = kd + jnp.maximum(cx, 0.0), kd - jnp.minimum(cx, 0.0)
        w3, w4 = kd + jnp.maximum(cy, 0.0), kd - jnp.minimum(cy, 0.0)
        packed = jnp.concatenate([1.0 - (w1 + w2 + w3 + w4), w1, w2, w3, w4], axis=0)
        packed = jnp.concatenate(thirds(packed), axis=0)
        at = pl.ds(pl.multiple_of(i * block_y, block_y), block_y)
        flip_ref[at, pl.ds(0, 15 * levels)] = packed.T
        return 0

    lax.fori_loop(0, block_x, flip, 0, unroll=4)
    hear(0, 1)
    tell(1, (ahead_y, behind_y))
    kinds = 5 * levels
    r = lax.broadcasted_iota(jnp.int32, (3 * kinds, members), 0)
    pick = [((r == k) | (r == k + kinds) | (r == k + 2 * kinds)).astype(F32).astype(BF16) for k in range(kinds)]
    pair = 2 * block_y

    def widen(n, _):
        left = flip_ref[pl.ds(pl.multiple_of(n * pair, pair), pair), pl.ds(0, 3 * kinds)].astype(BF16)
        for k in range(0, kinds, 2):
            right = jnp.concatenate(pick[k : k + 2], axis=1)
            spread_out = jnp.dot(left, right, preferred_element_type=F32)
            for u in range(2):
                for v in range(2):
                    kind, l = divmod(k + v, levels)
                    piece_out = spread_out[u * block_y : (u + 1) * block_y, v * members : (v + 1) * members]
                    wide_ref[kind, rows_of(n * 2 + u, l), :] = piece_out
        return 0

    lax.fori_loop(0, block_x // 2, widen, 0)
    local, owner = local_ref[...], owner_ref[...]
    ix = floor_div(local, block_y * levels, size)
    rest = local - ix * (block_y * levels)
    iy = floor_div(rest, levels, block_y * levels)
    lev = rest - iy * levels
    ox = floor_div(owner, ny, nx * ny)
    oy = owner - ox * ny
    mine = owner == gx * ny + gy
    place_ref[...] = jnp.where(mine, (ix * levels + lev) * block_y + iy, size)
    px = (ox - gx) * block_x + ix + nx * block_x
    py = (oy - gy) * block_y + iy + ny * block_y
    code = ((px * 1024 + py) * 128 + reach_ref[...]).T
    inv = lax.rsqrt(variance_ref[...])
    field_ref[pl.ds(size, 8), :] = jnp.zeros((8, members), F32)
    shift = (value_ref[...] * inv).T
    inv = inv.T
    width = place_ref.shape[1]
    tables = [
        pltpu.make_async_copy(place_ref.at[r], place_s.at[pl.ds(r * width, width)], table_sem.at[r])
        for r in range(count // width)
    ]
    for table in tables:
        table.start()
    hear(1, 2)
    tell(2, (ahead_y,))
    inside(x_ref, mid_ref)
    border(first, x_ref, mid_ref, 0)
    pack(mid_ref, 1)
    second = sends(mid_ref, 1)
    for copy in second:
        copy.start()
    hear(2, 1)
    tell(3, (up, down))
    inside(mid_ref, field_ref)
    hear(3, 2)
    tell(4, (up,))
    fetch.wait()
    for table in tables:
        table.wait()
    for d in range(count // width):
        rows = pl.ds(d * width, width)
        code_ref[rows, :] = jnp.broadcast_to(code[:, d : d + 1], (width, members))
        inv_ref[rows, :] = jnp.broadcast_to(inv[:, d : d + 1], (width, members))
        noise_ref[rows, :] = noise_ref[rows, :] + jnp.broadcast_to(shift[:, d : d + 1], (width, members))

    def spot(g, _):
        for u in range(8):
            spot_s[g * 8 + u] = place_s[order_ref[g * 8 + u]]
        return 0

    groups = count // 8
    lax.fori_loop(0, groups, spot, 0)

    def prepare(g, _):
        for u in range(8):
            at = pl.ds(g * 8 + u, 1)
            o = pl.ds(order_ref[g * 8 + u], 1)
            w_ref[at, :] = noise_ref[o, :]
            rows_c[at, :] = code_ref[o, :]
            rows_i[at, :] = inv_ref[o, :]
        return 0

    border(second, mid_ref, field_ref, 1)
    hear(4, 1)
    keep = pltpu.make_async_copy(field_ref, state_hbm, copy_sem.at[0])
    keep.start()

    def pick_rows(base, rows):
        def body(g, _):
            for u in range(8):
                k = base + g * 8 + u
                part_ref[pl.ds(k, 1), :] = field_ref[pl.ds(spot_s[k], 1), :]
            return 0

        lax.fori_loop(0, rows // 8, body, 0)

    mine = pl.ds(pl.multiple_of(core * half, half), half)
    swaps = []
    part = half // SWAPS
    for c in range(SWAPS):
        base = pl.multiple_of((1 - core) * half + c * part, part)
        pick_rows(base, part)
        swaps.append(
            pltpu.make_async_remote_copy(
                src_ref=part_ref.at[pl.ds(base, part)], dst_ref=half_ref.at[pl.ds(c * part, part)],
                send_sem=swap_send.at[c], recv_sem=swap_recv.at[c], device_id=partner, device_id_type=MESH,
            )
        )
        swaps[-1].start()
    pick_rows(core * half, half)
    for swap in swaps:
        swap.wait_recv()
    sum_ref[...] = (part_ref[mine, :] + half_ref[...]).reshape(sum_ref.shape)

    def scatter(a, t, device):
        pltpu.make_async_remote_copy(
            src_ref=sum_ref.at[t], dst_ref=slots_ref.at[chip], send_sem=send_sem.at[1], recv_sem=recv_sem.at[1],
            device_id=device, device_id_type=MESH,
        ).start()

    others(scatter)
    slots_ref[chip] = sum_ref[chip]
    lax.fori_loop(0, groups // 2, prepare, 0)
    some = slots_ref.at[pl.ds(0, chips - 1)]
    pltpu.make_async_copy(some, some, recv_sem.at[1]).wait()
    own = pl.ds(pl.multiple_of(core * half + chip * piece, piece), piece)
    y_ref[own, :] = jnp.sum(slots_ref[...], axis=0)

    def gather(a, t, device):
        pltpu.make_async_remote_copy(
            src_ref=y_ref.at[own], dst_ref=y_ref.at[own], send_sem=send_sem.at[2], recv_sem=line_recv.at[a],
            device_id=device, device_id_type=MESH,
        ).start()

    others(gather)
    lax.fori_loop(groups // 2, groups, prepare, 0)
    stores = [
        pltpu.make_async_copy(source, target, copy_sem.at[1 + i])
        for i, (source, target) in enumerate(((w_ref, w_hbm), (rows_c, rows_c_hbm), (rows_i, rows_i_hbm)))
    ]
    for store in stores:
        store.start()
    block = my * piece

    def share(a):
        ox = lax.rem(gx + nx - a, nx)
        rows = pl.ds(pl.multiple_of(core * half + ox * block, block), block)
        return pltpu.make_async_remote_copy(
            src_ref=y_ref.at[rows], dst_ref=y_ref.at[rows], send_sem=share_send.at[a], recv_sem=share_recv.at[a],
            device_id=partner, device_id_type=MESH,
        )

    near = y_ref.at[pl.ds(0, block - piece)]
    pltpu.make_async_copy(near, near, line_recv.at[0]).wait()
    share(0).start()
    row_block = y_ref.at[pl.ds(0, block)]

    def pass_on(a, _):
        pltpu.make_async_copy(row_block, row_block, line_recv.at[a]).wait()
        share(a).start()
        return 0

    lax.fori_loop(1, nx, pass_on, 0)
    for copy in first + second:
        copy.wait_send()
    for swap in swaps:
        swap.wait_send()
    keep.wait()
    for store in stores:
        store.wait()
    pltpu.make_async_copy(some, some, send_sem.at[1]).wait()
    pltpu.make_async_copy(some, some, send_sem.at[2]).wait()

    def finish(a, _):
        share(a).wait()
        return 0

    lax.fori_loop(0, nx, finish, 0)


def split(x):
    high = x.astype(BF16)
    return high, (x - high.astype(F32)).astype(BF16)


def wide(x):
    return jnp.concatenate(split(x), axis=1)


def project(side, x):
    pair = lax.dot_general(wide(x), side, (((1,), (1,)), ((), ())), preferred_element_type=F32)
    half = pair.shape[1] // 2
    return pair[:, :half] + pair[:, half:]


def spread(solved, g):
    return jnp.dot(wide(g), solved, preferred_element_type=F32)


def stack_solved(v, scale):
    high, low = split(v * scale)
    return jnp.concatenate([high, low, high, low], axis=0)


def sharpen(r, v, t, eye, last):
    t = 2.0 * t * t - 1.0
    back = 1.0 / t
    gain = 1.0 + back
    rh, rl = split(r)
    vh, vl = split(v)
    left = jnp.concatenate([rh, rl], axis=1)
    head = jnp.concatenate([rh, vh], axis=1)
    tail = jnp.concatenate([rl, vl], axis=1)
    right = jnp.concatenate([head, tail, head, tail], axis=0)
    prod = jnp.dot(left, right, preferred_element_type=F32)
    v = gain * (v + prod[:, 2 * OB :])
    r = None if last else gain * prod[:, : 2 * OB] - back * eye
    return r, v, t


def begin(p, rhs, norm, eye):
    c = 1.0 + jnp.maximum(norm, 0.0625)
    top = c + 1.0
    alpha = 2.0 / top
    return ((c - 1.0) / top) * eye - alpha * p, alpha * rhs, top / (c - 1.0)


def hinted(x):
    return x if isinstance(x, int) else pl.multiple_of(x, OB)


def assimilate(
    span_x, span_y,
    shape,
    rows_c, rows_i, y_in, w_ref, x_hbm, out_hbm,
    rows_x, rows_y, rows_r, y_ref, t_ref, v_ref, cur_ref, side_ref, solved_ref, lanes_ref,
    first_ref, pair_ref, mix_ref, back_ref, both_ref, out_ref, copy_sem,
):
    block_x, levels, block_y, members = shape
    size = block_x * levels * block_y
    load = pltpu.make_async_copy(x_hbm.at[pl.ds(0, size)], out_ref, copy_sem.at[0])
    load.start()
    count = y_in.shape[0]
    batches = count // OB
    scale = 1.0 / (members - 1.0)
    code = rows_c[...]
    rows_x[...] = ((code >> 17) - span_x).astype(F32)
    rows_y[...] = (((code >> 7) & 1023) - span_y).astype(F32)
    reach = (code & 127).astype(F32)
    rows_r[...] = 1.0 / (reach * reach)
    y_ref[...] = y_in[...] * rows_i[...]
    cur_ref[...] = y_ref[pl.ds(0, OB), :]
    lane = lax.broadcasted_iota(jnp.int32, (OB, 2 * OB), 1)
    row = lax.broadcasted_iota(jnp.int32, (OB, 2 * OB), 0)
    upper = lane >= OB
    eye = jnp.where((lane == row) | (lane == row + OB), 1.0, 0.0).astype(F32)
    ys = lax.broadcasted_iota(jnp.int32, (block_y, 1), 0).astype(F32)
    none = jnp.zeros((OB, 2 * members), BF16)

    def rho_rows(at, px, py, ir):
        dx = rows_x[at, :] - px
        dy = rows_y[at, :] - py
        near = jnp.maximum(1.0 - (dx * dx + dy * dy) * ir, 0.0)
        return near * near

    def fold(x):
        return x[:, :members] + x[:, members:]

    def cells(n):
        px, py, ir = both_ref[pl.ds(0, 1), :], both_ref[pl.ds(1, 1), :], both_ref[pl.ds(2, 1), :]
        dy = ys - py
        dy2 = dy * dy * ir
        rhos = []
        for u in range(6):
            dx = jnp.float32(n * 6 + u) - px
            near = jnp.maximum((1.0 - dx * dx * ir) - dy2, 0.0)
            rhos.append((near * near)[None, None])
        rho = jnp.concatenate(rhos, axis=0)
        rows = 6 * levels * block_y
        at = pl.ds(n * rows, rows)
        flat = (rows, members)
        tall = (6, levels, block_y, members)
        old = out_ref[at, :]
        raw = project(pair_ref[...], old)
        g = (raw.reshape(tall) * rho).reshape(flat)
        raw = raw + fold(jnp.dot(wide(g), mix_ref[...], preferred_element_type=F32))
        g = (raw.reshape(tall) * rho).reshape(flat)
        new = old + fold(jnp.dot(wide(g), back_ref[...], preferred_element_type=F32))
        out_ref[at, :] = new
        return at

    def step(first, blocks, odd, b):
        fresh = b is None
        b = 0 if fresh else b
        now = pl.ds(hinted(b * OB), OB)
        after = pl.ds(hinted(jnp.minimum(b + 1, batches - 1) * OB), OB)
        pieces = []
        if not fresh:
            side0, solved0 = side_ref[...], solved_ref[...]
            px0, py0, ir0 = lanes_ref[pl.ds(0, 1), :], lanes_ref[pl.ds(1, 1), :], lanes_ref[pl.ds(2, 1), :]

            def later(start, size):
                at = pl.ds(start, size)
                old = y_ref[at, :]
                y_ref[at, :] = old + spread(solved0, project(side0, old) * rho_rows(at, px0, py0, ir0))

            for start in range((first + 1) * OB, count, 1024):
                pieces.append(functools.partial(later, start, min(1024, count - start)))
        ahead_of = len(pieces)
        for n in blocks:
            pieces.append(functools.partial(cells, n))
        plan = list([0.3, 0.6, 0.8, 1, 1, 1, 1] if odd else [0.3, 0.6, 0.8, 1, 1, 1, 1])
        total = len(pieces)
        done = [0]

        def fill():
            share = plan.pop(0)
            upto = total if not plan else min(total, round(share * total))
            while done[0] < upto:
                pieces[done[0]]()
                done[0] += 1

        hx = cur_ref[...]
        centred = hx - jnp.mean(hx, axis=1, keepdims=True)
        high, low = split(centred)
        high2 = jnp.concatenate([high, high], axis=1)
        low2 = jnp.concatenate([low, low], axis=1)
        side = jnp.concatenate([high2, low2, low2, high2], axis=0)
        fill()
        p = project(side, centred) * scale
        fill()
        norm = jnp.max(jnp.sum(jnp.abs(p), axis=0, keepdims=True), axis=1, keepdims=True)
        rhs = w_ref[now, :] - hx
        r, v, t = begin(p, rhs, norm, eye)
        for i in range(4):
            r, v, t = sharpen(r, v, t, eye, i + 1 == 4)
            fill()
            if i == 2:
                while done[0] < ahead_of:
                    pieces[done[0]]()
                    done[0] += 1
                ahead = y_ref[after, :]
                px = jnp.sum(rows_x[now, :] * eye, axis=0, keepdims=True)
                py = jnp.sum(rows_y[now, :] * eye, axis=0, keepdims=True)
                ir = jnp.sum(rows_r[now, :] * eye, axis=0, keepdims=True)
                g = project(side, ahead) * rho_rows(after, px, py, ir)
                if odd:
                    mix = project(side, first_ref[...])

        def settle(v):
            solved = stack_solved(v, scale)
            cur_ref[...] = ahead + spread(solved, g)
            solved_ref[...] = solved
            if odd:
                bh = jnp.concatenate([solved0[:OB], solved[:OB]], axis=0)
                bl = jnp.concatenate([solved0[OB : 2 * OB], solved[OB : 2 * OB]], axis=0)
                half = jnp.concatenate([bh, bl], axis=1)
                back_ref[...] = jnp.concatenate([half, half], axis=0)
            else:
                first_ref[...] = v * scale

        fill()
        settle(v)
        side_ref[...] = side
        lanes_ref[pl.ds(0, 1), :] = px
        lanes_ref[pl.ds(1, 1), :] = py
        lanes_ref[pl.ds(2, 1), :] = ir
        if odd:
            pair_ref[...] = jnp.concatenate([side0[:OB], high2, side0[OB : 2 * OB], low2], axis=0)
            mh, ml = split(jnp.where(upper, mix, 0.0))
            mrow = jnp.concatenate([mh, ml], axis=1)
            mix_ref[...] = jnp.concatenate([mrow, none, mrow, none], axis=0)
            low_half = ~upper[:1, :]
            both_ref[pl.ds(0, 1), :] = jnp.where(low_half, px0, px)
            both_ref[pl.ds(1, 1), :] = jnp.where(low_half, py0, py)
            both_ref[pl.ds(2, 1), :] = jnp.where(low_half, ir0, ir)

        @pl.when(jnp.max(norm) > QUICK)
        def _():
            t_ref[...] = p + eye
            v_ref[...] = rhs

            @pl.when(jnp.max(norm) <= WIDE)
            def _():
                r, v, t = begin(p, rhs, norm, eye)
                for i in range(LONG):
                    r, v, t = sharpen(r, v, t, eye, i + 1 == LONG)
                v_ref[...] = v

            @pl.when(jnp.max(norm) > WIDE)
            def _():
                lax.fori_loop(0, OB, pivot, 0)

            settle(v_ref[...])

    def pivot(k, _):
        trow = t_ref[pl.ds(k, 1), :]
        here = lane[:1, :] == k
        inverse = 1.0 / jnp.sum(jnp.where(here, trow, 0.0), axis=1, keepdims=True)
        trow = trow * inverse
        vrow = v_ref[pl.ds(k, 1), :] * inverse
        mat = t_ref[...]
        col = jnp.sum(jnp.where(lane == k, mat, 0.0), axis=1, keepdims=True)
        mine = row == k
        t_ref[...] = jnp.where(mine, trow, mat - col * trow)
        v_ref[...] = jnp.where(mine, vrow, v_ref[...] - col * vrow)
        return 0

    groups = block_x // 6
    early, late = range(groups // 2), range(groups // 2, groups)
    step(0, (), False, None)
    step(0, (), True, 1)

    def two(first, q, _):
        step(first, early, False, 2 * q)
        step(first, late, True, 2 * q + 1)
        return 0

    load.wait()
    two(0, 1, 0)
    for first in range(4, batches, 4):
        lax.fori_loop(first // 2, min(first + 4, batches) // 2, functools.partial(two, first), 0)
    stores = []
    for n in range(groups):
        at = cells(n)
        stores.append(pltpu.make_async_copy(out_ref.at[at], out_hbm.at[at], copy_sem.at[1 + n]))
        stores[-1].start()
    for store in stores:
        store.wait()


def run_assimilate(shape, spans, *args):
    vmem = pl.BlockSpec(memory_space=pltpu.VMEM)
    hbm = pl.BlockSpec(memory_space=pl.ANY)
    count, members = args[0].shape
    size = shape[0] * shape[1] * shape[2]
    out = pl.pallas_call(
        functools.partial(assimilate, *spans, shape),
        out_shape=jax.ShapeDtypeStruct((size, members), F32),
        in_specs=[vmem] * (len(args) - 1) + [hbm],
        out_specs=hbm,
        scratch_shapes=[
            pltpu.VMEM((count, members), F32),
            pltpu.VMEM((count, members), F32),
            pltpu.VMEM((count, members), F32),
            pltpu.VMEM((count, members), F32),
            pltpu.VMEM((OB, 2 * OB), F32),
            pltpu.VMEM((OB, members), F32),
            pltpu.VMEM((OB, members), F32),
            pltpu.VMEM((4 * OB, 2 * members), BF16),
            pltpu.VMEM((4 * OB, members), BF16),
            pltpu.VMEM((8, members), F32),
            pltpu.VMEM((OB, members), F32),
            pltpu.VMEM((4 * OB, 2 * members), BF16),
            pltpu.VMEM((4 * OB, 2 * members), BF16),
            pltpu.VMEM((4 * OB, 2 * members), BF16),
            pltpu.VMEM((8, members), F32),
            pltpu.VMEM((size, members), F32),
            pltpu.SemaphoreType.DMA((1 + shape[0] // 6,)),
        ],
        name="assimilate",
    )(*args)
    return out.reshape(shape)


def per_device(
    ensemble,
    cfl_ratio_primary_axis,
    cfl_ratio_secondary_axis,
    spreading_ratio,
    obs_owner,
    obs_local,
    batch_order,
    obs_reach,
    obs_value,
    obs_variance,
    obs_noise,
):
    block_x, block_y, levels, members = ensemble.shape
    span_x, span_y = lax.axis_size("gx"), lax.axis_size("gy")
    span = span_x * span_y
    count = obs_local.shape[0]
    size = block_x * levels * block_y
    strip = levels * block_y
    lines = block_x * levels
    flat = jnp.transpose(ensemble, (0, 2, 1, 3)).reshape(size, members)
    plane = (levels * block_x, block_y)
    coefs = [
        jnp.transpose(c, (2, 0, 1)).reshape(plane)
        for c in (cfl_ratio_primary_axis, cfl_ratio_secondary_axis, spreading_ratio)
    ]
    tile = (count // 128, 128)
    tables = [v.reshape(tile) for v in (obs_owner, obs_local, obs_reach, obs_value, obs_variance)]
    vmem = pl.BlockSpec(memory_space=pltpu.VMEM)
    smem = pl.BlockSpec(memory_space=pltpu.SMEM)
    hbm = pl.BlockSpec(memory_space=pl.ANY)
    chips = span // 2
    table = jax.ShapeDtypeStruct((count, members), F32)
    codes = jax.ShapeDtypeStruct((count, members), jnp.int32)
    full = pltpu.VMEM((count, members), F32)
    state, seen, wanted, rows_c, rows_i = pl.pallas_call(
        exchange,
        out_shape=[jax.ShapeDtypeStruct((size + 8, members), F32), table, table, codes, table],
        in_specs=[hbm] + [vmem] * 8 + [smem, hbm],
        out_specs=[hbm, vmem, hbm, hbm, hbm],
        scratch_shapes=[
            pltpu.VMEM((size + 8, members), F32),
            pltpu.VMEM((size, members), F32),
            pltpu.VMEM((5, size, members), F32),
            pltpu.VMEM((block_x * block_y, 128), F32),
            pltpu.VMEM((2, 2, lines, members), F32),
            pltpu.VMEM((2, 2, strip, members), F32),
            pltpu.VMEM((2, 2, lines, members), F32),
            full,
            full,
            pltpu.VMEM((count, members), jnp.int32),
            full,
            full,
            pltpu.VMEM((count // 2, members), F32),
            pltpu.VMEM((chips, count // span, members), F32),
            pltpu.VMEM((chips, count // span, members), F32),
            pltpu.VMEM((count, members), jnp.int32),
            full,
            pltpu.VMEM(tile, jnp.int32),
            pltpu.SMEM((count,), jnp.int32),
            pltpu.SMEM((count,), jnp.int32),
            pltpu.SemaphoreType.DMA((2, 4)),
            pltpu.SemaphoreType.DMA((2, 4)),
            pltpu.SemaphoreType.DMA((4,)),
            pltpu.SemaphoreType.DMA((4,)),
            pltpu.SemaphoreType.DMA((5,)),
            pltpu.SemaphoreType.DMA((count // 128,)),
            pltpu.SemaphoreType.DMA((span_x,)),
            pltpu.SemaphoreType.DMA((span_x,)),
            pltpu.SemaphoreType.DMA((span_x,)),
            pltpu.SemaphoreType.REGULAR((5,)),
            pltpu.VMEM((size, members), F32),
            pltpu.SemaphoreType.DMA,
            pltpu.SemaphoreType.DMA((SWAPS,)),
            pltpu.SemaphoreType.DMA((SWAPS,)),
        ],
        compiler_params=pltpu.CompilerParams(collective_id=0, has_side_effects=True),
        name="exchange",
    )(flat, *coefs, *tables, batch_order, obs_noise)
    shape = (block_x, levels, block_y, members)
    spans = (span_x * block_x, span_y * block_y)
    out = run_assimilate(shape, spans, rows_c, rows_i, seen, wanted, state)
    return jnp.transpose(out, (0, 2, 1, 3))


def solution(mesh):
    return jax.shard_map(
        per_device,
        mesh=mesh,
        in_specs=(
            P("gx", "gy", None, None),
            P("gx", "gy", None),
            P("gx", "gy", None),
            P("gx", "gy", None),
            P(),
            P(),
            P(),
            P(),
            P(),
            P(),
            P(),
        ),
        out_specs=P("gx", "gy", None, None),
        check_vma=False,
    )
```
